256 devices in a mesh: seq: 8 (over z_lo, core), chan: 8 (over x, z_hi), batch: 4 (over y).
Axes of the slice: x: 4, y: 4, z: 8 (z_hi: 2, z_lo: 4; z = z_hi * 4 + z_lo), core: 2. Of those that a mesh axis runs over, the one named last changes fastest.
Arguments:
- tokens: bfloat16 [262144, 1024], P(('batch', 'seq'), 'chan'), parts along dimension 0, may hold values from -6 to 6
- gate_in: bfloat16 [262144, 1024], P(('batch', 'seq'), 'chan'), parts along dimension 0, may hold values from -6 to 6
- mix_first: bfloat16 [512, 512], replicated, may hold values from -0.25 to 0.25
- mix_second: bfloat16 [128, 128], replicated, may hold values from -0.5 to 0.5
- twiddle: float32 [128, 512], P('seq'), may hold values from 0.5 to 2
- out_proj: bfloat16 [1024, 1024], replicated, may hold values from -0.1875 to 0.1875
Outputs:
- mixed: bfloat16 [262144, 1024], P(('batch', 'seq'), 'chan'), parts along dimension 0
The draws below stay inside these ranges and needn't reach their ends.
There are 4 independent parts, one for each index of `batch`. The reference program is written for one: setup_inputs(seed, part) draws one part's arguments, and reference() takes and returns one part's arrays. A program takes and returns all parts, laid end to end along the dimension named above; an argument that names none is the same for every part. Nothing has to cross between parts.
All inputs are finite; a program needn't handle non-finite values.
Results may differ from the reference program's by a relative error of at most 0.012.
Values may be sent and summed in bfloat16 or wider, within the bound.
A program may use at most 128 MiB of HBM per device.

```python
import math
import jax
import jax.numpy as jnp
from jax import lax

D = 1024
B1 = 512
L = 65536
B2 = 128
N_CHAN = 8


def level_of(rng, dims, shards, low, high):
    level = 1.0
    for position, parts in shards:
        heights = jax.random.uniform(jax.random.fold_in(jax.random.fold_in(rng, 6), position), (parts,), jnp.float32, low / len(shards), high / len(shards))
        level = level * jnp.repeat(jnp.exp(heights), dims[position] // parts).reshape((-1,) + (1,) * (len(dims) - 1 - position))
    return level


def scatter_about(stream_key, extent, spread, limit, shards=(), held_as=jnp.bfloat16):
    gain = level_of(stream_key, extent, shards, -0.22, 0.18) if shards else 1.0
    result = jax.random.normal(stream_key, extent, jnp.float32) * spread * gain
    return jnp.minimum(jnp.maximum(result, -limit), limit).astype(held_as)


def setup_inputs(seed: int = 0, part: int = 0) -> dict:
    arg_keys = jax.random.split(jax.random.key(seed), 7)
    own_keys = jax.random.split(jax.random.fold_in(arg_keys[6], part), 7)
    return {
        "tokens": scatter_about(own_keys[0], (L, D), 1.0, 6.0, ((0, 8), (1, 8))),
        "gate_in": scatter_about(own_keys[1], (L, D), 1.0, 6.0, ((0, 8), (1, 8))),
        "mix_first": scatter_about(arg_keys[2], (B1, B1), B1 ** -0.5, 0.25),
        "mix_second": scatter_about(arg_keys[3], (B2, B2), B2 ** -0.5, 0.5),
        "twiddle": jnp.clip(jnp.exp(math.log(2.0) - 1.3862944 * jax.random.uniform(arg_keys[4], (B2, B1), jnp.float32) ** level_of(arg_keys[4], (B2, B1), ((0, 8),), -0.2, 0.2)), 0.5, 2.0),
        "out_proj": scatter_about(arg_keys[5], (D, D), D ** -0.5, 0.1875),
    }


def reference(tokens, gate_in, mix_first, mix_second, twiddle, out_proj):
    blocked = tokens.astype(jnp.float32).reshape(B2, B1, D)
    first_mixed = jnp.einsum('ik,bkc->bic', mix_first.astype(jnp.float32), blocked)
    first_mixed = (first_mixed * twiddle[:, :, None]).astype(jnp.bfloat16)
    second_mixed = jnp.einsum('jb,bic->jic', mix_second.astype(jnp.float32), first_mixed.astype(jnp.float32))
    second_mixed = second_mixed.astype(jnp.bfloat16)
    hidden = (second_mixed.reshape(L, D).astype(jnp.float32) * gate_in.astype(jnp.float32)).astype(jnp.bfloat16)
    group_width = D // N_CHAN

    def add_group(running, group):
        columns = lax.dynamic_slice_in_dim(hidden, group * group_width, group_width, 1)
        weight_rows = lax.dynamic_slice_in_dim(out_proj, group * group_width, group_width, 0)
        partial_term = jnp.dot(columns, weight_rows, preferred_element_type=jnp.float32).astype(jnp.bfloat16)
        partial_term = lax.optimization_barrier(partial_term)
        return running + partial_term.astype(jnp.float32), None

    total, unused = lax.scan(add_group, jnp.zeros((L, D), jnp.float32), jnp.arange(N_CHAN, dtype=jnp.int32))
    return total.astype(jnp.bfloat16)
```

```python
import jax
import jax.numpy as jnp
from jax import lax
from jax.sharding import PartitionSpec as P

B1 = 512
CHUNKS = 2


def _roll_lead(x, me, n, axis):
    idx = (me - jnp.arange(n)) % n
    return jnp.take(x, idx, axis=axis)


def _exchange(pieces, axis, n, me):
    out = [pieces[0]]
    for t in range(1, n):
        perm = [(d, (d + t) % n) for d in range(n)]
        out.append(lax.ppermute(pieces[t], axis, perm))
    return out


def body(tokens, gate_in, mix_first, mix_second, twiddle, out_proj):
    seq_rows, chan_cols = tokens.shape
    n_seq = lax.axis_size("seq")
    n_chan = lax.axis_size("chan")
    me_s = lax.axis_index("seq")
    me_c = lax.axis_index("chan")
    blocks_here = seq_rows // B1
    per_dev_i = B1 // n_seq
    w = per_dev_i // CHUNKS
    j_per = blocks_here // n_chan

    blocked = tokens.reshape(blocks_here, B1, chan_cols)
    first = jnp.einsum("ik,bkc->bic", mix_first, blocked, preferred_element_type=jnp.float32)
    first = (first * twiddle[:, :, None]).astype(jnp.bfloat16)
    first = first.reshape(blocks_here, n_seq, per_dev_i, chan_cols)

    m2 = mix_second.reshape(mix_second.shape[0], n_seq, blocks_here)
    m2 = _roll_lead(m2, me_s, n_seq, axis=1)
    gate = gate_in.reshape(blocks_here, n_seq, per_dev_i, chan_cols)
    gate = _roll_lead(gate, me_s, n_seq, axis=1)
    wts = out_proj.reshape(n_chan, chan_cols, out_proj.shape[1])
    wts = _roll_lead(wts, me_c, n_chan, axis=0)

    outs = []
    for k in range(CHUNKS):
        sl = slice(k * w, (k + 1) * w)
        part = first[:, :, sl, :]
        send = [lax.dynamic_index_in_dim(part, (me_s + t) % n_seq, axis=1, keepdims=False) for t in range(n_seq)]
        recv = jnp.stack(_exchange(send, "seq", n_seq, me_s))
        second = jnp.einsum("jtb,tbic->jic", m2, recv, preferred_element_type=jnp.float32)
        second = second.astype(jnp.bfloat16).reshape(n_seq, blocks_here, w, chan_cols)
        send = [lax.dynamic_index_in_dim(second, (me_s + t) % n_seq, axis=0, keepdims=False) for t in range(n_seq)]
        back = jnp.stack(_exchange(send, "seq", n_seq, me_s), axis=1)
        hidden = (back.astype(jnp.float32) * gate[:, :, sl, :].astype(jnp.float32)).astype(jnp.bfloat16)
        hidden = hidden.reshape(n_chan, j_per, n_seq, w, chan_cols)
        send = [lax.dynamic_index_in_dim(hidden, (me_c + t) % n_chan, axis=0, keepdims=False) for t in range(n_chan)]
        rows = jnp.stack(_exchange(send, "chan", n_chan, me_c))
        mixed = jnp.einsum("tjswc,tcd->jswd", rows, wts, preferred_element_type=jnp.float32)
        mixed = mixed.astype(jnp.bfloat16).reshape(j_per, n_seq, w, n_chan, chan_cols)
        send = [lax.dynamic_index_in_dim(mixed, (me_c + t) % n_chan, axis=3, keepdims=False) for t in range(n_chan)]
        got = jnp.stack(_exchange(send, "chan", n_chan, me_c))
        outs.append(got)
    res = jnp.stack(outs, axis=4)
    res = res.reshape(n_chan, j_per, n_seq, w, CHUNKS, chan_cols)
    src_c = (me_c - jnp.arange(n_chan)) % n_chan
    inv_c = (me_c - jnp.arange(n_chan)) % n_chan
    res = jnp.take(res, inv_c, axis=0)
    res = jnp.take(res, (me_s - jnp.arange(n_seq)) % n_seq, axis=2)
    del src_c
    res = jnp.transpose(res, (0, 1, 2, 4, 3, 5))
    return res.reshape(seq_rows, chan_cols)


def solution(mesh):
    placed = (
        P(("batch", "seq"), "chan"),
        P(("batch", "seq"), "chan"),
        P(),
        P(),
        P("seq", None),
        P(),
    )
    return jax.shard_map(
        body, mesh=mesh, in_specs=placed, out_specs=P(("batch", "seq"), "chan"), check_vma=False
    )
```

```python
import jax
import jax.numpy as jnp
from jax import lax
from jax.sharding import PartitionSpec as P

B1 = 512


def body(tokens, gate_in, mix_first, mix_second, twiddle, out_proj):
    seq_rows, chan_cols = tokens.shape
    n_seq = lax.axis_size("seq")
    n_chan = lax.axis_size("chan")
    blocks_here = seq_rows // B1
    per_dev_i = B1 // n_seq
    d_out = out_proj.shape[1]

    blocked = tokens.reshape(blocks_here, B1, chan_cols)
    mf = mix_first.reshape(n_seq, per_dev_i, B1)
    tw = twiddle.reshape(blocks_here, n_seq, per_dev_i).transpose(1, 0, 2)
    first = jnp.einsum("dik,bkc->dbic", mf, blocked, preferred_element_type=jnp.float32)
    first = (first * tw[:, :, :, None]).astype(jnp.bfloat16)
    got = lax.all_to_all(first, "seq", split_axis=0, concat_axis=0, tiled=False)
    got = got.reshape(n_seq * blocks_here, per_dev_i * chan_cols)
    second = jnp.dot(mix_second, got, preferred_element_type=jnp.float32).astype(jnp.bfloat16)
    second = second.reshape(n_seq, blocks_here, per_dev_i, chan_cols)
    back = lax.all_to_all(second, "seq", split_axis=0, concat_axis=0, tiled=False)
    back = back.transpose(1, 0, 2, 3).reshape(seq_rows, chan_cols)
    hidden = (back.astype(jnp.float32) * gate_in.astype(jnp.float32)).astype(jnp.bfloat16)
    rows_per = seq_rows // n_chan
    hidden = hidden.reshape(n_chan, rows_per, chan_cols)
    full = lax.all_to_all(hidden, "chan", split_axis=0, concat_axis=0, tiled=False)
    wts = out_proj.reshape(n_chan, chan_cols, n_chan, d_out // n_chan)
    mixed = jnp.einsum("spc,scex->epx", full, wts, preferred_element_type=jnp.float32)
    mixed = mixed.astype(jnp.bfloat16)
    res = lax.all_to_all(mixed, "chan", split_axis=0, concat_axis=0, tiled=False)
    return res.reshape(seq_rows, chan_cols)


def solution(mesh):
    placed = (
        P(("batch", "seq"), "chan"),
        P(("batch", "seq"), "chan"),
        P(),
        P(),
        P("seq", None),
        P(),
    )
    return jax.shard_map(
        body, mesh=mesh, in_specs=placed, out_specs=P(("batch", "seq"), "chan"), check_vma=False
    )
```

```python
import functools

import jax
import jax.numpy as jnp
from jax import lax
from jax.sharding import PartitionSpec as P
from jax.experimental import pallas as pl
from jax.experimental.pallas import tpu as pltpu

B1 = 512


def _a2a_kernel(axis, n, x_ref, o_ref, send_sem, recv_sem, loc_sem):
    me = lax.axis_index(axis)
    barrier = pltpu.get_barrier_semaphore()
    for t in range(1, n):
        pl.semaphore_signal(barrier, inc=1, device_id={axis: (me + t) % n},
                            device_id_type=pl.DeviceIdType.MESH)
    pl.semaphore_wait(barrier, n - 1)
    local = pltpu.make_async_copy(x_ref.at[me], o_ref.at[me], loc_sem)
    local.start()
    copies = []
    for t in range(1, n):
        dst = (me + t) % n
        c = pltpu.make_async_remote_copy(
            src_ref=x_ref.at[dst],
            dst_ref=o_ref.at[me],
            send_sem=send_sem.at[t],
            recv_sem=recv_sem.at[t],
            device_id={axis: dst},
            device_id_type=pl.DeviceIdType.MESH,
        )
        c.start()
        copies.append(c)
    local.wait()
    for c in copies:
        c.wait_send()
    for c in copies:
        c.wait_recv()


def _a2a(x, axis, cid):
    n = x.shape[0]
    return pl.pallas_call(
        functools.partial(_a2a_kernel, axis, n),
        out_shape=jax.ShapeDtypeStruct(x.shape, x.dtype),
        in_specs=[pl.BlockSpec(memory_space=pl.ANY)],
        out_specs=pl.BlockSpec(memory_space=pl.ANY),
        scratch_shapes=[
            pltpu.SemaphoreType.DMA((n,)),
            pltpu.SemaphoreType.DMA((n,)),
            pltpu.SemaphoreType.DMA,
        ],
        compiler_params=pltpu.CompilerParams(collective_id=cid, has_side_effects=True),
    )(x)


def body(tokens, gate_in, mix_first, mix_second, twiddle, out_proj):
    seq_rows, chan_cols = tokens.shape
    n_seq = lax.axis_size("seq")
    n_chan = lax.axis_size("chan")
    blocks_here = seq_rows // B1
    per_dev_i = B1 // n_seq
    d_out = out_proj.shape[1]

    blocked = tokens.reshape(blocks_here, B1, chan_cols)
    mf = mix_first.reshape(n_seq, per_dev_i, B1)
    tw = twiddle.reshape(blocks_here, n_seq, per_dev_i).transpose(1, 0, 2)
    first = jnp.einsum("dik,bkc->dbic", mf, blocked, preferred_element_type=jnp.float32)
    first = (first * tw[:, :, :, None]).astype(jnp.bfloat16)
    got = _a2a(first, "seq", 0)
    got = got.reshape(n_seq * blocks_here, per_dev_i * chan_cols)
    second = jnp.dot(mix_second, got, preferred_element_type=jnp.float32).astype(jnp.bfloat16)
    second = second.reshape(n_seq, blocks_here, per_dev_i, chan_cols)
    back = _a2a(second, "seq", 1)
    back = back.transpose(1, 0, 2, 3).reshape(seq_rows, chan_cols)
    hidden = (back.astype(jnp.float32) * gate_in.astype(jnp.float32)).astype(jnp.bfloat16)
    rows_per = seq_rows // n_chan
    hidden = hidden.reshape(n_chan, rows_per, chan_cols)
    full = _a2a(hidden, "chan", 2)
    wts = out_proj.reshape(n_chan, chan_cols, n_chan, d_out // n_chan)
    mixed = jnp.einsum("spc,scex->epx", full, wts, preferred_element_type=jnp.float32)
    mixed = mixed.astype(jnp.bfloat16)
    res = _a2a(mixed, "chan", 3)
    return res.reshape(seq_rows, chan_cols)


def solution(mesh):
    placed = (
        P(("batch", "seq"), "chan"),
        P(("batch", "seq"), "chan"),
        P(),
        P(),
        P("seq", None),
        P(),
    )
    return jax.shard_map(
        body, mesh=mesh, in_specs=placed, out_specs=P(("batch", "seq"), "chan"), check_vma=False
    )
```

```python
import functools

import jax
import jax.numpy as jnp
from jax import lax
from jax.sharding import PartitionSpec as P
from jax.experimental import pallas as pl
from jax.experimental.pallas import tpu as pltpu

B1 = 512
CHUNKS = 4


def _a2a_kernel(axis, n, x_ref, o_ref, send_sem, recv_sem, loc_sem):
    me = lax.axis_index(axis)
    barrier = pltpu.get_barrier_semaphore()
    for t in range(1, n):
        pl.semaphore_signal(barrier, inc=1, device_id={axis: (me + t) % n},
                            device_id_type=pl.DeviceIdType.MESH)
    pl.semaphore_wait(barrier, n - 1)
    local = pltpu.make_async_copy(x_ref.at[me], o_ref.at[me], loc_sem)
    local.start()
    copies = []
    for t in range(1, n):
        dst = (me + t) % n
        c = pltpu.make_async_remote_copy(
            src_ref=x_ref.at[dst],
            dst_ref=o_ref.at[me],
            send_sem=send_sem.at[t],
            recv_sem=recv_sem.at[t],
            device_id={axis: dst},
            device_id_type=pl.DeviceIdType.MESH,
        )
        c.start()
        copies.append(c)
    local.wait()
    for c in copies:
        c.wait_send()
    for c in copies:
        c.wait_recv()


def _a2a(x, axis, cid):
    n = x.shape[0]
    return pl.pallas_call(
        functools.partial(_a2a_kernel, axis, n),
        out_shape=jax.ShapeDtypeStruct(x.shape, x.dtype),
        in_specs=[pl.BlockSpec(memory_space=pl.ANY)],
        out_specs=pl.BlockSpec(memory_space=pl.ANY),
        scratch_shapes=[
            pltpu.SemaphoreType.DMA((n,)),
            pltpu.SemaphoreType.DMA((n,)),
            pltpu.SemaphoreType.DMA,
        ],
        compiler_params=pltpu.CompilerParams(collective_id=cid, has_side_effects=True),
    )(x)


def _back_gate_send_kernel(k_chunks, second_ref, gate_ref, full_ref, recv_s, gv, hid,
                           s_send, s_recv, c_send, c_recv, g_sem):
    n_s, n_j, n_i, _ = second_ref.shape
    n_c = full_ref.shape[0]
    jp = n_j // n_c
    w = n_i // k_chunks
    me_s = lax.axis_index("seq")
    me_c = lax.axis_index("chan")
    mesh_ids = pl.DeviceIdType.MESH
    barrier = pltpu.get_barrier_semaphore()
    for t in range(1, n_s):
        pl.semaphore_signal(barrier, inc=1, device_id={"seq": (me_s + t) % n_s}, device_id_type=mesh_ids)
    for t in range(1, n_c):
        pl.semaphore_signal(barrier, inc=1, device_id={"chan": (me_c + t) % n_c}, device_id_type=mesh_ids)
    pl.semaphore_wait(barrier, (n_s - 1) + (n_c - 1))

    gcopy = pltpu.make_async_copy(gate_ref, gv, g_sem)
    gcopy.start()
    seq_copies = []
    for k in range(k_chunks):
        isl = pl.ds(k * w, w)
        row = []
        for t in range(n_s):
            if t == 0:
                c = pltpu.make_async_copy(second_ref.at[me_s, :, isl], recv_s.at[me_s, :, isl], s_recv.at[k, 0])
            else:
                dst = (me_s + t) % n_s
                c = pltpu.make_async_remote_copy(
                    src_ref=second_ref.at[dst, :, isl],
                    dst_ref=recv_s.at[me_s, :, isl],
                    send_sem=s_send.at[k, t],
                    recv_sem=s_recv.at[k, t],
                    device_id={"seq": dst},
                    device_id_type=mesh_ids,
                )
            c.start()
            row.append(c)
        seq_copies.append(row)
    gcopy.wait()
    chan_copies = []
    for k in range(k_chunks):
        isl = pl.ds(k * w, w)
        for t in range(n_s):
            if t == 0:
                seq_copies[k][t].wait()
            else:
                seq_copies[k][t].wait_recv()
        for s in range(n_s):
            prod = recv_s[s, :, isl, :].astype(jnp.float32) * gv[:, s, isl, :].astype(jnp.float32)
            hid[:, s, isl, :] = prod.astype(hid.dtype)
        for t in range(n_c):
            dst = (me_c + t) % n_c
            src_view = hid.at[pl.ds(dst * jp, jp), :, isl, :]
            dst_view = full_ref.at[me_c, :, :, isl, :]
            if t == 0:
                c = pltpu.make_async_copy(src_view, dst_view, c_recv.at[k, 0])
            else:
                c = pltpu.make_async_remote_copy(
                    src_ref=src_view,
                    dst_ref=dst_view,
                    send_sem=c_send.at[k, t],
                    recv_sem=c_recv.at[k, t],
                    device_id={"chan": dst},
                    device_id_type=mesh_ids,
                )
            c.start()
            chan_copies.append((t, c))
    for row in seq_copies:
        for c in row[1:]:
            c.wait_send()
    for t, c in chan_copies:
        if t == 0:
            c.wait()
        else:
            c.wait_send()
    for t, c in chan_copies:
        if t != 0:
            c.wait_recv()


def _back_gate_send(second, gate, n_c, k_chunks, cid):
    n_s, n_j, n_i, cols = second.shape
    jp = n_j // n_c
    return pl.pallas_call(
        functools.partial(_back_gate_send_kernel, k_chunks),
        out_shape=jax.ShapeDtypeStruct((n_c, jp, n_s, n_i, cols), second.dtype),
        in_specs=[pl.BlockSpec(memory_space=pl.ANY)] * 2,
        out_specs=pl.BlockSpec(memory_space=pl.ANY),
        scratch_shapes=[
            pltpu.VMEM((n_s, n_j, n_i, cols), second.dtype),
            pltpu.VMEM((n_j, n_s, n_i, cols), second.dtype),
            pltpu.VMEM((n_j, n_s, n_i, cols), second.dtype),
            pltpu.SemaphoreType.DMA((k_chunks, n_s)),
            pltpu.SemaphoreType.DMA((k_chunks, n_s)),
            pltpu.SemaphoreType.DMA((k_chunks, n_c)),
            pltpu.SemaphoreType.DMA((k_chunks, n_c)),
            pltpu.SemaphoreType.DMA,
        ],
        compiler_params=pltpu.CompilerParams(collective_id=cid, has_side_effects=True),
    )(second, gate)


def body(tokens, gate_in, mix_first, mix_second, twiddle, out_proj):
    seq_rows, chan_cols = tokens.shape
    n_seq = lax.axis_size("seq")
    n_chan = lax.axis_size("chan")
    blocks_here = seq_rows // B1
    per_dev_i = B1 // n_seq
    d_out = out_proj.shape[1]

    blocked = tokens.reshape(blocks_here, B1, chan_cols)
    mf = mix_first.reshape(n_seq, per_dev_i, B1)
    tw = twiddle.reshape(blocks_here, n_seq, per_dev_i).transpose(1, 0, 2)
    first = jnp.einsum("dik,bkc->dbic", mf, blocked, preferred_element_type=jnp.float32)
    first = (first * tw[:, :, :, None]).astype(jnp.bfloat16)
    got = _a2a(first, "seq", 0)
    got = got.reshape(n_seq * blocks_here, per_dev_i * chan_cols)
    second = jnp.dot(mix_second, got, preferred_element_type=jnp.float32).astype(jnp.bfloat16)
    second = second.reshape(n_seq, blocks_here, per_dev_i, chan_cols)
    gate = gate_in.reshape(blocks_here, n_seq, per_dev_i, chan_cols)
    full = _back_gate_send(second, gate, n_chan, CHUNKS, 1)
    rows_per = seq_rows // n_chan
    full = full.reshape(n_chan, rows_per, chan_cols)
    wts = out_proj.reshape(n_chan, chan_cols, n_chan, d_out // n_chan)
    mixed = jnp.einsum("spc,scex->epx", full, wts, preferred_element_type=jnp.float32)
    mixed = mixed.astype(jnp.bfloat16)
    res = _a2a(mixed, "chan", 3)
    return res.reshape(seq_rows, chan_cols)


def solution(mesh):
    placed = (
        P(("batch", "seq"), "chan"),
        P(("batch", "seq"), "chan"),
        P(),
        P(),
        P("seq", None),
        P(),
    )
    return jax.shard_map(
        body, mesh=mesh, in_specs=placed, out_specs=P(("batch", "seq"), "chan"), check_vma=False
    )
```

```python
import functools

import jax
import jax.numpy as jnp
from jax import lax
from jax.sharding import PartitionSpec as P
from jax.experimental import pallas as pl
from jax.experimental.pallas import tpu as pltpu

B1 = 512
CHUNKS = 4
LEAD = 2


def _a2a_kernel(axis, n, x_ref, o_ref, send_sem, recv_sem, loc_sem):
    me = lax.axis_index(axis)
    barrier = pltpu.get_barrier_semaphore()
    for t in range(1, n):
        pl.semaphore_signal(barrier, inc=1, device_id={axis: (me + t) % n},
                            device_id_type=pl.DeviceIdType.MESH)
    pl.semaphore_wait(barrier, n - 1)
    local = pltpu.make_async_copy(x_ref.at[me], o_ref.at[me], loc_sem)
    local.start()
    copies = []
    for t in range(1, n):
        dst = (me + t) % n
        c = pltpu.make_async_remote_copy(
            src_ref=x_ref.at[dst],
            dst_ref=o_ref.at[me],
            send_sem=send_sem.at[t],
            recv_sem=recv_sem.at[t],
            device_id={axis: dst},
            device_id_type=pl.DeviceIdType.MESH,
        )
        c.start()
        copies.append(c)
    local.wait()
    for c in copies:
        c.wait_send()
    for c in copies:
        c.wait_recv()


def _a2a(x, axis, cid):
    n = x.shape[0]
    return pl.pallas_call(
        functools.partial(_a2a_kernel, axis, n),
        out_shape=jax.ShapeDtypeStruct(x.shape, x.dtype),
        in_specs=[pl.BlockSpec(memory_space=pl.ANY)],
        out_specs=pl.BlockSpec(memory_space=pl.ANY),
        scratch_shapes=[
            pltpu.SemaphoreType.DMA((n,)),
            pltpu.SemaphoreType.DMA((n,)),
            pltpu.SemaphoreType.DMA,
        ],
        compiler_params=pltpu.CompilerParams(collective_id=cid, has_side_effects=True),
    )(x)


def _back_gate_send_kernel(k_chunks, second_ref, gate_ref, full_ref, recv_s, gv, hid,
                           s_send, s_recv, c_send, c_recv, g_sem):
    n_s, n_j, n_i, _ = second_ref.shape
    n_c = full_ref.shape[0]
    jp = n_j // n_c
    w = n_i // k_chunks
    me_s = lax.axis_index("seq")
    me_c = lax.axis_index("chan")
    mesh_ids = pl.DeviceIdType.MESH
    barrier = pltpu.get_barrier_semaphore()
    for t in range(1, n_s):
        pl.semaphore_signal(barrier, inc=1, device_id={"seq": (me_s + t) % n_s}, device_id_type=mesh_ids)
    for t in range(1, n_c):
        pl.semaphore_signal(barrier, inc=1, device_id={"chan": (me_c + t) % n_c}, device_id_type=mesh_ids)
    pl.semaphore_wait(barrier, (n_s - 1) + (n_c - 1))

    gcopy = pltpu.make_async_copy(gate_ref, gv, g_sem)
    gcopy.start()
    def issue_seq(k):
        isl = pl.ds(k * w, w)
        row = []
        for t in range(n_s):
            if t == 0:
                c = pltpu.make_async_copy(second_ref.at[me_s, :, isl], recv_s.at[me_s, :, isl], s_recv.at[k, 0])
            else:
                dst = (me_s + t) % n_s
                c = pltpu.make_async_remote_copy(
                    src_ref=second_ref.at[dst, :, isl],
                    dst_ref=recv_s.at[me_s, :, isl],
                    send_sem=s_send.at[k, t],
                    recv_sem=s_recv.at[k, t],
                    device_id={"seq": dst},
                    device_id_type=mesh_ids,
                )
            c.start()
            row.append(c)
        return row

    seq_copies = [issue_seq(k) for k in range(min(LEAD, k_chunks))]
    gcopy.wait()
    chan_copies = []
    for k in range(k_chunks):
        isl = pl.ds(k * w, w)
        for t in range(n_s):
            if t == 0:
                seq_copies[k][t].wait()
            else:
                seq_copies[k][t].wait_recv()
        for s in range(n_s):
            prod = recv_s[s, :, isl, :].astype(jnp.float32) * gv[:, s, isl, :].astype(jnp.float32)
            hid[:, s, isl, :] = prod.astype(hid.dtype)
        for t in range(n_c):
            dst = (me_c + t) % n_c
            src_view = hid.at[pl.ds(dst * jp, jp), :, isl, :]
            dst_view = full_ref.at[me_c, :, :, isl, :]
            if t == 0:
                c = pltpu.make_async_copy(src_view, dst_view, c_recv.at[k, 0])
            else:
                c = pltpu.make_async_remote_copy(
                    src_ref=src_view,
                    dst_ref=dst_view,
                    send_sem=c_send.at[k, t],
                    recv_sem=c_recv.at[k, t],
                    device_id={"chan": dst},
                    device_id_type=mesh_ids,
                )
            c.start()
            chan_copies.append((t, c))
        if k + LEAD < k_chunks:
            seq_copies.append(issue_seq(k + LEAD))
    for row in seq_copies:
        for c in row[1:]:
            c.wait_send()
    for t, c in chan_copies:
        if t == 0:
            c.wait()
        else:
            c.wait_send()
    for t, c in chan_copies:
        if t != 0:
            c.wait_recv()


def _back_gate_send(second, gate, n_c, k_chunks, cid):
    n_s, n_j, n_i, cols = second.shape
    jp = n_j // n_c
    return pl.pallas_call(
        functools.partial(_back_gate_send_kernel, k_chunks),
        out_shape=jax.ShapeDtypeStruct((n_c, jp, n_s, n_i, cols), second.dtype),
        in_specs=[pl.BlockSpec(memory_space=pl.ANY)] * 2,
        out_specs=pl.BlockSpec(memory_space=pl.ANY),
        scratch_shapes=[
            pltpu.VMEM((n_s, n_j, n_i, cols), second.dtype),
            pltpu.VMEM((n_j, n_s, n_i, cols), second.dtype),
            pltpu.VMEM((n_j, n_s, n_i, cols), second.dtype),
            pltpu.SemaphoreType.DMA((k_chunks, n_s)),
            pltpu.SemaphoreType.DMA((k_chunks, n_s)),
            pltpu.SemaphoreType.DMA((k_chunks, n_c)),
            pltpu.SemaphoreType.DMA((k_chunks, n_c)),
            pltpu.SemaphoreType.DMA,
        ],
        compiler_params=pltpu.CompilerParams(collective_id=cid, has_side_effects=True),
    )(second, gate)


def body(tokens, gate_in, mix_first, mix_second, twiddle, out_proj):
    seq_rows, chan_cols = tokens.shape
    n_seq = lax.axis_size("seq")
    n_chan = lax.axis_size("chan")
    blocks_here = seq_rows // B1
    per_dev_i = B1 // n_seq
    d_out = out_proj.shape[1]

    blocked = tokens.reshape(blocks_here, B1, chan_cols)
    mf = mix_first.reshape(n_seq, per_dev_i, B1)
    tw = twiddle.reshape(blocks_here, n_seq, per_dev_i).transpose(1, 0, 2)
    first = jnp.einsum("dik,bkc->dbic", mf, blocked, preferred_element_type=jnp.float32)
    first = (first * tw[:, :, :, None]).astype(jnp.bfloat16)
    got = _a2a(first, "seq", 0)
    got = got.reshape(n_seq * blocks_here, per_dev_i * chan_cols)
    second = jnp.dot(mix_second, got, preferred_element_type=jnp.float32).astype(jnp.bfloat16)
    second = second.reshape(n_seq, blocks_here, per_dev_i, chan_cols)
    gate = gate_in.reshape(blocks_here, n_seq, per_dev_i, chan_cols)
    full = _back_gate_send(second, gate, n_chan, CHUNKS, 1)
    rows_per = seq_rows // n_chan
    full = full.reshape(n_chan, rows_per, chan_cols)
    wts = out_proj.reshape(n_chan, chan_cols, n_chan, d_out // n_chan)
    mixed = jnp.einsum("spc,scex->epx", full, wts, preferred_element_type=jnp.float32)
    mixed = mixed.astype(jnp.bfloat16)
    res = _a2a(mixed, "chan", 3)
    return res.reshape(seq_rows, chan_cols)


def solution(mesh):
    placed = (
        P(("batch", "seq"), "chan"),
        P(("batch", "seq"), "chan"),
        P(),
        P(),
        P("seq", None),
        P(),
    )
    return jax.shard_map(
        body, mesh=mesh, in_specs=placed, out_specs=P(("batch", "seq"), "chan"), check_vma=False
    )
```

```python
import functools

import jax
import jax.numpy as jnp
from jax import lax
from jax.sharding import PartitionSpec as P
from jax.experimental import pallas as pl
from jax.experimental.pallas import tpu as pltpu

B1 = 512
CHUNKS = 4
LEAD = 2


def _a2a_kernel(axis, n, x_ref, o_ref, send_sem, recv_sem, loc_sem):
    me = lax.axis_index(axis)
    barrier = pltpu.get_barrier_semaphore()
    for t in range(1, n):
        pl.semaphore_signal(barrier, inc=1, device_id={axis: (me + t) % n},
                            device_id_type=pl.DeviceIdType.MESH)
    pl.semaphore_wait(barrier, n - 1)
    local = pltpu.make_async_copy(x_ref.at[me], o_ref.at[me], loc_sem)
    local.start()
    copies = []
    for t in range(1, n):
        dst = (me + t) % n
        c = pltpu.make_async_remote_copy(
            src_ref=x_ref.at[dst],
            dst_ref=o_ref.at[me],
            send_sem=send_sem.at[t],
            recv_sem=recv_sem.at[t],
            device_id={axis: dst},
            device_id_type=pl.DeviceIdType.MESH,
        )
        c.start()
        copies.append(c)
    local.wait()
    for c in copies:
        c.wait_send()
    for c in copies:
        c.wait_recv()


def _a2a(x, axis, cid):
    n = x.shape[0]
    return pl.pallas_call(
        functools.partial(_a2a_kernel, axis, n),
        out_shape=jax.ShapeDtypeStruct(x.shape, x.dtype),
        in_specs=[pl.BlockSpec(memory_space=pl.ANY)],
        out_specs=pl.BlockSpec(memory_space=pl.ANY),
        scratch_shapes=[
            pltpu.SemaphoreType.DMA((n,)),
            pltpu.SemaphoreType.DMA((n,)),
            pltpu.SemaphoreType.DMA,
        ],
        compiler_params=pltpu.CompilerParams(collective_id=cid, has_side_effects=True),
    )(x)


def _back_gate_send_kernel(k_chunks, second_ref, gate_ref, full_ref, recv_s, gv, hid,
                           s_send, s_recv, c_send, c_recv, g_sem):
    n_s, n_j, n_i, _ = second_ref.shape
    n_c = full_ref.shape[0]
    jp = n_j // n_c
    w = n_i // k_chunks
    me_s = lax.axis_index("seq")
    me_c = lax.axis_index("chan")
    mesh_ids = pl.DeviceIdType.MESH
    barrier = pltpu.get_barrier_semaphore()
    for t in range(1, n_s):
        pl.semaphore_signal(barrier, inc=1, device_id={"seq": (me_s + t) % n_s}, device_id_type=mesh_ids)
    for t in range(1, n_c):
        pl.semaphore_signal(barrier, inc=1, device_id={"chan": (me_c + t) % n_c}, device_id_type=mesh_ids)
    pl.semaphore_wait(barrier, (n_s - 1) + (n_c - 1))

    gcopy = pltpu.make_async_copy(gate_ref, gv, g_sem)
    gcopy.start()
    def issue_seq(k):
        isl = pl.ds(k * w, w)
        row = []
        for t in range(n_s):
            if t == 0:
                c = pltpu.make_async_copy(second_ref.at[me_s, :, isl], recv_s.at[me_s, :, isl], s_recv.at[k, 0])
            else:
                dst = (me_s + t) % n_s
                c = pltpu.make_async_remote_copy(
                    src_ref=second_ref.at[dst, :, isl],
                    dst_ref=recv_s.at[me_s, :, isl],
                    send_sem=s_send.at[k, t],
                    recv_sem=s_recv.at[k, t],
                    device_id={"seq": dst},
                    device_id_type=mesh_ids,
                )
            c.start()
            row.append(c)
        return row

    seq_copies = [issue_seq(k) for k in range(min(LEAD, k_chunks))]
    gcopy.wait()
    chan_copies = []
    for k in range(k_chunks):
        isl = pl.ds(k * w, w)
        for t in range(n_s):
            if t == 0:
                seq_copies[k][t].wait()
            else:
                seq_copies[k][t].wait_recv()
        for s in range(n_s):
            prod = recv_s[s, :, isl, :].astype(jnp.float32) * gv[:, pl.ds(s * n_i + k * w, w), :].astype(jnp.float32)
            hid[:, s, isl, :] = prod.astype(hid.dtype)
        for t in range(n_c):
            dst = (me_c + t) % n_c
            src_view = hid.at[pl.ds(dst * jp, jp), :, isl, :]
            dst_view = full_ref.at[me_c, :, :, isl, :]
            if t == 0:
                c = pltpu.make_async_copy(src_view, dst_view, c_recv.at[k, 0])
            else:
                c = pltpu.make_async_remote_copy(
                    src_ref=src_view,
                    dst_ref=dst_view,
                    send_sem=c_send.at[k, t],
                    recv_sem=c_recv.at[k, t],
                    device_id={"chan": dst},
                    device_id_type=mesh_ids,
                )
            c.start()
            chan_copies.append((t, c))
        if k + LEAD < k_chunks:
            seq_copies.append(issue_seq(k + LEAD))
    for row in seq_copies:
        for c in row[1:]:
            c.wait_send()
    for t, c in chan_copies:
        if t == 0:
            c.wait()
        else:
            c.wait_send()
    for t, c in chan_copies:
        if t != 0:
            c.wait_recv()


def _back_gate_send(second, gate, n_c, k_chunks, cid):
    n_s, n_j, n_i, cols = second.shape
    jp = n_j // n_c
    return pl.pallas_call(
        functools.partial(_back_gate_send_kernel, k_chunks),
        out_shape=jax.ShapeDtypeStruct((n_c, jp, n_s, n_i, cols), second.dtype),
        in_specs=[pl.BlockSpec(memory_space=pl.ANY)] * 2,
        out_specs=pl.BlockSpec(memory_space=pl.ANY),
        scratch_shapes=[
            pltpu.VMEM((n_s, n_j, n_i, cols), second.dtype),
            pltpu.VMEM((n_j, n_s * n_i, cols), second.dtype),
            pltpu.VMEM((n_j, n_s, n_i, cols), second.dtype),
            pltpu.SemaphoreType.DMA((k_chunks, n_s)),
            pltpu.SemaphoreType.DMA((k_chunks, n_s)),
            pltpu.SemaphoreType.DMA((k_chunks, n_c)),
            pltpu.SemaphoreType.DMA((k_chunks, n_c)),
            pltpu.SemaphoreType.DMA,
        ],
        compiler_params=pltpu.CompilerParams(collective_id=cid, has_side_effects=True),
    )(second, gate)


def _mix_blocks_kernel(m_ref, x_ref, o_ref):
    m = m_ref[...]
    for i in range(x_ref.shape[1]):
        o_ref[:, i, :] = jnp.dot(m, x_ref[:, i, :], preferred_element_type=jnp.float32).astype(o_ref.dtype)


def _mix_blocks(m, x, tile=16):
    rows, n_i, cols = x.shape
    return pl.pallas_call(
        _mix_blocks_kernel,
        out_shape=jax.ShapeDtypeStruct((m.shape[0], n_i, cols), x.dtype),
        grid=(n_i // tile,),
        in_specs=[
            pl.BlockSpec((m.shape[0], rows), lambda t: (0, 0)),
            pl.BlockSpec((rows, tile, cols), lambda t: (0, t, 0)),
        ],
        out_specs=pl.BlockSpec((m.shape[0], tile, cols), lambda t: (0, t, 0)),
    )(m, x)


def body(tokens, gate_in, mix_first, mix_second, twiddle, out_proj):
    seq_rows, chan_cols = tokens.shape
    n_seq = lax.axis_size("seq")
    n_chan = lax.axis_size("chan")
    blocks_here = seq_rows // B1
    per_dev_i = B1 // n_seq
    d_out = out_proj.shape[1]

    blocked = tokens.reshape(blocks_here, B1, chan_cols)
    mf = mix_first.reshape(n_seq, per_dev_i, B1)
    tw = twiddle.reshape(blocks_here, n_seq, per_dev_i).transpose(1, 0, 2)
    first = jnp.einsum("dik,bkc->dbic", mf, blocked, preferred_element_type=jnp.float32)
    first = (first * tw[:, :, :, None]).astype(jnp.bfloat16)
    got = _a2a(first, "seq", 0)
    got = got.reshape(n_seq * blocks_here, per_dev_i, chan_cols)
    second = _mix_blocks(mix_second, got).reshape(n_seq, blocks_here, per_dev_i, chan_cols)
    gate = gate_in.reshape(blocks_here, B1, chan_cols)
    full = _back_gate_send(second, gate, n_chan, CHUNKS, 1)
    rows_per = seq_rows // n_chan
    full = full.reshape(n_chan, rows_per, chan_cols)
    wts = out_proj.reshape(n_chan, chan_cols, n_chan, d_out // n_chan)
    mixed = jnp.einsum("spc,scex->epx", full, wts, preferred_element_type=jnp.float32)
    mixed = mixed.astype(jnp.bfloat16)
    res = _a2a(mixed, "chan", 3)
    return res.reshape(seq_rows, chan_cols)


def solution(mesh):
    placed = (
        P(("batch", "seq"), "chan"),
        P(("batch", "seq"), "chan"),
        P(),
        P(),
        P("seq", None),
        P(),
    )
    return jax.shard_map(
        body, mesh=mesh, in_specs=placed, out_specs=P(("batch", "seq"), "chan"), check_vma=False
    )
```

```python
import functools

import jax
import jax.numpy as jnp
from jax import lax
from jax.sharding import PartitionSpec as P
from jax.experimental import pallas as pl
from jax.experimental.pallas import tpu as pltpu

B1 = 512
CHUNKS = 4
LEAD = 2


def _a2a_kernel(axis, n, x_ref, o_ref, send_sem, recv_sem, loc_sem):
    me = lax.axis_index(axis)
    barrier = pltpu.get_barrier_semaphore()
    for t in range(1, n):
        pl.semaphore_signal(barrier, inc=1, device_id={axis: (me + t) % n},
                            device_id_type=pl.DeviceIdType.MESH)
    pl.semaphore_wait(barrier, n - 1)
    local = pltpu.make_async_copy(x_ref.at[me], o_ref.at[me], loc_sem)
    local.start()
    copies = []
    for t in range(1, n):
        dst = (me + t) % n
        c = pltpu.make_async_remote_copy(
            src_ref=x_ref.at[dst],
            dst_ref=o_ref.at[me],
            send_sem=send_sem.at[t],
            recv_sem=recv_sem.at[t],
            device_id={axis: dst},
            device_id_type=pl.DeviceIdType.MESH,
        )
        c.start()
        copies.append(c)
    local.wait()
    for c in copies:
        c.wait_send()
    for c in copies:
        c.wait_recv()


def _a2a(x, axis, cid):
    n = x.shape[0]
    return pl.pallas_call(
        functools.partial(_a2a_kernel, axis, n),
        out_shape=jax.ShapeDtypeStruct(x.shape, x.dtype),
        in_specs=[pl.BlockSpec(memory_space=pl.ANY)],
        out_specs=pl.BlockSpec(memory_space=pl.ANY),
        scratch_shapes=[
            pltpu.SemaphoreType.DMA((n,)),
            pltpu.SemaphoreType.DMA((n,)),
            pltpu.SemaphoreType.DMA,
        ],
        compiler_params=pltpu.CompilerParams(collective_id=cid, has_side_effects=True),
    )(x)


def _back_gate_send_kernel(k_chunks, second_ref, gate_ref, full_ref, recv_s, gv, hid,
                           s_send, s_recv, c_send, c_recv, g_sem):
    n_s, n_j, n_i, _ = second_ref.shape
    n_c = full_ref.shape[0]
    jp = n_j // n_c
    w = n_i // k_chunks
    me_s = lax.axis_index("seq")
    me_c = lax.axis_index("chan")
    mesh_ids = pl.DeviceIdType.MESH
    barrier = pltpu.get_barrier_semaphore()
    for t in range(1, n_s):
        pl.semaphore_signal(barrier, inc=1, device_id={"seq": (me_s + t) % n_s}, device_id_type=mesh_ids)
    for t in range(1, n_c):
        pl.semaphore_signal(barrier, inc=1, device_id={"chan": (me_c + t) % n_c}, device_id_type=mesh_ids)
    pl.semaphore_wait(barrier, (n_s - 1) + (n_c - 1))

    gcopy = pltpu.make_async_copy(gate_ref, gv, g_sem)
    gcopy.start()
    def issue_seq(k):
        isl = pl.ds(k * w, w)
        row = []
        for t in range(n_s):
            if t == 0:
                c = pltpu.make_async_copy(second_ref.at[me_s, :, isl], recv_s.at[me_s, :, isl], s_recv.at[k, 0])
            else:
                dst = (me_s + t) % n_s
                c = pltpu.make_async_remote_copy(
                    src_ref=second_ref.at[dst, :, isl],
                    dst_ref=recv_s.at[me_s, :, isl],
                    send_sem=s_send.at[k, t],
                    recv_sem=s_recv.at[k, t],
                    device_id={"seq": dst},
                    device_id_type=mesh_ids,
                )
            c.start()
            row.append(c)
        return row

    seq_copies = [issue_seq(k) for k in range(min(LEAD, k_chunks))]
    gcopy.wait()
    chan_copies = []
    for k in range(k_chunks):
        isl = pl.ds(k * w, w)
        for t in range(n_s):
            if t == 0:
                seq_copies[k][t].wait()
            else:
                seq_copies[k][t].wait_recv()
        for s in range(n_s):
            prod = recv_s[s, :, isl, :].astype(jnp.float32) * gv[:, pl.ds(s * n_i + k * w, w), :].astype(jnp.float32)
            hid[:, s, isl, :] = prod.astype(hid.dtype)
        for t in range(n_c):
            dst = (me_c + t) % n_c
            src_view = hid.at[pl.ds(dst * jp, jp), :, isl, :]
            dst_view = full_ref.at[me_c, :, :, isl, :]
            if t == 0:
                c = pltpu.make_async_copy(src_view, dst_view, c_recv.at[k, 0])
            else:
                c = pltpu.make_async_remote_copy(
                    src_ref=src_view,
                    dst_ref=dst_view,
                    send_sem=c_send.at[k, t],
                    recv_sem=c_recv.at[k, t],
                    device_id={"chan": dst},
                    device_id_type=mesh_ids,
                )
            c.start()
            chan_copies.append((t, c))
        if k + LEAD < k_chunks:
            seq_copies.append(issue_seq(k + LEAD))
    for row in seq_copies:
        for c in row[1:]:
            c.wait_send()
    for t, c in chan_copies:
        if t == 0:
            c.wait()
        else:
            c.wait_send()
    for t, c in chan_copies:
        if t != 0:
            c.wait_recv()


def _back_gate_send(second, gate, n_c, k_chunks, cid):
    n_s, n_j, n_i, cols = second.shape
    jp = n_j // n_c
    return pl.pallas_call(
        functools.partial(_back_gate_send_kernel, k_chunks),
        out_shape=jax.ShapeDtypeStruct((n_c, jp, n_s, n_i, cols), second.dtype),
        in_specs=[pl.BlockSpec(memory_space=pl.ANY)] * 2,
        out_specs=pl.BlockSpec(memory_space=pl.ANY),
        scratch_shapes=[
            pltpu.VMEM((n_s, n_j, n_i, cols), second.dtype),
            pltpu.VMEM((n_j, n_s * n_i, cols), second.dtype),
            pltpu.VMEM((n_j, n_s, n_i, cols), second.dtype),
            pltpu.SemaphoreType.DMA((k_chunks, n_s)),
            pltpu.SemaphoreType.DMA((k_chunks, n_s)),
            pltpu.SemaphoreType.DMA((k_chunks, n_c)),
            pltpu.SemaphoreType.DMA((k_chunks, n_c)),
            pltpu.SemaphoreType.DMA,
        ],
        compiler_params=pltpu.CompilerParams(collective_id=cid, has_side_effects=True),
    )(second, gate)


def _mix_blocks_kernel(m_ref, x_ref, o_ref):
    m = m_ref[...]
    for i in range(x_ref.shape[1]):
        o_ref[:, i, :] = jnp.dot(m, x_ref[:, i, :], preferred_element_type=jnp.float32).astype(o_ref.dtype)


def _mix_blocks(m, x, tile=16):
    rows, n_i, cols = x.shape
    return pl.pallas_call(
        _mix_blocks_kernel,
        out_shape=jax.ShapeDtypeStruct((m.shape[0], n_i, cols), x.dtype),
        grid=(n_i // tile,),
        in_specs=[
            pl.BlockSpec((m.shape[0], rows), lambda t: (0, 0)),
            pl.BlockSpec((rows, tile, cols), lambda t: (0, t, 0)),
        ],
        out_specs=pl.BlockSpec((m.shape[0], tile, cols), lambda t: (0, t, 0)),
    )(m, x)


def _project_send_kernel(full_ref, w_ref, res_ref, stage, send_sem, recv_sem):
    n_c, rows, cols = full_ref.shape
    me = lax.axis_index("chan")
    mesh_ids = pl.DeviceIdType.MESH
    barrier = pltpu.get_barrier_semaphore()
    for t in range(1, n_c):
        pl.semaphore_signal(barrier, inc=1, device_id={"chan": (me + t) % n_c}, device_id_type=mesh_ids)
    pl.semaphore_wait(barrier, n_c - 1)
    copies = []
    for t in list(range(1, n_c)) + [0]:
        dst = (me + t) % n_c
        out_cols = pl.ds(pl.multiple_of(dst * cols, cols), cols)
        acc = jnp.zeros((rows, cols), jnp.float32)
        for s in range(n_c):
            acc += jnp.dot(full_ref[s], w_ref[pl.ds(s * cols, cols), out_cols],
                           preferred_element_type=jnp.float32)
        stage[t] = acc.astype(stage.dtype)
        if t == 0:
            c = pltpu.make_async_copy(stage.at[t], res_ref.at[me], recv_sem.at[0])
        else:
            c = pltpu.make_async_remote_copy(
                src_ref=stage.at[t],
                dst_ref=res_ref.at[me],
                send_sem=send_sem.at[t],
                recv_sem=recv_sem.at[t],
                device_id={"chan": dst},
                device_id_type=mesh_ids,
            )
        c.start()
        copies.append((t, c))
    for t, c in copies:
        if t == 0:
            c.wait()
        else:
            c.wait_send()
    for t, c in copies:
        if t != 0:
            c.wait_recv()


def _project_send(full, w, cid):
    n_c, rows, cols = full.shape
    return pl.pallas_call(
        _project_send_kernel,
        out_shape=jax.ShapeDtypeStruct((n_c, rows, cols), full.dtype),
        in_specs=[pl.BlockSpec(memory_space=pltpu.VMEM)] * 2,
        out_specs=pl.BlockSpec(memory_space=pl.ANY),
        scratch_shapes=[
            pltpu.VMEM((n_c, rows, cols), full.dtype),
            pltpu.SemaphoreType.DMA((n_c,)),
            pltpu.SemaphoreType.DMA((n_c,)),
        ],
        compiler_params=pltpu.CompilerParams(collective_id=cid, has_side_effects=True),
    )(full, w)


def body(tokens, gate_in, mix_first, mix_second, twiddle, out_proj):
    seq_rows, chan_cols = tokens.shape
    n_seq = lax.axis_size("seq")
    n_chan = lax.axis_size("chan")
    blocks_here = seq_rows // B1
    per_dev_i = B1 // n_seq
    d_out = out_proj.shape[1]

    blocked = tokens.reshape(blocks_here, B1, chan_cols)
    mf = mix_first.reshape(n_seq, per_dev_i, B1)
    tw = twiddle.reshape(blocks_here, n_seq, per_dev_i).transpose(1, 0, 2)
    first = jnp.einsum("dik,bkc->dbic", mf, blocked, preferred_element_type=jnp.float32)
    first = (first * tw[:, :, :, None]).astype(jnp.bfloat16)
    got = _a2a(first, "seq", 0)
    got = got.reshape(n_seq * blocks_here, per_dev_i, chan_cols)
    second = _mix_blocks(mix_second, got).reshape(n_seq, blocks_here, per_dev_i, chan_cols)
    gate = gate_in.reshape(blocks_here, B1, chan_cols)
    full = _back_gate_send(second, gate, n_chan, CHUNKS, 1)
    rows_per = seq_rows // n_chan
    full = full.reshape(n_chan, rows_per, chan_cols)
    res = _project_send(full, out_proj, 3)
    return res.reshape(seq_rows, chan_cols)


def solution(mesh):
    placed = (
        P(("batch", "seq"), "chan"),
        P(("batch", "seq"), "chan"),
        P(),
        P(),
        P("seq", None),
        P(),
    )
    return jax.shard_map(
        body, mesh=mesh, in_specs=placed, out_specs=P(("batch", "seq"), "chan"), check_vma=False
    )
```

```python
import functools

import jax
import jax.numpy as jnp
from jax import lax
from jax.sharding import PartitionSpec as P
from jax.experimental import pallas as pl
from jax.experimental.pallas import tpu as pltpu

B1 = 512
CHUNKS = 4
LEAD = 2


def _a2a_kernel(axis, n, x_ref, o_ref, send_sem, recv_sem, loc_sem):
    me = lax.axis_index(axis)
    barrier = pltpu.get_barrier_semaphore()
    for t in range(1, n):
        pl.semaphore_signal(barrier, inc=1, device_id={axis: (me + t) % n},
                            device_id_type=pl.DeviceIdType.MESH)
    pl.semaphore_wait(barrier, n - 1)
    local = pltpu.make_async_copy(x_ref.at[me], o_ref.at[me], loc_sem)
    local.start()
    copies = []
    for t in range(1, n):
        dst = (me + t) % n
        c = pltpu.make_async_remote_copy(
            src_ref=x_ref.at[dst],
            dst_ref=o_ref.at[me],
            send_sem=send_sem.at[t],
            recv_sem=recv_sem.at[t],
            device_id={axis: dst},
            device_id_type=pl.DeviceIdType.MESH,
        )
        c.start()
        copies.append(c)
    local.wait()
    for c in copies:
        c.wait_send()
    for c in copies:
        c.wait_recv()


def _a2a(x, axis, cid):
    n = x.shape[0]
    return pl.pallas_call(
        functools.partial(_a2a_kernel, axis, n),
        out_shape=jax.ShapeDtypeStruct(x.shape, x.dtype),
        in_specs=[pl.BlockSpec(memory_space=pl.ANY)],
        out_specs=pl.BlockSpec(memory_space=pl.ANY),
        scratch_shapes=[
            pltpu.SemaphoreType.DMA((n,)),
            pltpu.SemaphoreType.DMA((n,)),
            pltpu.SemaphoreType.DMA,
        ],
        compiler_params=pltpu.CompilerParams(collective_id=cid, has_side_effects=True),
    )(x)


def _back_gate_send_kernel(k_chunks, m_ref, got_ref, gate_ref, full_ref, sec, recv_s, gv, hid,
                           s_send, s_recv, c_send, c_recv, g_sem):
    n_s, n_j, n_i, _ = sec.shape
    n_c = full_ref.shape[0]
    jp = n_j // n_c
    w = n_i // k_chunks
    me_s = lax.axis_index("seq")
    me_c = lax.axis_index("chan")
    mesh_ids = pl.DeviceIdType.MESH
    barrier = pltpu.get_barrier_semaphore()
    for t in range(1, n_s):
        pl.semaphore_signal(barrier, inc=1, device_id={"seq": (me_s + t) % n_s}, device_id_type=mesh_ids)
    for t in range(1, n_c):
        pl.semaphore_signal(barrier, inc=1, device_id={"chan": (me_c + t) % n_c}, device_id_type=mesh_ids)
    pl.semaphore_wait(barrier, (n_s - 1) + (n_c - 1))

    gcopy = pltpu.make_async_copy(gate_ref, gv, g_sem)
    gcopy.start()
    def issue_seq(k):
        isl = pl.ds(k * w, w)
        m = m_ref[...]
        for i in range(k * w, (k + 1) * w):
            part = jnp.dot(m, got_ref[:, i, :], preferred_element_type=jnp.float32)
            sec[:, :, i, :] = part.astype(sec.dtype).reshape(n_s, n_j, part.shape[-1])
        row = []
        for t in range(n_s):
            if t == 0:
                c = pltpu.make_async_copy(sec.at[me_s, :, isl], recv_s.at[me_s, :, isl], s_recv.at[k, 0])
            else:
                dst = (me_s + t) % n_s
                c = pltpu.make_async_remote_copy(
                    src_ref=sec.at[dst, :, isl],
                    dst_ref=recv_s.at[me_s, :, isl],
                    send_sem=s_send.at[k, t],
                    recv_sem=s_recv.at[k, t],
                    device_id={"seq": dst},
                    device_id_type=mesh_ids,
                )
            c.start()
            row.append(c)
        return row

    seq_copies = [issue_seq(k) for k in range(min(LEAD, k_chunks))]
    gcopy.wait()
    chan_copies = []
    for k in range(k_chunks):
        isl = pl.ds(k * w, w)
        for t in range(n_s):
            if t == 0:
                seq_copies[k][t].wait()
            else:
                seq_copies[k][t].wait_recv()
        for s in range(n_s):
            prod = recv_s[s, :, isl, :].astype(jnp.float32) * gv[:, pl.ds(s * n_i + k * w, w), :].astype(jnp.float32)
            hid[:, s, isl, :] = prod.astype(hid.dtype)
        for t in range(n_c):
            dst = (me_c + t) % n_c
            src_view = hid.at[pl.ds(dst * jp, jp), :, isl, :]
            dst_view = full_ref.at[me_c, :, :, isl, :]
            if t == 0:
                c = pltpu.make_async_copy(src_view, dst_view, c_recv.at[k, 0])
            else:
                c = pltpu.make_async_remote_copy(
                    src_ref=src_view,
                    dst_ref=dst_view,
                    send_sem=c_send.at[k, t],
                    recv_sem=c_recv.at[k, t],
                    device_id={"chan": dst},
                    device_id_type=mesh_ids,
                )
            c.start()
            chan_copies.append((t, c))
        if k + LEAD < k_chunks:
            seq_copies.append(issue_seq(k + LEAD))
    for row in seq_copies:
        for c in row[1:]:
            c.wait_send()
    for t, c in chan_copies:
        if t == 0:
            c.wait()
        else:
            c.wait_send()
    for t, c in chan_copies:
        if t != 0:
            c.wait_recv()


def _back_gate_send(m2, got, gate, n_s, n_c, k_chunks, cid):
    _, n_i, cols = got.shape
    n_j = got.shape[0] // n_s
    jp = n_j // n_c
    return pl.pallas_call(
        functools.partial(_back_gate_send_kernel, k_chunks),
        out_shape=jax.ShapeDtypeStruct((n_c, jp, n_s, n_i, cols), got.dtype),
        in_specs=[pl.BlockSpec(memory_space=pltpu.VMEM)] * 2 + [pl.BlockSpec(memory_space=pl.ANY)],
        out_specs=pl.BlockSpec(memory_space=pl.ANY),
        scratch_shapes=[
            pltpu.VMEM((n_s, n_j, n_i, cols), got.dtype),
            pltpu.VMEM((n_s, n_j, n_i, cols), got.dtype),
            pltpu.VMEM((n_j, n_s * n_i, cols), got.dtype),
            pltpu.VMEM((n_j, n_s, n_i, cols), got.dtype),
            pltpu.SemaphoreType.DMA((k_chunks, n_s)),
            pltpu.SemaphoreType.DMA((k_chunks, n_s)),
            pltpu.SemaphoreType.DMA((k_chunks, n_c)),
            pltpu.SemaphoreType.DMA((k_chunks, n_c)),
            pltpu.SemaphoreType.DMA,
        ],
        compiler_params=pltpu.CompilerParams(collective_id=cid, has_side_effects=True),
    )(m2, got, gate)


def body(tokens, gate_in, mix_first, mix_second, twiddle, out_proj):
    seq_rows, chan_cols = tokens.shape
    n_seq = lax.axis_size("seq")
    n_chan = lax.axis_size("chan")
    blocks_here = seq_rows // B1
    per_dev_i = B1 // n_seq
    d_out = out_proj.shape[1]

    blocked = tokens.reshape(blocks_here, B1, chan_cols)
    mf = mix_first.reshape(n_seq, per_dev_i, B1)
    tw = twiddle.reshape(blocks_here, n_seq, per_dev_i).transpose(1, 0, 2)
    first = jnp.einsum("dik,bkc->dbic", mf, blocked, preferred_element_type=jnp.float32)
    first = (first * tw[:, :, :, None]).astype(jnp.bfloat16)
    got = _a2a(first, "seq", 0)
    got = got.reshape(n_seq * blocks_here, per_dev_i, chan_cols)
    gate = gate_in.reshape(blocks_here, B1, chan_cols)
    full = _back_gate_send(mix_second, got, gate, n_seq, n_chan, CHUNKS, 1)
    rows_per = seq_rows // n_chan
    full = full.reshape(n_chan, rows_per, chan_cols)
    wts = out_proj.reshape(n_chan, chan_cols, n_chan, d_out // n_chan)
    mixed = jnp.einsum("spc,scex->epx", full, wts, preferred_element_type=jnp.float32)
    mixed = mixed.astype(jnp.bfloat16)
    res = _a2a(mixed, "chan", 3)
    return res.reshape(seq_rows, chan_cols)


def solution(mesh):
    placed = (
        P(("batch", "seq"), "chan"),
        P(("batch", "seq"), "chan"),
        P(),
        P(),
        P("seq", None),
        P(),
    )
    return jax.shard_map(
        body, mesh=mesh, in_specs=placed, out_specs=P(("batch", "seq"), "chan"), check_vma=False
    )
```

```python
import functools

import jax
import jax.numpy as jnp
from jax import lax
from jax.sharding import PartitionSpec as P
from jax.experimental import pallas as pl
from jax.experimental.pallas import tpu as pltpu

B1 = 512
CHUNKS = 4
LEAD = 2


def _a2a_kernel(axis, n, x_ref, o_ref, send_sem, recv_sem, loc_sem):
    me = lax.axis_index(axis)
    barrier = pltpu.get_barrier_semaphore()
    for t in range(1, n):
        pl.semaphore_signal(barrier, inc=1, device_id={axis: (me + t) % n},
                            device_id_type=pl.DeviceIdType.MESH)
    pl.semaphore_wait(barrier, n - 1)
    local = pltpu.make_async_copy(x_ref.at[me], o_ref.at[me], loc_sem)
    local.start()
    copies = []
    for t in range(1, n):
        dst = (me + t) % n
        c = pltpu.make_async_remote_copy(
            src_ref=x_ref.at[dst],
            dst_ref=o_ref.at[me],
            send_sem=send_sem.at[t],
            recv_sem=recv_sem.at[t],
            device_id={axis: dst},
            device_id_type=pl.DeviceIdType.MESH,
        )
        c.start()
        copies.append(c)
    local.wait()
    for c in copies:
        c.wait_send()
    for c in copies:
        c.wait_recv()


def _a2a(x, axis, cid):
    n = x.shape[0]
    return pl.pallas_call(
        functools.partial(_a2a_kernel, axis, n),
        out_shape=jax.ShapeDtypeStruct(x.shape, x.dtype),
        in_specs=[pl.BlockSpec(memory_space=pl.ANY)],
        out_specs=pl.BlockSpec(memory_space=pl.ANY),
        scratch_shapes=[
            pltpu.SemaphoreType.DMA((n,)),
            pltpu.SemaphoreType.DMA((n,)),
            pltpu.SemaphoreType.DMA,
        ],
        compiler_params=pltpu.CompilerParams(collective_id=cid, has_side_effects=True),
    )(x)


def _back_gate_send_kernel(k_chunks, m_ref, got_ref, gate_ref, full_ref, sec, recv_s, gv, hid,
                           s_send, s_recv, c_send, c_recv, g_sem):
    n_s, n_j, n_i, _ = sec.shape
    n_c = full_ref.shape[0]
    jp = n_j // n_c
    w = n_i // k_chunks
    me_s = lax.axis_index("seq")
    me_c = lax.axis_index("chan")
    mesh_ids = pl.DeviceIdType.MESH
    barrier = pltpu.get_barrier_semaphore()
    for t in range(1, n_s):
        pl.semaphore_signal(barrier, inc=1, device_id={"seq": (me_s + t) % n_s}, device_id_type=mesh_ids)
    for t in range(1, n_c):
        pl.semaphore_signal(barrier, inc=1, device_id={"chan": (me_c + t) % n_c}, device_id_type=mesh_ids)
    pl.semaphore_wait(barrier, (n_s - 1) + (n_c - 1))

    gcopy = pltpu.make_async_copy(gate_ref, gv, g_sem)
    gcopy.start()
    def issue_seq(k):
        isl = pl.ds(k * w, w)
        m = m_ref[...]
        for i in range(k * w, (k + 1) * w):
            part = jnp.dot(m, got_ref[:, i, :], preferred_element_type=jnp.float32)
            sec[:, :, i, :] = part.astype(sec.dtype).reshape(n_s, n_j, part.shape[-1])
        row = []
        for t in range(n_s):
            if t == 0:
                c = pltpu.make_async_copy(sec.at[me_s, :, isl], recv_s.at[me_s, :, isl], s_recv.at[k, 0])
            else:
                dst = (me_s + t) % n_s
                c = pltpu.make_async_remote_copy(
                    src_ref=sec.at[dst, :, isl],
                    dst_ref=recv_s.at[me_s, :, isl],
                    send_sem=s_send.at[k, t],
                    recv_sem=s_recv.at[k, t],
                    device_id={"seq": dst},
                    device_id_type=mesh_ids,
                )
            c.start()
            row.append(c)
        return row

    seq_copies = [issue_seq(k) for k in range(min(LEAD, k_chunks))]
    gcopy.wait()
    chan_copies = []
    for k in range(k_chunks):
        isl = pl.ds(k * w, w)
        for t in range(n_s):
            if t == 0:
                seq_copies[k][t].wait()
            else:
                seq_copies[k][t].wait_recv()
        for s in range(n_s):
            prod = recv_s[s, :, isl, :].astype(jnp.float32) * gv[:, pl.ds(s * n_i + k * w, w), :].astype(jnp.float32)
            hid[:, s, isl, :] = prod.astype(hid.dtype)
        for t in range(n_c):
            dst = (me_c + t) % n_c
            src_view = hid.at[pl.ds(dst * jp, jp), :, isl, :]
            dst_view = full_ref.at[me_c, :, :, isl, :]
            if t == 0:
                c = pltpu.make_async_copy(src_view, dst_view, c_recv.at[k, 0])
            else:
                c = pltpu.make_async_remote_copy(
                    src_ref=src_view,
                    dst_ref=dst_view,
                    send_sem=c_send.at[k, t],
                    recv_sem=c_recv.at[k, t],
                    device_id={"chan": dst},
                    device_id_type=mesh_ids,
                )
            c.start()
            chan_copies.append((t, c))
        if k + LEAD < k_chunks:
            seq_copies.append(issue_seq(k + LEAD))
    for row in seq_copies:
        for c in row[1:]:
            c.wait_send()
    for t, c in chan_copies:
        if t == 0:
            c.wait()
        else:
            c.wait_send()
    for t, c in chan_copies:
        if t != 0:
            c.wait_recv()


def _back_gate_send(m2, got, gate, n_s, n_c, k_chunks, cid):
    _, n_i, cols = got.shape
    n_j = got.shape[0] // n_s
    jp = n_j // n_c
    return pl.pallas_call(
        functools.partial(_back_gate_send_kernel, k_chunks),
        out_shape=jax.ShapeDtypeStruct((n_c, jp, n_s, n_i, cols), got.dtype),
        in_specs=[pl.BlockSpec(memory_space=pltpu.VMEM)] * 2 + [pl.BlockSpec(memory_space=pl.ANY)],
        out_specs=pl.BlockSpec(memory_space=pl.ANY),
        scratch_shapes=[
            pltpu.VMEM((n_s, n_j, n_i, cols), got.dtype),
            pltpu.VMEM((n_s, n_j, n_i, cols), got.dtype),
            pltpu.VMEM((n_j, n_s * n_i, cols), got.dtype),
            pltpu.VMEM((n_j, n_s, n_i, cols), got.dtype),
            pltpu.SemaphoreType.DMA((k_chunks, n_s)),
            pltpu.SemaphoreType.DMA((k_chunks, n_s)),
            pltpu.SemaphoreType.DMA((k_chunks, n_c)),
            pltpu.SemaphoreType.DMA((k_chunks, n_c)),
            pltpu.SemaphoreType.DMA,
        ],
        compiler_params=pltpu.CompilerParams(collective_id=cid, has_side_effects=True),
    )(m2, got, gate)


def _first_send_kernel(mf_ref, tok_ref, tw_ref, got_ref, stage, send_sem, recv_sem):
    n, n_b, n_i, cols = stage.shape
    me = lax.axis_index("seq")
    mesh_ids = pl.DeviceIdType.MESH
    barrier = pltpu.get_barrier_semaphore()
    for t in range(1, n):
        pl.semaphore_signal(barrier, inc=1, device_id={"seq": (me + t) % n}, device_id_type=mesh_ids)
    pl.semaphore_wait(barrier, n - 1)
    copies = []
    for t in list(range(1, n)) + [0]:
        dst = (me + t) % n
        rows = pl.ds(pl.multiple_of(dst * n_i, n_i), n_i)
        m = mf_ref[rows, :]
        for b in range(n_b):
            part = jnp.dot(m, tok_ref[b], preferred_element_type=jnp.float32)
            stage[t, b] = (part * tw_ref[rows, pl.ds(b, 1)]).astype(stage.dtype)
        if t == 0:
            c = pltpu.make_async_copy(stage.at[t], got_ref.at[me], recv_sem.at[0])
        else:
            c = pltpu.make_async_remote_copy(
                src_ref=stage.at[t],
                dst_ref=got_ref.at[me],
                send_sem=send_sem.at[t],
                recv_sem=recv_sem.at[t],
                device_id={"seq": dst},
                device_id_type=mesh_ids,
            )
        c.start()
        copies.append((t, c))
    for t, c in copies:
        if t == 0:
            c.wait()
        else:
            c.wait_send()
    for t, c in copies:
        if t != 0:
            c.wait_recv()


def _first_send(mix_first, blocked, tw_t, n, cid):
    n_b, _, cols = blocked.shape
    n_i = mix_first.shape[0] // n
    return pl.pallas_call(
        _first_send_kernel,
        out_shape=jax.ShapeDtypeStruct((n, n_b, n_i, cols), blocked.dtype),
        in_specs=[pl.BlockSpec(memory_space=pltpu.VMEM)] * 3,
        out_specs=pl.BlockSpec(memory_space=pl.ANY),
        scratch_shapes=[
            pltpu.VMEM((n, n_b, n_i, cols), blocked.dtype),
            pltpu.SemaphoreType.DMA((n,)),
            pltpu.SemaphoreType.DMA((n,)),
        ],
        compiler_params=pltpu.CompilerParams(collective_id=cid, has_side_effects=True),
    )(mix_first, blocked, tw_t)


def _project_kernel(full_ref, w_ref, o_ref):
    n_c, _, cols = full_ref.shape
    acc = jnp.zeros(o_ref.shape[1:], jnp.float32)
    for s in range(n_c):
        acc += jnp.dot(full_ref[s], w_ref[pl.ds(s * cols, cols), :], preferred_element_type=jnp.float32)
    o_ref[0] = acc.astype(o_ref.dtype)


def _project(full, w):
    n_c, rows, cols = full.shape
    return pl.pallas_call(
        _project_kernel,
        out_shape=jax.ShapeDtypeStruct((w.shape[1] // cols, rows, cols), full.dtype),
        grid=(w.shape[1] // cols,),
        in_specs=[
            pl.BlockSpec((n_c, rows, cols), lambda e: (0, 0, 0)),
            pl.BlockSpec((w.shape[0], cols), lambda e: (0, e)),
        ],
        out_specs=pl.BlockSpec((1, rows, cols), lambda e: (e, 0, 0)),
    )(full, w)


def body(tokens, gate_in, mix_first, mix_second, twiddle, out_proj):
    seq_rows, chan_cols = tokens.shape
    n_seq = lax.axis_size("seq")
    n_chan = lax.axis_size("chan")
    blocks_here = seq_rows // B1
    per_dev_i = B1 // n_seq
    d_out = out_proj.shape[1]

    blocked = tokens.reshape(blocks_here, B1, chan_cols)
    got = _first_send(mix_first, blocked, twiddle.T, n_seq, 0)
    got = got.reshape(n_seq * blocks_here, per_dev_i, chan_cols)
    gate = gate_in.reshape(blocks_here, B1, chan_cols)
    full = _back_gate_send(mix_second, got, gate, n_seq, n_chan, CHUNKS, 1)
    rows_per = seq_rows // n_chan
    full = full.reshape(n_chan, rows_per, chan_cols)
    mixed = _project(full, out_proj)
    res = _a2a(mixed, "chan", 3)
    return res.reshape(seq_rows, chan_cols)


def solution(mesh):
    placed = (
        P(("batch", "seq"), "chan"),
        P(("batch", "seq"), "chan"),
        P(),
        P(),
        P("seq", None),
        P(),
    )
    return jax.shard_map(
        body, mesh=mesh, in_specs=placed, out_specs=P(("batch", "seq"), "chan"), check_vma=False
    )
```

```python
import functools

import jax
import jax.numpy as jnp
from jax import lax
from jax.sharding import PartitionSpec as P
from jax.experimental import pallas as pl
from jax.experimental.pallas import tpu as pltpu

B1 = 512
CHUNKS = 4
LEAD = 2


def _a2a_kernel(axis, n, x_ref, o_ref, send_sem, recv_sem, loc_sem):
    me = lax.axis_index(axis)
    barrier = pltpu.get_barrier_semaphore()
    for t in range(1, n):
        pl.semaphore_signal(barrier, inc=1, device_id={axis: (me + t) % n},
                            device_id_type=pl.DeviceIdType.MESH)
    pl.semaphore_wait(barrier, n - 1)
    local = pltpu.make_async_copy(x_ref.at[me], o_ref.at[me], loc_sem)
    local.start()
    copies = []
    for t in range(1, n):
        dst = (me + t) % n
        c = pltpu.make_async_remote_copy(
            src_ref=x_ref.at[dst],
            dst_ref=o_ref.at[me],
            send_sem=send_sem.at[t],
            recv_sem=recv_sem.at[t],
            device_id={axis: dst},
            device_id_type=pl.DeviceIdType.MESH,
        )
        c.start()
        copies.append(c)
    local.wait()
    for c in copies:
        c.wait_send()
    for c in copies:
        c.wait_recv()


def _a2a(x, axis, cid):
    n = x.shape[0]
    return pl.pallas_call(
        functools.partial(_a2a_kernel, axis, n),
        out_shape=jax.ShapeDtypeStruct(x.shape, x.dtype),
        in_specs=[pl.BlockSpec(memory_space=pl.ANY)],
        out_specs=pl.BlockSpec(memory_space=pl.ANY),
        scratch_shapes=[
            pltpu.SemaphoreType.DMA((n,)),
            pltpu.SemaphoreType.DMA((n,)),
            pltpu.SemaphoreType.DMA,
        ],
        compiler_params=pltpu.CompilerParams(collective_id=cid, has_side_effects=True),
    )(x)


def _back_gate_send_kernel(k_chunks, m_ref, got_ref, gate_ref, full_ref, sec, recv_s, gv, hid,
                           s_send, s_recv, c_send, c_recv, g_sem):
    n_s, n_j, n_i, _ = sec.shape
    n_c = full_ref.shape[0]
    jp = n_j // n_c
    w = n_i // k_chunks
    me_s = lax.axis_index("seq")
    me_c = lax.axis_index("chan")
    mesh_ids = pl.DeviceIdType.MESH
    barrier = pltpu.get_barrier_semaphore()
    for t in range(1, n_s):
        pl.semaphore_signal(barrier, inc=1, device_id={"seq": (me_s + t) % n_s}, device_id_type=mesh_ids)
    for t in range(1, n_c):
        pl.semaphore_signal(barrier, inc=1, device_id={"chan": (me_c + t) % n_c}, device_id_type=mesh_ids)
    pl.semaphore_wait(barrier, (n_s - 1) + (n_c - 1))

    gcopy = pltpu.make_async_copy(gate_ref, gv, g_sem)
    gcopy.start()
    def issue_seq(k):
        isl = pl.ds(k * w, w)
        m = m_ref[...]
        for i in range(k * w, (k + 1) * w):
            part = jnp.dot(m, got_ref[:, i, :], preferred_element_type=jnp.float32)
            sec[:, :, i, :] = part.astype(sec.dtype).reshape(n_s, n_j, part.shape[-1])
        row = []
        for t in range(n_s):
            if t == 0:
                c = pltpu.make_async_copy(sec.at[me_s, :, isl], recv_s.at[me_s, :, isl], s_recv.at[k, 0])
            else:
                dst = (me_s + t) % n_s
                c = pltpu.make_async_remote_copy(
                    src_ref=sec.at[dst, :, isl],
                    dst_ref=recv_s.at[me_s, :, isl],
                    send_sem=s_send.at[k, t],
                    recv_sem=s_recv.at[k, t],
                    device_id={"seq": dst},
                    device_id_type=mesh_ids,
                )
            c.start()
            row.append(c)
        return row

    seq_copies = [issue_seq(k) for k in range(min(LEAD, k_chunks))]
    gcopy.wait()
    chan_copies = []
    for k in range(k_chunks):
        isl = pl.ds(k * w, w)
        for t in range(n_s):
            if t == 0:
                seq_copies[k][t].wait()
            else:
                seq_copies[k][t].wait_recv()
        for s in range(n_s):
            prod = recv_s[s, :, isl, :].astype(jnp.float32) * gv[:, pl.ds(s * n_i + k * w, w), :].astype(jnp.float32)
            hid[:, s, isl, :] = prod.astype(hid.dtype)
        for t in range(n_c):
            dst = (me_c + t) % n_c
            src_view = hid.at[pl.ds(dst * jp, jp), :, isl, :]
            dst_view = full_ref.at[me_c, :, :, isl, :]
            if t == 0:
                c = pltpu.make_async_copy(src_view, dst_view, c_recv.at[k, 0])
            else:
                c = pltpu.make_async_remote_copy(
                    src_ref=src_view,
                    dst_ref=dst_view,
                    send_sem=c_send.at[k, t],
                    recv_sem=c_recv.at[k, t],
                    device_id={"chan": dst},
                    device_id_type=mesh_ids,
                )
            c.start()
            chan_copies.append((t, c))
        if k + LEAD < k_chunks:
            seq_copies.append(issue_seq(k + LEAD))
    for row in seq_copies:
        for c in row[1:]:
            c.wait_send()
    for t, c in chan_copies:
        if t == 0:
            c.wait()
        else:
            c.wait_send()
    for t, c in chan_copies:
        if t != 0:
            c.wait_recv()


def _back_gate_send(m2, got, gate, n_s, n_c, k_chunks, cid):
    _, n_i, cols = got.shape
    n_j = got.shape[0] // n_s
    jp = n_j // n_c
    return pl.pallas_call(
        functools.partial(_back_gate_send_kernel, k_chunks),
        out_shape=jax.ShapeDtypeStruct((n_c, jp, n_s, n_i, cols), got.dtype),
        in_specs=[pl.BlockSpec(memory_space=pltpu.VMEM)] * 2 + [pl.BlockSpec(memory_space=pl.ANY)],
        out_specs=pl.BlockSpec(memory_space=pl.ANY),
        scratch_shapes=[
            pltpu.VMEM((n_s, n_j, n_i, cols), got.dtype),
            pltpu.VMEM((n_s, n_j, n_i, cols), got.dtype),
            pltpu.VMEM((n_j, n_s * n_i, cols), got.dtype),
            pltpu.VMEM((n_j, n_s, n_i, cols), got.dtype),
            pltpu.SemaphoreType.DMA((k_chunks, n_s)),
            pltpu.SemaphoreType.DMA((k_chunks, n_s)),
            pltpu.SemaphoreType.DMA((k_chunks, n_c)),
            pltpu.SemaphoreType.DMA((k_chunks, n_c)),
            pltpu.SemaphoreType.DMA,
        ],
        compiler_params=pltpu.CompilerParams(collective_id=cid, has_side_effects=True),
    )(m2, got, gate)


def _first_send_kernel(mf_ref, tok_ref, tw_ref, got_ref, stage, send_sem, recv_sem):
    n, n_b, n_i, cols = stage.shape
    me = lax.axis_index("seq")
    mesh_ids = pl.DeviceIdType.MESH
    barrier = pltpu.get_barrier_semaphore()
    for t in range(1, n):
        pl.semaphore_signal(barrier, inc=1, device_id={"seq": (me + t) % n}, device_id_type=mesh_ids)
    pl.semaphore_wait(barrier, n - 1)
    copies = []
    for t in list(range(1, n)) + [0]:
        dst = (me + t) % n
        rows = pl.ds(pl.multiple_of(dst * n_i, n_i), n_i)
        m = mf_ref[rows, :]
        for b in range(n_b):
            part = jnp.dot(m, tok_ref[b], preferred_element_type=jnp.float32)
            stage[t, b] = (part * tw_ref[rows, pl.ds(b, 1)]).astype(stage.dtype)
        if t == 0:
            c = pltpu.make_async_copy(stage.at[t], got_ref.at[me], recv_sem.at[0])
        else:
            c = pltpu.make_async_remote_copy(
                src_ref=stage.at[t],
                dst_ref=got_ref.at[me],
                send_sem=send_sem.at[t],
                recv_sem=recv_sem.at[t],
                device_id={"seq": dst},
                device_id_type=mesh_ids,
            )
        c.start()
        copies.append((t, c))
    for t, c in copies:
        if t == 0:
            c.wait()
        else:
            c.wait_send()
    for t, c in copies:
        if t != 0:
            c.wait_recv()


def _first_send(mix_first, blocked, tw_t, n, cid):
    n_b, _, cols = blocked.shape
    n_i = mix_first.shape[0] // n
    return pl.pallas_call(
        _first_send_kernel,
        out_shape=jax.ShapeDtypeStruct((n, n_b, n_i, cols), blocked.dtype),
        in_specs=[pl.BlockSpec(memory_space=pltpu.VMEM)] * 3,
        out_specs=pl.BlockSpec(memory_space=pl.ANY),
        scratch_shapes=[
            pltpu.VMEM((n, n_b, n_i, cols), blocked.dtype),
            pltpu.SemaphoreType.DMA((n,)),
            pltpu.SemaphoreType.DMA((n,)),
        ],
        compiler_params=pltpu.CompilerParams(collective_id=cid, has_side_effects=True),
    )(mix_first, blocked, tw_t)


def body(tokens, gate_in, mix_first, mix_second, twiddle, out_proj):
    seq_rows, chan_cols = tokens.shape
    n_seq = lax.axis_size("seq")
    n_chan = lax.axis_size("chan")
    blocks_here = seq_rows // B1
    per_dev_i = B1 // n_seq
    d_out = out_proj.shape[1]

    blocked = tokens.reshape(blocks_here, B1, chan_cols)
    got = _first_send(mix_first, blocked, twiddle.T, n_seq, 0)
    got = got.reshape(n_seq * blocks_here, per_dev_i, chan_cols)
    gate = gate_in.reshape(blocks_here, B1, chan_cols)
    full = _back_gate_send(mix_second, got, gate, n_seq, n_chan, CHUNKS, 1)
    rows_per = seq_rows // n_chan
    full = full.reshape(n_chan, rows_per, chan_cols)
    wts = out_proj.reshape(n_chan, chan_cols, n_chan, d_out // n_chan)
    mixed = jnp.einsum("spc,scex->epx", full, wts, preferred_element_type=jnp.float32)
    mixed = mixed.astype(jnp.bfloat16)
    res = _a2a(mixed, "chan", 3)
    return res.reshape(seq_rows, chan_cols)


def solution(mesh):
    placed = (
        P(("batch", "seq"), "chan"),
        P(("batch", "seq"), "chan"),
        P(),
        P(),
        P("seq", None),
        P(),
    )
    return jax.shard_map(
        body, mesh=mesh, in_specs=placed, out_specs=P(("batch", "seq"), "chan"), check_vma=False
    )
```

```python
import functools

import jax
import jax.numpy as jnp
from jax import lax
from jax.sharding import PartitionSpec as P
from jax.experimental import pallas as pl
from jax.experimental.pallas import tpu as pltpu

B1 = 512
CHUNKS = 4
LEAD = 2


def _a2a_kernel(axis, n, x_ref, o_ref, send_sem, recv_sem, loc_sem):
    me = lax.axis_index(axis)
    barrier = pltpu.get_barrier_semaphore()
    for t in range(1, n):
        pl.semaphore_signal(barrier, inc=1, device_id={axis: (me + t) % n},
                            device_id_type=pl.DeviceIdType.MESH)
    pl.semaphore_wait(barrier, n - 1)
    local = pltpu.make_async_copy(x_ref.at[me], o_ref.at[me], loc_sem)
    local.start()
    copies = []
    for t in range(1, n):
        dst = (me + t) % n
        c = pltpu.make_async_remote_copy(
            src_ref=x_ref.at[dst],
            dst_ref=o_ref.at[me],
            send_sem=send_sem.at[t],
            recv_sem=recv_sem.at[t],
            device_id={axis: dst},
            device_id_type=pl.DeviceIdType.MESH,
        )
        c.start()
        copies.append(c)
    local.wait()
    for c in copies:
        c.wait_send()
    for c in copies:
        c.wait_recv()


def _a2a(x, axis, cid):
    n = x.shape[0]
    return pl.pallas_call(
        functools.partial(_a2a_kernel, axis, n),
        out_shape=jax.ShapeDtypeStruct(x.shape, x.dtype),
        in_specs=[pl.BlockSpec(memory_space=pl.ANY)],
        out_specs=pl.BlockSpec(memory_space=pl.ANY),
        scratch_shapes=[
            pltpu.SemaphoreType.DMA((n,)),
            pltpu.SemaphoreType.DMA((n,)),
            pltpu.SemaphoreType.DMA,
        ],
        compiler_params=pltpu.CompilerParams(collective_id=cid, has_side_effects=True),
    )(x)


def _layer_tail_kernel(k_chunks, m_ref, got_ref, w_ref, gate_ref, res_ref, sec, recv_s, gv, hid,
                       fullv, stage, s_send, s_recv, c_send, c_recv, o_send, o_recv, g_sem):
    n_s, n_j, n_i, cols = sec.shape
    n_c = fullv.shape[0]
    jp = n_j // n_c
    w = n_i // k_chunks
    rows = jp * n_s * w
    me_s = lax.axis_index("seq")
    me_c = lax.axis_index("chan")
    mesh_ids = pl.DeviceIdType.MESH
    barrier = pltpu.get_barrier_semaphore()
    for t in range(1, n_s):
        pl.semaphore_signal(barrier, inc=1, device_id={"seq": (me_s + t) % n_s}, device_id_type=mesh_ids)
    for t in range(1, n_c):
        pl.semaphore_signal(barrier, inc=1, device_id={"chan": (me_c + t) % n_c}, device_id_type=mesh_ids)
    pl.semaphore_wait(barrier, (n_s - 1) + (n_c - 1))

    gcopy = pltpu.make_async_copy(gate_ref, gv, g_sem)
    gcopy.start()

    def exchange(src_view, dst_view, t, dst, axis, send_sem, recv_sem):
        if t == 0:
            c = pltpu.make_async_copy(src_view, dst_view, recv_sem)
        else:
            c = pltpu.make_async_remote_copy(
                src_ref=src_view,
                dst_ref=dst_view,
                send_sem=send_sem,
                recv_sem=recv_sem,
                device_id={axis: dst},
                device_id_type=mesh_ids,
            )
        c.start()
        return c

    def issue_seq(k):
        isl = pl.ds(k * w, w)
        m = m_ref[...]
        for i in range(k * w, (k + 1) * w):
            part = jnp.dot(m, got_ref[:, i, :], preferred_element_type=jnp.float32)
            sec[:, :, i, :] = part.astype(sec.dtype).reshape(n_s, n_j, cols)
        row = []
        for t in range(n_s):
            dst = (me_s + t) % n_s
            row.append(exchange(sec.at[dst, :, isl], recv_s.at[me_s, :, isl], t, dst, "seq",
                                s_send.at[k, t], s_recv.at[k, t]))
        return row

    def project(k):
        isl = pl.ds(k * w, w)
        for t, c in enumerate(chan_copies[k]):
            if t == 0:
                c.wait()
            else:
                c.wait_recv()
        acc = jnp.zeros((rows, w_ref.shape[1]), jnp.float32)
        for s in range(n_c):
            x = fullv[s, :, :, isl, :].reshape(rows, cols)
            acc += jnp.dot(x, w_ref[pl.ds(s * cols, cols), :], preferred_element_type=jnp.float32)
        stage[k] = acc.astype(stage.dtype).reshape(jp, n_s, w, w_ref.shape[1])
        row = []
        for t in list(range(1, n_c)) + [0]:
            dst = (me_c + t) % n_c
            src_view = stage.at[k, :, :, :, pl.ds(pl.multiple_of(dst * cols, cols), cols)]
            row.append((t, exchange(src_view, res_ref.at[me_c, :, :, isl, :], t, dst, "chan",
                                    o_send.at[k, t], o_recv.at[k, t])))
        out_copies.append(row)

    seq_copies = [issue_seq(k) for k in range(min(LEAD, k_chunks))]
    gcopy.wait()
    chan_copies = []
    out_copies = []
    for k in range(k_chunks):
        isl = pl.ds(k * w, w)
        for t in range(n_s):
            if t == 0:
                seq_copies[k][t].wait()
            else:
                seq_copies[k][t].wait_recv()
        for s in range(n_s):
            prod = recv_s[s, :, isl, :].astype(jnp.float32) * gv[:, pl.ds(s * n_i + k * w, w), :].astype(jnp.float32)
            hid[:, s, isl, :] = prod.astype(hid.dtype)
        row = []
        for t in range(n_c):
            dst = (me_c + t) % n_c
            row.append(exchange(hid.at[pl.ds(dst * jp, jp), :, isl, :], fullv.at[me_c, :, :, isl, :],
                                t, dst, "chan", c_send.at[k, t], c_recv.at[k, t]))
        chan_copies.append(row)
        if k + LEAD < k_chunks:
            seq_copies.append(issue_seq(k + LEAD))
        if k >= 1:
            project(k - 1)
    project(k_chunks - 1)
    for row in seq_copies:
        for c in row[1:]:
            c.wait_send()
    for row in chan_copies:
        for c in row[1:]:
            c.wait_send()
    for row in out_copies:
        for t, c in row:
            if t == 0:
                c.wait()
            else:
                c.wait_send()
    for row in out_copies:
        for t, c in row:
            if t != 0:
                c.wait_recv()


def _layer_tail(m2, got, w, gate, n_s, n_c, k_chunks, cid):
    _, n_i, cols = got.shape
    n_j = got.shape[0] // n_s
    jp = n_j // n_c
    dt = got.dtype
    return pl.pallas_call(
        functools.partial(_layer_tail_kernel, k_chunks),
        out_shape=jax.ShapeDtypeStruct((n_c, jp, n_s, n_i, cols), dt),
        in_specs=[pl.BlockSpec(memory_space=pltpu.VMEM)] * 3 + [pl.BlockSpec(memory_space=pl.ANY)],
        out_specs=pl.BlockSpec(memory_space=pl.ANY),
        scratch_shapes=[
            pltpu.VMEM((n_s, n_j, n_i, cols), dt),
            pltpu.VMEM((n_s, n_j, n_i, cols), dt),
            pltpu.VMEM((n_j, n_s * n_i, cols), dt),
            pltpu.VMEM((n_j, n_s, n_i, cols), dt),
            pltpu.VMEM((n_c, jp, n_s, n_i, cols), dt),
            pltpu.VMEM((k_chunks, jp, n_s, n_i // k_chunks, w.shape[1]), dt),
            pltpu.SemaphoreType.DMA((k_chunks, n_s)),
            pltpu.SemaphoreType.DMA((k_chunks, n_s)),
            pltpu.SemaphoreType.DMA((k_chunks, n_c)),
            pltpu.SemaphoreType.DMA((k_chunks, n_c)),
            pltpu.SemaphoreType.DMA((k_chunks, n_c)),
            pltpu.SemaphoreType.DMA((k_chunks, n_c)),
            pltpu.SemaphoreType.DMA,
        ],
        compiler_params=pltpu.CompilerParams(collective_id=cid, has_side_effects=True),
    )(m2, got, w, gate)


def body(tokens, gate_in, mix_first, mix_second, twiddle, out_proj):
    seq_rows, chan_cols = tokens.shape
    n_seq = lax.axis_size("seq")
    n_chan = lax.axis_size("chan")
    blocks_here = seq_rows // B1
    per_dev_i = B1 // n_seq
    d_out = out_proj.shape[1]

    blocked = tokens.reshape(blocks_here, B1, chan_cols)
    mf = mix_first.reshape(n_seq, per_dev_i, B1)
    tw = twiddle.reshape(blocks_here, n_seq, per_dev_i).transpose(1, 0, 2)
    first = jnp.einsum("dik,bkc->dbic", mf, blocked, preferred_element_type=jnp.float32)
    first = (first * tw[:, :, :, None]).astype(jnp.bfloat16)
    got = _a2a(first, "seq", 0)
    got = got.reshape(n_seq * blocks_here, per_dev_i, chan_cols)
    gate = gate_in.reshape(blocks_here, B1, chan_cols)
    res = _layer_tail(mix_second, got, out_proj, gate, n_seq, n_chan, CHUNKS, 1)
    return res.reshape(seq_rows, chan_cols)


def solution(mesh):
    placed = (
        P(("batch", "seq"), "chan"),
        P(("batch", "seq"), "chan"),
        P(),
        P(),
        P("seq", None),
        P(),
    )
    return jax.shard_map(
        body, mesh=mesh, in_specs=placed, out_specs=P(("batch", "seq"), "chan"), check_vma=False
    )
```

```python
import functools

import jax
import jax.numpy as jnp
from jax import lax
from jax.sharding import PartitionSpec as P
from jax.experimental import pallas as pl
from jax.experimental.pallas import tpu as pltpu

B1 = 512
CHUNKS = 8
LEAD = 2


def _a2a_kernel(axis, n, x_ref, o_ref, send_sem, recv_sem, loc_sem):
    me = lax.axis_index(axis)
    barrier = pltpu.get_barrier_semaphore()
    for t in range(1, n):
        pl.semaphore_signal(barrier, inc=1, device_id={axis: (me + t) % n},
                            device_id_type=pl.DeviceIdType.MESH)
    pl.semaphore_wait(barrier, n - 1)
    local = pltpu.make_async_copy(x_ref.at[me], o_ref.at[me], loc_sem)
    local.start()
    copies = []
    for t in range(1, n):
        dst = (me + t) % n
        c = pltpu.make_async_remote_copy(
            src_ref=x_ref.at[dst],
            dst_ref=o_ref.at[me],
            send_sem=send_sem.at[t],
            recv_sem=recv_sem.at[t],
            device_id={axis: dst},
            device_id_type=pl.DeviceIdType.MESH,
        )
        c.start()
        copies.append(c)
    local.wait()
    for c in copies:
        c.wait_send()
    for c in copies:
        c.wait_recv()


def _a2a(x, axis, cid):
    n = x.shape[0]
    return pl.pallas_call(
        functools.partial(_a2a_kernel, axis, n),
        out_shape=jax.ShapeDtypeStruct(x.shape, x.dtype),
        in_specs=[pl.BlockSpec(memory_space=pl.ANY)],
        out_specs=pl.BlockSpec(memory_space=pl.ANY),
        scratch_shapes=[
            pltpu.SemaphoreType.DMA((n,)),
            pltpu.SemaphoreType.DMA((n,)),
            pltpu.SemaphoreType.DMA,
        ],
        compiler_params=pltpu.CompilerParams(collective_id=cid, has_side_effects=True),
    )(x)


def _back_gate_send_kernel(k_chunks, m_ref, got_ref, gate_ref, full_ref, sec, recv_s, gv, hid,
                           s_send, s_recv, c_send, c_recv, g_sem):
    n_s, n_j, n_i, _ = sec.shape
    n_c = full_ref.shape[0]
    jp = n_j // n_c
    w = n_i // k_chunks
    me_s = lax.axis_index("seq")
    me_c = lax.axis_index("chan")
    mesh_ids = pl.DeviceIdType.MESH
    barrier = pltpu.get_barrier_semaphore()
    for t in range(1, n_s):
        pl.semaphore_signal(barrier, inc=1, device_id={"seq": (me_s + t) % n_s}, device_id_type=mesh_ids)
    for t in range(1, n_c):
        pl.semaphore_signal(barrier, inc=1, device_id={"chan": (me_c + t) % n_c}, device_id_type=mesh_ids)
    pl.semaphore_wait(barrier, (n_s - 1) + (n_c - 1))

    gcopy = pltpu.make_async_copy(gate_ref, gv, g_sem)
    gcopy.start()
    def issue_seq(k):
        isl = pl.ds(k * w, w)
        m = m_ref[...]
        for i in range(k * w, (k + 1) * w):
            part = jnp.dot(m, got_ref[:, i, :], preferred_element_type=jnp.float32)
            sec[:, :, i, :] = part.astype(sec.dtype).reshape(n_s, n_j, part.shape[-1])
        row = []
        for t in range(n_s):
            if t == 0:
                c = pltpu.make_async_copy(sec.at[me_s, :, isl], recv_s.at[me_s, :, isl], s_recv.at[k, 0])
            else:
                dst = (me_s + t) % n_s
                c = pltpu.make_async_remote_copy(
                    src_ref=sec.at[dst, :, isl],
                    dst_ref=recv_s.at[me_s, :, isl],
                    send_sem=s_send.at[k, t],
                    recv_sem=s_recv.at[k, t],
                    device_id={"seq": dst},
                    device_id_type=mesh_ids,
                )
            c.start()
            row.append(c)
        return row

    seq_copies = [issue_seq(k) for k in range(min(LEAD, k_chunks))]
    gcopy.wait()
    chan_copies = []
    for k in range(k_chunks):
        isl = pl.ds(k * w, w)
        for t in range(n_s):
            if t == 0:
                seq_copies[k][t].wait()
            else:
                seq_copies[k][t].wait_recv()
        for s in range(n_s):
            prod = recv_s[s, :, isl, :].astype(jnp.float32) * gv[:, pl.ds(s * n_i + k * w, w), :].astype(jnp.float32)
            hid[:, s, isl, :] = prod.astype(hid.dtype)
        for t in range(n_c):
            dst = (me_c + t) % n_c
            src_view = hid.at[pl.ds(dst * jp, jp), :, isl, :]
            dst_view = full_ref.at[me_c, :, :, isl, :]
            if t == 0:
                c = pltpu.make_async_copy(src_view, dst_view, c_recv.at[k, 0])
            else:
                c = pltpu.make_async_remote_copy(
                    src_ref=src_view,
                    dst_ref=dst_view,
                    send_sem=c_send.at[k, t],
                    recv_sem=c_recv.at[k, t],
                    device_id={"chan": dst},
                    device_id_type=mesh_ids,
                )
            c.start()
            chan_copies.append((t, c))
        if k + LEAD < k_chunks:
            seq_copies.append(issue_seq(k + LEAD))
    for row in seq_copies:
        for c in row[1:]:
            c.wait_send()
    for t, c in chan_copies:
        if t == 0:
            c.wait()
        else:
            c.wait_send()
    for t, c in chan_copies:
        if t != 0:
            c.wait_recv()


def _back_gate_send(m2, got, gate, n_s, n_c, k_chunks, cid):
    _, n_i, cols = got.shape
    n_j = got.shape[0] // n_s
    jp = n_j // n_c
    return pl.pallas_call(
        functools.partial(_back_gate_send_kernel, k_chunks),
        out_shape=jax.ShapeDtypeStruct((n_c, jp, n_s, n_i, cols), got.dtype),
        in_specs=[pl.BlockSpec(memory_space=pltpu.VMEM)] * 2 + [pl.BlockSpec(memory_space=pl.ANY)],
        out_specs=pl.BlockSpec(memory_space=pl.ANY),
        scratch_shapes=[
            pltpu.VMEM((n_s, n_j, n_i, cols), got.dtype),
            pltpu.VMEM((n_s, n_j, n_i, cols), got.dtype),
            pltpu.VMEM((n_j, n_s * n_i, cols), got.dtype),
            pltpu.VMEM((n_j, n_s, n_i, cols), got.dtype),
            pltpu.SemaphoreType.DMA((k_chunks, n_s)),
            pltpu.SemaphoreType.DMA((k_chunks, n_s)),
            pltpu.SemaphoreType.DMA((k_chunks, n_c)),
            pltpu.SemaphoreType.DMA((k_chunks, n_c)),
            pltpu.SemaphoreType.DMA,
        ],
        compiler_params=pltpu.CompilerParams(collective_id=cid, has_side_effects=True),
    )(m2, got, gate)


def body(tokens, gate_in, mix_first, mix_second, twiddle, out_proj):
    seq_rows, chan_cols = tokens.shape
    n_seq = lax.axis_size("seq")
    n_chan = lax.axis_size("chan")
    blocks_here = seq_rows // B1
    per_dev_i = B1 // n_seq
    d_out = out_proj.shape[1]

    blocked = tokens.reshape(blocks_here, B1, chan_cols)
    mf = mix_first.reshape(n_seq, per_dev_i, B1)
    tw = twiddle.reshape(blocks_here, n_seq, per_dev_i).transpose(1, 0, 2)
    first = jnp.einsum("dik,bkc->dbic", mf, blocked, preferred_element_type=jnp.float32)
    first = (first * tw[:, :, :, None]).astype(jnp.bfloat16)
    got = _a2a(first, "seq", 0)
    got = got.reshape(n_seq * blocks_here, per_dev_i, chan_cols)
    gate = gate_in.reshape(blocks_here, B1, chan_cols)
    full = _back_gate_send(mix_second, got, gate, n_seq, n_chan, CHUNKS, 1)
    rows_per = seq_rows // n_chan
    full = full.reshape(n_chan, rows_per, chan_cols)
    wts = out_proj.reshape(n_chan, chan_cols, n_chan, d_out // n_chan)
    mixed = jnp.einsum("spc,scex->epx", full, wts, preferred_element_type=jnp.float32)
    mixed = mixed.astype(jnp.bfloat16)
    res = _a2a(mixed, "chan", 3)
    return res.reshape(seq_rows, chan_cols)


def solution(mesh):
    placed = (
        P(("batch", "seq"), "chan"),
        P(("batch", "seq"), "chan"),
        P(),
        P(),
        P("seq", None),
        P(),
    )
    return jax.shard_map(
        body, mesh=mesh, in_specs=placed, out_specs=P(("batch", "seq"), "chan"), check_vma=False
    )
```

```python
import functools

import jax
import jax.numpy as jnp
from jax import lax
from jax.sharding import PartitionSpec as P
from jax.experimental import pallas as pl
from jax.experimental.pallas import tpu as pltpu

B1 = 512
CHUNKS = 4
LEAD = 1


def _a2a_kernel(axis, n, x_ref, o_ref, send_sem, recv_sem, loc_sem):
    me = lax.axis_index(axis)
    barrier = pltpu.get_barrier_semaphore()
    for t in range(1, n):
        pl.semaphore_signal(barrier, inc=1, device_id={axis: (me + t) % n},
                            device_id_type=pl.DeviceIdType.MESH)
    pl.semaphore_wait(barrier, n - 1)
    local = pltpu.make_async_copy(x_ref.at[me], o_ref.at[me], loc_sem)
    local.start()
    copies = []
    for t in range(1, n):
        dst = (me + t) % n
        c = pltpu.make_async_remote_copy(
            src_ref=x_ref.at[dst],
            dst_ref=o_ref.at[me],
            send_sem=send_sem.at[t],
            recv_sem=recv_sem.at[t],
            device_id={axis: dst},
            device_id_type=pl.DeviceIdType.MESH,
        )
        c.start()
        copies.append(c)
    local.wait()
    for c in copies:
        c.wait_send()
    for c in copies:
        c.wait_recv()


def _a2a(x, axis, cid):
    n = x.shape[0]
    return pl.pallas_call(
        functools.partial(_a2a_kernel, axis, n),
        out_shape=jax.ShapeDtypeStruct(x.shape, x.dtype),
        in_specs=[pl.BlockSpec(memory_space=pl.ANY)],
        out_specs=pl.BlockSpec(memory_space=pl.ANY),
        scratch_shapes=[
            pltpu.SemaphoreType.DMA((n,)),
            pltpu.SemaphoreType.DMA((n,)),
            pltpu.SemaphoreType.DMA,
        ],
        compiler_params=pltpu.CompilerParams(collective_id=cid, has_side_effects=True),
    )(x)


def _back_gate_send_kernel(k_chunks, m_ref, got_ref, gate_ref, full_ref, sec, recv_s, gv, hid,
                           s_send, s_recv, c_send, c_recv, g_sem):
    n_s, n_j, n_i, _ = sec.shape
    n_c = full_ref.shape[0]
    jp = n_j // n_c
    w = n_i // k_chunks
    me_s = lax.axis_index("seq")
    me_c = lax.axis_index("chan")
    mesh_ids = pl.DeviceIdType.MESH
    barrier = pltpu.get_barrier_semaphore()
    for t in range(1, n_s):
        pl.semaphore_signal(barrier, inc=1, device_id={"seq": (me_s + t) % n_s}, device_id_type=mesh_ids)
    for t in range(1, n_c):
        pl.semaphore_signal(barrier, inc=1, device_id={"chan": (me_c + t) % n_c}, device_id_type=mesh_ids)
    pl.semaphore_wait(barrier, (n_s - 1) + (n_c - 1))

    gcopy = pltpu.make_async_copy(gate_ref, gv, g_sem)
    gcopy.start()
    def issue_seq(k):
        isl = pl.ds(k * w, w)
        m = m_ref[...]
        for i in range(k * w, (k + 1) * w):
            part = jnp.dot(m, got_ref[:, i, :], preferred_element_type=jnp.float32)
            sec[:, :, i, :] = part.astype(sec.dtype).reshape(n_s, n_j, part.shape[-1])
        row = []
        for t in range(n_s):
            if t == 0:
                c = pltpu.make_async_copy(sec.at[me_s, :, isl], recv_s.at[me_s, :, isl], s_recv.at[k, 0])
            else:
                dst = (me_s + t) % n_s
                c = pltpu.make_async_remote_copy(
                    src_ref=sec.at[dst, :, isl],
                    dst_ref=recv_s.at[me_s, :, isl],
                    send_sem=s_send.at[k, t],
                    recv_sem=s_recv.at[k, t],
                    device_id={"seq": dst},
                    device_id_type=mesh_ids,
                )
            c.start()
            row.append(c)
        return row

    seq_copies = [issue_seq(k) for k in range(min(LEAD, k_chunks))]
    gcopy.wait()
    chan_copies = []
    for k in range(k_chunks):
        isl = pl.ds(k * w, w)
        for t in range(n_s):
            if t == 0:
                seq_copies[k][t].wait()
            else:
                seq_copies[k][t].wait_recv()
        for s in range(n_s):
            prod = recv_s[s, :, isl, :].astype(jnp.float32) * gv[:, pl.ds(s * n_i + k * w, w), :].astype(jnp.float32)
            hid[:, s, isl, :] = prod.astype(hid.dtype)
        for t in range(n_c):
            dst = (me_c + t) % n_c
            src_view = hid.at[pl.ds(dst * jp, jp), :, isl, :]
            dst_view = full_ref.at[me_c, :, :, isl, :]
            if t == 0:
                c = pltpu.make_async_copy(src_view, dst_view, c_recv.at[k, 0])
            else:
                c = pltpu.make_async_remote_copy(
                    src_ref=src_view,
                    dst_ref=dst_view,
                    send_sem=c_send.at[k, t],
                    recv_sem=c_recv.at[k, t],
                    device_id={"chan": dst},
                    device_id_type=mesh_ids,
                )
            c.start()
            chan_copies.append((t, c))
        if k + LEAD < k_chunks:
            seq_copies.append(issue_seq(k + LEAD))
    for row in seq_copies:
        for c in row[1:]:
            c.wait_send()
    for t, c in chan_copies:
        if t == 0:
            c.wait()
        else:
            c.wait_send()
    for t, c in chan_copies:
        if t != 0:
            c.wait_recv()


def _back_gate_send(m2, got, gate, n_s, n_c, k_chunks, cid):
    _, n_i, cols = got.shape
    n_j = got.shape[0] // n_s
    jp = n_j // n_c
    return pl.pallas_call(
        functools.partial(_back_gate_send_kernel, k_chunks),
        out_shape=jax.ShapeDtypeStruct((n_c, jp, n_s, n_i, cols), got.dtype),
        in_specs=[pl.BlockSpec(memory_space=pltpu.VMEM)] * 2 + [pl.BlockSpec(memory_space=pl.ANY)],
        out_specs=pl.BlockSpec(memory_space=pl.ANY),
        scratch_shapes=[
            pltpu.VMEM((n_s, n_j, n_i, cols), got.dtype),
            pltpu.VMEM((n_s, n_j, n_i, cols), got.dtype),
            pltpu.VMEM((n_j, n_s * n_i, cols), got.dtype),
            pltpu.VMEM((n_j, n_s, n_i, cols), got.dtype),
            pltpu.SemaphoreType.DMA((k_chunks, n_s)),
            pltpu.SemaphoreType.DMA((k_chunks, n_s)),
            pltpu.SemaphoreType.DMA((k_chunks, n_c)),
            pltpu.SemaphoreType.DMA((k_chunks, n_c)),
            pltpu.SemaphoreType.DMA,
        ],
        compiler_params=pltpu.CompilerParams(collective_id=cid, has_side_effects=True),
    )(m2, got, gate)


def body(tokens, gate_in, mix_first, mix_second, twiddle, out_proj):
    seq_rows, chan_cols = tokens.shape
    n_seq = lax.axis_size("seq")
    n_chan = lax.axis_size("chan")
    blocks_here = seq_rows // B1
    per_dev_i = B1 // n_seq
    d_out = out_proj.shape[1]

    blocked = tokens.reshape(blocks_here, B1, chan_cols)
    mf = mix_first.reshape(n_seq, per_dev_i, B1)
    tw = twiddle.reshape(blocks_here, n_seq, per_dev_i).transpose(1, 0, 2)
    first = jnp.einsum("dik,bkc->dbic", mf, blocked, preferred_element_type=jnp.float32)
    first = (first * tw[:, :, :, None]).astype(jnp.bfloat16)
    got = _a2a(first, "seq", 0)
    got = got.reshape(n_seq * blocks_here, per_dev_i, chan_cols)
    gate = gate_in.reshape(blocks_here, B1, chan_cols)
    full = _back_gate_send(mix_second, got, gate, n_seq, n_chan, CHUNKS, 1)
    rows_per = seq_rows // n_chan
    full = full.reshape(n_chan, rows_per, chan_cols)
    wts = out_proj.reshape(n_chan, chan_cols, n_chan, d_out // n_chan)
    mixed = jnp.einsum("spc,scex->epx", full, wts, preferred_element_type=jnp.float32)
    mixed = mixed.astype(jnp.bfloat16)
    res = _a2a(mixed, "chan", 3)
    return res.reshape(seq_rows, chan_cols)


def solution(mesh):
    placed = (
        P(("batch", "seq"), "chan"),
        P(("batch", "seq"), "chan"),
        P(),
        P(),
        P("seq", None),
        P(),
    )
    return jax.shard_map(
        body, mesh=mesh, in_specs=placed, out_specs=P(("batch", "seq"), "chan"), check_vma=False
    )
```

```python
import functools

import jax
import jax.numpy as jnp
from jax import lax
from jax.sharding import PartitionSpec as P
from jax.experimental import pallas as pl
from jax.experimental.pallas import tpu as pltpu

B1 = 512
CHUNKS = 4
LEAD = 2


def _a2a_kernel(axis, n, x_ref, o_ref, send_sem, recv_sem, loc_sem):
    me = lax.axis_index(axis)
    cols = o_ref.shape[-1]

    def piece(d):
        if len(x_ref.shape) == len(o_ref.shape):
            return x_ref.at[d]
        return x_ref.at[:, pl.ds(pl.multiple_of(d * cols, cols), cols)]

    barrier = pltpu.get_barrier_semaphore()
    for t in range(1, n):
        pl.semaphore_signal(barrier, inc=1, device_id={axis: (me + t) % n},
                            device_id_type=pl.DeviceIdType.MESH)
    pl.semaphore_wait(barrier, n - 1)
    local = pltpu.make_async_copy(piece(me), o_ref.at[me], loc_sem)
    local.start()
    copies = []
    for t in range(1, n):
        dst = (me + t) % n
        c = pltpu.make_async_remote_copy(
            src_ref=piece(dst),
            dst_ref=o_ref.at[me],
            send_sem=send_sem.at[t],
            recv_sem=recv_sem.at[t],
            device_id={axis: dst},
            device_id_type=pl.DeviceIdType.MESH,
        )
        c.start()
        copies.append(c)
    local.wait()
    for c in copies:
        c.wait_send()
    for c in copies:
        c.wait_recv()


def _a2a(x, axis, cid, n=None):
    if n is None:
        n = x.shape[0]
        shape = x.shape
    else:
        shape = (n, x.shape[0], x.shape[1] // n)
    return pl.pallas_call(
        functools.partial(_a2a_kernel, axis, n),
        out_shape=jax.ShapeDtypeStruct(shape, x.dtype),
        in_specs=[pl.BlockSpec(memory_space=pl.ANY)],
        out_specs=pl.BlockSpec(memory_space=pl.ANY),
        scratch_shapes=[
            pltpu.SemaphoreType.DMA((n,)),
            pltpu.SemaphoreType.DMA((n,)),
            pltpu.SemaphoreType.DMA,
        ],
        compiler_params=pltpu.CompilerParams(collective_id=cid, has_side_effects=True),
    )(x)


def _back_gate_send_kernel(k_chunks, m_ref, got_ref, gate_ref, full_ref, sec, recv_s, gv, hid,
                           s_send, s_recv, c_send, c_recv, g_sem):
    n_s, n_j, n_i, cols = sec.shape
    n_c = full_ref.shape[-1] // cols
    jp = n_j // n_c
    w = n_i // k_chunks
    me_s = lax.axis_index("seq")
    me_c = lax.axis_index("chan")
    mesh_ids = pl.DeviceIdType.MESH
    barrier = pltpu.get_barrier_semaphore()
    for t in range(1, n_s):
        pl.semaphore_signal(barrier, inc=1, device_id={"seq": (me_s + t) % n_s}, device_id_type=mesh_ids)
    for t in range(1, n_c):
        pl.semaphore_signal(barrier, inc=1, device_id={"chan": (me_c + t) % n_c}, device_id_type=mesh_ids)
    pl.semaphore_wait(barrier, (n_s - 1) + (n_c - 1))

    gcopy = pltpu.make_async_copy(gate_ref, gv, g_sem)
    gcopy.start()
    def issue_seq(k):
        isl = pl.ds(k * w, w)
        m = m_ref[...]
        for i in range(k * w, (k + 1) * w):
            part = jnp.dot(m, got_ref[:, i, :], preferred_element_type=jnp.float32)
            sec[:, :, i, :] = part.astype(sec.dtype).reshape(n_s, n_j, part.shape[-1])
        row = []
        for t in range(n_s):
            if t == 0:
                c = pltpu.make_async_copy(sec.at[me_s, :, isl], recv_s.at[me_s, :, isl], s_recv.at[k, 0])
            else:
                dst = (me_s + t) % n_s
                c = pltpu.make_async_remote_copy(
                    src_ref=sec.at[dst, :, isl],
                    dst_ref=recv_s.at[me_s, :, isl],
                    send_sem=s_send.at[k, t],
                    recv_sem=s_recv.at[k, t],
                    device_id={"seq": dst},
                    device_id_type=mesh_ids,
                )
            c.start()
            row.append(c)
        return row

    seq_copies = [issue_seq(k) for k in range(min(LEAD, k_chunks))]
    gcopy.wait()
    chan_copies = []
    for k in range(k_chunks):
        isl = pl.ds(k * w, w)
        for t in range(n_s):
            if t == 0:
                seq_copies[k][t].wait()
            else:
                seq_copies[k][t].wait_recv()
        for s in range(n_s):
            prod = recv_s[s, :, isl, :].astype(jnp.float32) * gv[:, pl.ds(s * n_i + k * w, w), :].astype(jnp.float32)
            hid[:, s, isl, :] = prod.astype(hid.dtype)
        for t in range(n_c):
            dst = (me_c + t) % n_c
            src_view = hid.at[pl.ds(dst * jp, jp), :, isl, :]
            dst_view = full_ref.at[:, :, isl, pl.ds(pl.multiple_of(me_c * cols, cols), cols)]
            if t == 0:
                c = pltpu.make_async_copy(src_view, dst_view, c_recv.at[k, 0])
            else:
                c = pltpu.make_async_remote_copy(
                    src_ref=src_view,
                    dst_ref=dst_view,
                    send_sem=c_send.at[k, t],
                    recv_sem=c_recv.at[k, t],
                    device_id={"chan": dst},
                    device_id_type=mesh_ids,
                )
            c.start()
            chan_copies.append((t, c))
        if k + LEAD < k_chunks:
            seq_copies.append(issue_seq(k + LEAD))
    for row in seq_copies:
        for c in row[1:]:
            c.wait_send()
    for t, c in chan_copies:
        if t == 0:
            c.wait()
        else:
            c.wait_send()
    for t, c in chan_copies:
        if t != 0:
            c.wait_recv()


def _back_gate_send(m2, got, gate, n_s, n_c, k_chunks, cid):
    _, n_i, cols = got.shape
    n_j = got.shape[0] // n_s
    jp = n_j // n_c
    return pl.pallas_call(
        functools.partial(_back_gate_send_kernel, k_chunks),
        out_shape=jax.ShapeDtypeStruct((jp, n_s, n_i, n_c * cols), got.dtype),
        in_specs=[pl.BlockSpec(memory_space=pltpu.VMEM)] * 2 + [pl.BlockSpec(memory_space=pl.ANY)],
        out_specs=pl.BlockSpec(memory_space=pl.ANY),
        scratch_shapes=[
            pltpu.VMEM((n_s, n_j, n_i, cols), got.dtype),
            pltpu.VMEM((n_s, n_j, n_i, cols), got.dtype),
            pltpu.VMEM((n_j, n_s * n_i, cols), got.dtype),
            pltpu.VMEM((n_j, n_s, n_i, cols), got.dtype),
            pltpu.SemaphoreType.DMA((k_chunks, n_s)),
            pltpu.SemaphoreType.DMA((k_chunks, n_s)),
            pltpu.SemaphoreType.DMA((k_chunks, n_c)),
            pltpu.SemaphoreType.DMA((k_chunks, n_c)),
            pltpu.SemaphoreType.DMA,
        ],
        compiler_params=pltpu.CompilerParams(collective_id=cid, has_side_effects=True),
    )(m2, got, gate)


def body(tokens, gate_in, mix_first, mix_second, twiddle, out_proj):
    seq_rows, chan_cols = tokens.shape
    n_seq = lax.axis_size("seq")
    n_chan = lax.axis_size("chan")
    blocks_here = seq_rows // B1
    per_dev_i = B1 // n_seq
    d_out = out_proj.shape[1]

    blocked = tokens.reshape(blocks_here, B1, chan_cols)
    mf = mix_first.reshape(n_seq, per_dev_i, B1)
    tw = twiddle.reshape(blocks_here, n_seq, per_dev_i).transpose(1, 0, 2)
    first = jnp.einsum("dik,bkc->dbic", mf, blocked, preferred_element_type=jnp.float32)
    first = (first * tw[:, :, :, None]).astype(jnp.bfloat16)
    got = _a2a(first, "seq", 0)
    got = got.reshape(n_seq * blocks_here, per_dev_i, chan_cols)
    gate = gate_in.reshape(blocks_here, B1, chan_cols)
    full = _back_gate_send(mix_second, got, gate, n_seq, n_chan, CHUNKS, 1)
    rows_per = seq_rows // n_chan
    full = full.reshape(rows_per, n_chan * chan_cols)
    mixed = jnp.dot(full, out_proj, preferred_element_type=jnp.float32).astype(jnp.bfloat16)
    res = _a2a(mixed, "chan", 3, n=n_chan)
    return res.reshape(seq_rows, chan_cols)


def solution(mesh):
    placed = (
        P(("batch", "seq"), "chan"),
        P(("batch", "seq"), "chan"),
        P(),
        P(),
        P("seq", None),
        P(),
    )
    return jax.shard_map(
        body, mesh=mesh, in_specs=placed, out_specs=P(("batch", "seq"), "chan"), check_vma=False
    )
```

```python
import functools

import jax
import jax.numpy as jnp
from jax import lax
from jax.sharding import PartitionSpec as P
from jax.experimental import pallas as pl
from jax.experimental.pallas import tpu as pltpu

B1 = 512
CHUNKS = 4
LEAD = 2


def _a2a_kernel(axis, n, x_ref, o_ref, send_sem, recv_sem, loc_sem):
    me = lax.axis_index(axis)
    cols = o_ref.shape[-1]

    def piece(d):
        if len(x_ref.shape) == len(o_ref.shape):
            return x_ref.at[d]
        return x_ref.at[:, pl.ds(pl.multiple_of(d * cols, cols), cols)]

    barrier = pltpu.get_barrier_semaphore()
    for t in range(1, n):
        pl.semaphore_signal(barrier, inc=1, device_id={axis: (me + t) % n},
                            device_id_type=pl.DeviceIdType.MESH)
    pl.semaphore_wait(barrier, n - 1)
    local = pltpu.make_async_copy(piece(me), o_ref.at[me], loc_sem)
    local.start()
    copies = []
    for t in range(1, n):
        dst = (me + t) % n
        c = pltpu.make_async_remote_copy(
            src_ref=piece(dst),
            dst_ref=o_ref.at[me],
            send_sem=send_sem.at[t],
            recv_sem=recv_sem.at[t],
            device_id={axis: dst},
            device_id_type=pl.DeviceIdType.MESH,
        )
        c.start()
        copies.append(c)
    local.wait()
    for c in copies:
        c.wait_send()
    for c in copies:
        c.wait_recv()


def _a2a(x, axis, cid, n=None):
    if n is None:
        n = x.shape[0]
        shape = x.shape
    else:
        shape = (n, x.shape[0], x.shape[1] // n)
    return pl.pallas_call(
        functools.partial(_a2a_kernel, axis, n),
        out_shape=jax.ShapeDtypeStruct(shape, x.dtype),
        in_specs=[pl.BlockSpec(memory_space=pl.ANY)],
        out_specs=pl.BlockSpec(memory_space=pl.ANY),
        scratch_shapes=[
            pltpu.SemaphoreType.DMA((n,)),
            pltpu.SemaphoreType.DMA((n,)),
            pltpu.SemaphoreType.DMA,
        ],
        compiler_params=pltpu.CompilerParams(collective_id=cid, has_side_effects=True),
    )(x)


def _back_gate_send_kernel(k_chunks, m_ref, got_ref, gate_ref, full_ref, sec, recv_s, gv, hid,
                           s_send, s_recv, c_send, c_recv, g_sem):
    n_s, n_j, n_i, cols = sec.shape
    n_c = full_ref.shape[-1] // cols
    jp = n_j // n_c
    w = n_i // k_chunks
    me_s = lax.axis_index("seq")
    me_c = lax.axis_index("chan")
    mesh_ids = pl.DeviceIdType.MESH
    barrier = pltpu.get_barrier_semaphore()
    for t in range(1, n_s):
        pl.semaphore_signal(barrier, inc=1, device_id={"seq": (me_s + t) % n_s}, device_id_type=mesh_ids)
    for t in range(1, n_c):
        pl.semaphore_signal(barrier, inc=1, device_id={"chan": (me_c + t) % n_c}, device_id_type=mesh_ids)
    pl.semaphore_wait(barrier, (n_s - 1) + (n_c - 1))

    gcopy = pltpu.make_async_copy(gate_ref, gv, g_sem)
    gcopy.start()
    def issue_seq(k):
        isl = pl.ds(k * w, w)
        m = m_ref[...]
        for i in range(k * w, (k + 1) * w):
            part = jnp.dot(m, got_ref[:, i, :], preferred_element_type=jnp.float32)
            sec[:, :, i, :] = part.astype(sec.dtype).reshape(n_s, n_j, part.shape[-1])
        row = []
        for t in range(n_s):
            if t == 0:
                c = pltpu.make_async_copy(sec.at[me_s, :, isl], recv_s.at[me_s, :, isl], s_recv.at[k, 0])
            else:
                dst = (me_s + t) % n_s
                c = pltpu.make_async_remote_copy(
                    src_ref=sec.at[dst, :, isl],
                    dst_ref=recv_s.at[me_s, :, isl],
                    send_sem=s_send.at[k, t],
                    recv_sem=s_recv.at[k, t],
                    device_id={"seq": dst},
                    device_id_type=mesh_ids,
                )
            c.start()
            row.append(c)
        return row

    seq_copies = [issue_seq(k) for k in range(min(LEAD, k_chunks))]
    gcopy.wait()
    chan_copies = []
    for k in range(k_chunks):
        isl = pl.ds(k * w, w)
        for t in range(n_s):
            if t == 0:
                seq_copies[k][t].wait()
            else:
                seq_copies[k][t].wait_recv()
        for s in range(n_s):
            prod = recv_s[s, :, isl, :].astype(jnp.float32) * gv[:, pl.ds(s * n_i + k * w, w), :].astype(jnp.float32)
            hid[:, s, isl, :] = prod.astype(hid.dtype)
        for t in range(n_c):
            dst = (me_c + t) % n_c
            src_view = hid.at[pl.ds(dst * jp, jp), :, isl, :]
            dst_view = full_ref.at[:, :, isl, pl.ds(pl.multiple_of(me_c * cols, cols), cols)]
            if t == 0:
                c = pltpu.make_async_copy(src_view, dst_view, c_recv.at[k, 0])
            else:
                c = pltpu.make_async_remote_copy(
                    src_ref=src_view,
                    dst_ref=dst_view,
                    send_sem=c_send.at[k, t],
                    recv_sem=c_recv.at[k, t],
                    device_id={"chan": dst},
                    device_id_type=mesh_ids,
                )
            c.start()
            chan_copies.append((t, c))
        if k + LEAD < k_chunks:
            seq_copies.append(issue_seq(k + LEAD))
    for row in seq_copies:
        for c in row[1:]:
            c.wait_send()
    for t, c in chan_copies:
        if t == 0:
            c.wait()
        else:
            c.wait_send()
    for t, c in chan_copies:
        if t != 0:
            c.wait_recv()


def _back_gate_send(m2, got, gate, n_s, n_c, k_chunks, cid):
    _, n_i, cols = got.shape
    n_j = got.shape[0] // n_s
    jp = n_j // n_c
    return pl.pallas_call(
        functools.partial(_back_gate_send_kernel, k_chunks),
        out_shape=jax.ShapeDtypeStruct((jp, n_s, n_i, n_c * cols), got.dtype),
        in_specs=[pl.BlockSpec(memory_space=pltpu.VMEM)] * 2 + [pl.BlockSpec(memory_space=pl.ANY)],
        out_specs=pl.BlockSpec(memory_space=pl.ANY),
        scratch_shapes=[
            pltpu.VMEM((n_s, n_j, n_i, cols), got.dtype),
            pltpu.VMEM((n_s, n_j, n_i, cols), got.dtype),
            pltpu.VMEM((n_j, n_s * n_i, cols), got.dtype),
            pltpu.VMEM((n_j, n_s, n_i, cols), got.dtype),
            pltpu.SemaphoreType.DMA((k_chunks, n_s)),
            pltpu.SemaphoreType.DMA((k_chunks, n_s)),
            pltpu.SemaphoreType.DMA((k_chunks, n_c)),
            pltpu.SemaphoreType.DMA((k_chunks, n_c)),
            pltpu.SemaphoreType.DMA,
        ],
        compiler_params=pltpu.CompilerParams(collective_id=cid, has_side_effects=True),
    )(m2, got, gate)


def _project_send_kernel(full_ref, w_ref, res_ref, stage, send_sem, recv_sem):
    n_c, rows, cols = stage.shape
    me = lax.axis_index("chan")
    mesh_ids = pl.DeviceIdType.MESH
    barrier = pltpu.get_barrier_semaphore()
    for t in range(1, n_c):
        pl.semaphore_signal(barrier, inc=1, device_id={"chan": (me + t) % n_c}, device_id_type=mesh_ids)
    pl.semaphore_wait(barrier, n_c - 1)
    copies = []
    for t in list(range(1, n_c)) + [0]:
        dst = (me + t) % n_c
        out_cols = pl.ds(pl.multiple_of(dst * cols, cols), cols)
        part = jnp.dot(full_ref[...], w_ref[:, out_cols], preferred_element_type=jnp.float32)
        stage[t] = part.astype(stage.dtype)
        if t == 0:
            c = pltpu.make_async_copy(stage.at[t], res_ref.at[me], recv_sem.at[0])
        else:
            c = pltpu.make_async_remote_copy(
                src_ref=stage.at[t],
                dst_ref=res_ref.at[me],
                send_sem=send_sem.at[t],
                recv_sem=recv_sem.at[t],
                device_id={"chan": dst},
                device_id_type=mesh_ids,
            )
        c.start()
        copies.append((t, c))
    for t, c in copies:
        if t == 0:
            c.wait()
        else:
            c.wait_send()
    for t, c in copies:
        if t != 0:
            c.wait_recv()


def _project_send(full, w, n_c, cid):
    rows, _ = full.shape
    cols = w.shape[1] // n_c
    return pl.pallas_call(
        _project_send_kernel,
        out_shape=jax.ShapeDtypeStruct((n_c, rows, cols), full.dtype),
        in_specs=[pl.BlockSpec(memory_space=pltpu.VMEM)] * 2,
        out_specs=pl.BlockSpec(memory_space=pl.ANY),
        scratch_shapes=[
            pltpu.VMEM((n_c, rows, cols), full.dtype),
            pltpu.SemaphoreType.DMA((n_c,)),
            pltpu.SemaphoreType.DMA((n_c,)),
        ],
        compiler_params=pltpu.CompilerParams(collective_id=cid, has_side_effects=True),
    )(full, w)


def body(tokens, gate_in, mix_first, mix_second, twiddle, out_proj):
    seq_rows, chan_cols = tokens.shape
    n_seq = lax.axis_size("seq")
    n_chan = lax.axis_size("chan")
    blocks_here = seq_rows // B1
    per_dev_i = B1 // n_seq
    d_out = out_proj.shape[1]

    blocked = tokens.reshape(blocks_here, B1, chan_cols)
    mf = mix_first.reshape(n_seq, per_dev_i, B1)
    tw = twiddle.reshape(blocks_here, n_seq, per_dev_i).transpose(1, 0, 2)
    first = jnp.einsum("dik,bkc->dbic", mf, blocked, preferred_element_type=jnp.float32)
    first = (first * tw[:, :, :, None]).astype(jnp.bfloat16)
    got = _a2a(first, "seq", 0)
    got = got.reshape(n_seq * blocks_here, per_dev_i, chan_cols)
    gate = gate_in.reshape(blocks_here, B1, chan_cols)
    full = _back_gate_send(mix_second, got, gate, n_seq, n_chan, CHUNKS, 1)
    rows_per = seq_rows // n_chan
    full = full.reshape(rows_per, n_chan * chan_cols)
    res = _project_send(full, out_proj, n_chan, 3)
    return res.reshape(seq_rows, chan_cols)


def solution(mesh):
    placed = (
        P(("batch", "seq"), "chan"),
        P(("batch", "seq"), "chan"),
        P(),
        P(),
        P("seq", None),
        P(),
    )
    return jax.shard_map(
        body, mesh=mesh, in_specs=placed, out_specs=P(("batch", "seq"), "chan"), check_vma=False
    )
```

```python
import functools

import jax
import jax.numpy as jnp
from jax import lax
from jax.sharding import PartitionSpec as P
from jax.experimental import pallas as pl
from jax.experimental.pallas import tpu as pltpu

B1 = 512
CHUNKS = 4
LEAD = 2


def _a2a_kernel(axis, n, x_ref, o_ref, send_sem, recv_sem, loc_sem):
    me = lax.axis_index(axis)
    barrier = pltpu.get_barrier_semaphore()
    for t in range(1, n):
        pl.semaphore_signal(barrier, inc=1, device_id={axis: (me + t) % n},
                            device_id_type=pl.DeviceIdType.MESH)
    pl.semaphore_wait(barrier, n - 1)
    local = pltpu.make_async_copy(x_ref.at[me], o_ref.at[me], loc_sem)
    local.start()
    copies = []
    for t in list(range(1, n, 2)) + list(range(2, n, 2)):
        dst = (me + t) % n
        c = pltpu.make_async_remote_copy(
            src_ref=x_ref.at[dst],
            dst_ref=o_ref.at[me],
            send_sem=send_sem.at[t],
            recv_sem=recv_sem.at[t],
            device_id={axis: dst},
            device_id_type=pl.DeviceIdType.MESH,
        )
        c.start()
        copies.append(c)
    local.wait()
    for c in copies:
        c.wait_send()
    for c in copies:
        c.wait_recv()


def _a2a(x, axis, cid):
    n = x.shape[0]
    return pl.pallas_call(
        functools.partial(_a2a_kernel, axis, n),
        out_shape=jax.ShapeDtypeStruct(x.shape, x.dtype),
        in_specs=[pl.BlockSpec(memory_space=pl.ANY)],
        out_specs=pl.BlockSpec(memory_space=pl.ANY),
        scratch_shapes=[
            pltpu.SemaphoreType.DMA((n,)),
            pltpu.SemaphoreType.DMA((n,)),
            pltpu.SemaphoreType.DMA,
        ],
        compiler_params=pltpu.CompilerParams(collective_id=cid, has_side_effects=True),
    )(x)


def _back_gate_send_kernel(k_chunks, m_ref, got_ref, gate_ref, full_ref, sec, recv_s, gv, hid,
                           s_send, s_recv, c_send, c_recv, g_sem):
    n_s, n_j, n_i, _ = sec.shape
    n_c = full_ref.shape[0]
    jp = n_j // n_c
    w = n_i // k_chunks
    me_s = lax.axis_index("seq")
    me_c = lax.axis_index("chan")
    mesh_ids = pl.DeviceIdType.MESH
    barrier = pltpu.get_barrier_semaphore()
    for t in range(1, n_s):
        pl.semaphore_signal(barrier, inc=1, device_id={"seq": (me_s + t) % n_s}, device_id_type=mesh_ids)
    for t in range(1, n_c):
        pl.semaphore_signal(barrier, inc=1, device_id={"chan": (me_c + t) % n_c}, device_id_type=mesh_ids)
    pl.semaphore_wait(barrier, (n_s - 1) + (n_c - 1))

    gcopy = pltpu.make_async_copy(gate_ref, gv, g_sem)
    gcopy.start()
    def issue_seq(k):
        isl = pl.ds(k * w, w)
        m = m_ref[...]
        for i in range(k * w, (k + 1) * w):
            part = jnp.dot(m, got_ref[:, i, :], preferred_element_type=jnp.float32)
            sec[:, :, i, :] = part.astype(sec.dtype).reshape(n_s, n_j, part.shape[-1])
        row = []
        for t in range(n_s):
            if t == 0:
                c = pltpu.make_async_copy(sec.at[me_s, :, isl], recv_s.at[me_s, :, isl], s_recv.at[k, 0])
            else:
                dst = (me_s + t) % n_s
                c = pltpu.make_async_remote_copy(
                    src_ref=sec.at[dst, :, isl],
                    dst_ref=recv_s.at[me_s, :, isl],
                    send_sem=s_send.at[k, t],
                    recv_sem=s_recv.at[k, t],
                    device_id={"seq": dst},
                    device_id_type=mesh_ids,
                )
            c.start()
            row.append(c)
        return row

    seq_copies = [issue_seq(k) for k in range(min(LEAD, k_chunks))]
    gcopy.wait()
    chan_copies = []
    for k in range(k_chunks):
        isl = pl.ds(k * w, w)
        for t in range(n_s):
            if t == 0:
                seq_copies[k][t].wait()
            else:
                seq_copies[k][t].wait_recv()
        for s in range(n_s):
            prod = recv_s[s, :, isl, :].astype(jnp.float32) * gv[:, pl.ds(s * n_i + k * w, w), :].astype(jnp.float32)
            hid[:, s, isl, :] = prod.astype(hid.dtype)
        for t in range(n_c):
            dst = (me_c + t) % n_c
            src_view = hid.at[pl.ds(dst * jp, jp), :, isl, :]
            dst_view = full_ref.at[me_c, :, :, isl, :]
            if t == 0:
                c = pltpu.make_async_copy(src_view, dst_view, c_recv.at[k, 0])
            else:
                c = pltpu.make_async_remote_copy(
                    src_ref=src_view,
                    dst_ref=dst_view,
                    send_sem=c_send.at[k, t],
                    recv_sem=c_recv.at[k, t],
                    device_id={"chan": dst},
                    device_id_type=mesh_ids,
                )
            c.start()
            chan_copies.append((t, c))
        if k + LEAD < k_chunks:
            seq_copies.append(issue_seq(k + LEAD))
    for row in seq_copies:
        for c in row[1:]:
            c.wait_send()
    for t, c in chan_copies:
        if t == 0:
            c.wait()
        else:
            c.wait_send()
    for t, c in chan_copies:
        if t != 0:
            c.wait_recv()


def _back_gate_send(m2, got, gate, n_s, n_c, k_chunks, cid):
    _, n_i, cols = got.shape
    n_j = got.shape[0] // n_s
    jp = n_j // n_c
    return pl.pallas_call(
        functools.partial(_back_gate_send_kernel, k_chunks),
        out_shape=jax.ShapeDtypeStruct((n_c, jp, n_s, n_i, cols), got.dtype),
        in_specs=[pl.BlockSpec(memory_space=pltpu.VMEM)] * 2 + [pl.BlockSpec(memory_space=pl.ANY)],
        out_specs=pl.BlockSpec(memory_space=pl.ANY),
        scratch_shapes=[
            pltpu.VMEM((n_s, n_j, n_i, cols), got.dtype),
            pltpu.VMEM((n_s, n_j, n_i, cols), got.dtype),
            pltpu.VMEM((n_j, n_s * n_i, cols), got.dtype),
            pltpu.VMEM((n_j, n_s, n_i, cols), got.dtype),
            pltpu.SemaphoreType.DMA((k_chunks, n_s)),
            pltpu.SemaphoreType.DMA((k_chunks, n_s)),
            pltpu.SemaphoreType.DMA((k_chunks, n_c)),
            pltpu.SemaphoreType.DMA((k_chunks, n_c)),
            pltpu.SemaphoreType.DMA,
        ],
        compiler_params=pltpu.CompilerParams(collective_id=cid, has_side_effects=True),
    )(m2, got, gate)


def body(tokens, gate_in, mix_first, mix_second, twiddle, out_proj):
    seq_rows, chan_cols = tokens.shape
    n_seq = lax.axis_size("seq")
    n_chan = lax.axis_size("chan")
    blocks_here = seq_rows // B1
    per_dev_i = B1 // n_seq
    d_out = out_proj.shape[1]

    blocked = tokens.reshape(blocks_here, B1, chan_cols)
    mf = mix_first.reshape(n_seq, per_dev_i, B1)
    tw = twiddle.reshape(blocks_here, n_seq, per_dev_i).transpose(1, 0, 2)
    first = jnp.einsum("dik,bkc->dbic", mf, blocked, preferred_element_type=jnp.float32)
    first = (first * tw[:, :, :, None]).astype(jnp.bfloat16)
    got = _a2a(first, "seq", 0)
    got = got.reshape(n_seq * blocks_here, per_dev_i, chan_cols)
    gate = gate_in.reshape(blocks_here, B1, chan_cols)
    full = _back_gate_send(mix_second, got, gate, n_seq, n_chan, CHUNKS, 1)
    rows_per = seq_rows // n_chan
    full = full.reshape(n_chan, rows_per, chan_cols)
    wts = out_proj.reshape(n_chan, chan_cols, n_chan, d_out // n_chan)
    mixed = jnp.einsum("spc,scex->epx", full, wts, preferred_element_type=jnp.float32)
    mixed = mixed.astype(jnp.bfloat16)
    res = _a2a(mixed, "chan", 3)
    return res.reshape(seq_rows, chan_cols)


def solution(mesh):
    placed = (
        P(("batch", "seq"), "chan"),
        P(("batch", "seq"), "chan"),
        P(),
        P(),
        P("seq", None),
        P(),
    )
    return jax.shard_map(
        body, mesh=mesh, in_specs=placed, out_specs=P(("batch", "seq"), "chan"), check_vma=False
    )
```

```python
import functools

import jax
import jax.numpy as jnp
from jax import lax
from jax.sharding import PartitionSpec as P
from jax.experimental import pallas as pl
from jax.experimental.pallas import tpu as pltpu

B1 = 512
CHUNKS = 2
LEAD = 1


def _a2a_kernel(axis, n, x_ref, o_ref, send_sem, recv_sem, loc_sem):
    me = lax.axis_index(axis)
    barrier = pltpu.get_barrier_semaphore()
    for t in range(1, n):
        pl.semaphore_signal(barrier, inc=1, device_id={axis: (me + t) % n},
                            device_id_type=pl.DeviceIdType.MESH)
    pl.semaphore_wait(barrier, n - 1)
    local = pltpu.make_async_copy(x_ref.at[me], o_ref.at[me], loc_sem)
    local.start()
    copies = []
    for t in range(1, n):
        dst = (me + t) % n
        c = pltpu.make_async_remote_copy(
            src_ref=x_ref.at[dst],
            dst_ref=o_ref.at[me],
            send_sem=send_sem.at[t],
            recv_sem=recv_sem.at[t],
            device_id={axis: dst},
            device_id_type=pl.DeviceIdType.MESH,
        )
        c.start()
        copies.append(c)
    local.wait()
    for c in copies:
        c.wait_send()
    for c in copies:
        c.wait_recv()


def _a2a(x, axis, cid):
    n = x.shape[0]
    return pl.pallas_call(
        functools.partial(_a2a_kernel, axis, n),
        out_shape=jax.ShapeDtypeStruct(x.shape, x.dtype),
        in_specs=[pl.BlockSpec(memory_space=pl.ANY)],
        out_specs=pl.BlockSpec(memory_space=pl.ANY),
        scratch_shapes=[
            pltpu.SemaphoreType.DMA((n,)),
            pltpu.SemaphoreType.DMA((n,)),
            pltpu.SemaphoreType.DMA,
        ],
        compiler_params=pltpu.CompilerParams(collective_id=cid, has_side_effects=True),
    )(x)


def _back_gate_send_kernel(k_chunks, m_ref, got_ref, gate_ref, full_ref, sec, recv_s, gv, hid,
                           s_send, s_recv, c_send, c_recv, g_sem):
    n_s, n_j, n_i, _ = sec.shape
    n_c = full_ref.shape[0]
    jp = n_j // n_c
    w = n_i // k_chunks
    me_s = lax.axis_index("seq")
    me_c = lax.axis_index("chan")
    mesh_ids = pl.DeviceIdType.MESH
    barrier = pltpu.get_barrier_semaphore()
    for t in range(1, n_s):
        pl.semaphore_signal(barrier, inc=1, device_id={"seq": (me_s + t) % n_s}, device_id_type=mesh_ids)
    for t in range(1, n_c):
        pl.semaphore_signal(barrier, inc=1, device_id={"chan": (me_c + t) % n_c}, device_id_type=mesh_ids)
    pl.semaphore_wait(barrier, (n_s - 1) + (n_c - 1))

    gcopy = pltpu.make_async_copy(gate_ref, gv, g_sem)
    gcopy.start()
    def issue_seq(k):
        isl = pl.ds(k * w, w)
        m = m_ref[...]
        for i in range(k * w, (k + 1) * w):
            part = jnp.dot(m, got_ref[:, i, :], preferred_element_type=jnp.float32)
            sec[:, :, i, :] = part.astype(sec.dtype).reshape(n_s, n_j, part.shape[-1])
        row = []
        for t in range(n_s):
            if t == 0:
                c = pltpu.make_async_copy(sec.at[me_s, :, isl], recv_s.at[me_s, :, isl], s_recv.at[k, 0])
            else:
                dst = (me_s + t) % n_s
                c = pltpu.make_async_remote_copy(
                    src_ref=sec.at[dst, :, isl],
                    dst_ref=recv_s.at[me_s, :, isl],
                    send_sem=s_send.at[k, t],
                    recv_sem=s_recv.at[k, t],
                    device_id={"seq": dst},
                    device_id_type=mesh_ids,
                )
            c.start()
            row.append(c)
        return row

    seq_copies = [issue_seq(k) for k in range(min(LEAD, k_chunks))]
    gcopy.wait()
    chan_copies = []
    for k in range(k_chunks):
        isl = pl.ds(k * w, w)
        for t in range(n_s):
            if t == 0:
                seq_copies[k][t].wait()
            else:
                seq_copies[k][t].wait_recv()
        for s in range(n_s):
            prod = recv_s[s, :, isl, :].astype(jnp.float32) * gv[:, pl.ds(s * n_i + k * w, w), :].astype(jnp.float32)
            hid[:, s, isl, :] = prod.astype(hid.dtype)
        for t in range(n_c):
            dst = (me_c + t) % n_c
            src_view = hid.at[pl.ds(dst * jp, jp), :, isl, :]
            dst_view = full_ref.at[me_c, :, :, isl, :]
            if t == 0:
                c = pltpu.make_async_copy(src_view, dst_view, c_recv.at[k, 0])
            else:
                c = pltpu.make_async_remote_copy(
                    src_ref=src_view,
                    dst_ref=dst_view,
                    send_sem=c_send.at[k, t],
                    recv_sem=c_recv.at[k, t],
                    device_id={"chan": dst},
                    device_id_type=mesh_ids,
                )
            c.start()
            chan_copies.append((t, c))
        if k + LEAD < k_chunks:
            seq_copies.append(issue_seq(k + LEAD))
    for row in seq_copies:
        for c in row[1:]:
            c.wait_send()
    for t, c in chan_copies:
        if t == 0:
            c.wait()
        else:
            c.wait_send()
    for t, c in chan_copies:
        if t != 0:
            c.wait_recv()


def _back_gate_send(m2, got, gate, n_s, n_c, k_chunks, cid):
    _, n_i, cols = got.shape
    n_j = got.shape[0] // n_s
    jp = n_j // n_c
    return pl.pallas_call(
        functools.partial(_back_gate_send_kernel, k_chunks),
        out_shape=jax.ShapeDtypeStruct((n_c, jp, n_s, n_i, cols), got.dtype),
        in_specs=[pl.BlockSpec(memory_space=pltpu.VMEM)] * 2 + [pl.BlockSpec(memory_space=pl.ANY)],
        out_specs=pl.BlockSpec(memory_space=pl.ANY),
        scratch_shapes=[
            pltpu.VMEM((n_s, n_j, n_i, cols), got.dtype),
            pltpu.VMEM((n_s, n_j, n_i, cols), got.dtype),
            pltpu.VMEM((n_j, n_s * n_i, cols), got.dtype),
            pltpu.VMEM((n_j, n_s, n_i, cols), got.dtype),
            pltpu.SemaphoreType.DMA((k_chunks, n_s)),
            pltpu.SemaphoreType.DMA((k_chunks, n_s)),
            pltpu.SemaphoreType.DMA((k_chunks, n_c)),
            pltpu.SemaphoreType.DMA((k_chunks, n_c)),
            pltpu.SemaphoreType.DMA,
        ],
        compiler_params=pltpu.CompilerParams(collective_id=cid, has_side_effects=True),
    )(m2, got, gate)


def body(tokens, gate_in, mix_first, mix_second, twiddle, out_proj):
    seq_rows, chan_cols = tokens.shape
    n_seq = lax.axis_size("seq")
    n_chan = lax.axis_size("chan")
    blocks_here = seq_rows // B1
    per_dev_i = B1 // n_seq
    d_out = out_proj.shape[1]

    blocked = tokens.reshape(blocks_here, B1, chan_cols)
    mf = mix_first.reshape(n_seq, per_dev_i, B1)
    tw = twiddle.reshape(blocks_here, n_seq, per_dev_i).transpose(1, 0, 2)
    first = jnp.einsum("dik,bkc->dbic", mf, blocked, preferred_element_type=jnp.float32)
    first = (first * tw[:, :, :, None]).astype(jnp.bfloat16)
    got = _a2a(first, "seq", 0)
    got = got.reshape(n_seq * blocks_here, per_dev_i, chan_cols)
    gate = gate_in.reshape(blocks_here, B1, chan_cols)
    full = _back_gate_send(mix_second, got, gate, n_seq, n_chan, CHUNKS, 1)
    rows_per = seq_rows // n_chan
    full = full.reshape(n_chan, rows_per, chan_cols)
    wts = out_proj.reshape(n_chan, chan_cols, n_chan, d_out // n_chan)
    mixed = jnp.einsum("spc,scex->epx", full, wts, preferred_element_type=jnp.float32)
    mixed = mixed.astype(jnp.bfloat16)
    res = _a2a(mixed, "chan", 3)
    return res.reshape(seq_rows, chan_cols)


def solution(mesh):
    placed = (
        P(("batch", "seq"), "chan"),
        P(("batch", "seq"), "chan"),
        P(),
        P(),
        P("seq", None),
        P(),
    )
    return jax.shard_map(
        body, mesh=mesh, in_specs=placed, out_specs=P(("batch", "seq"), "chan"), check_vma=False
    )
```

```python
import functools

import jax
import jax.numpy as jnp
from jax import lax
from jax.sharding import PartitionSpec as P
from jax.experimental import pallas as pl
from jax.experimental.pallas import tpu as pltpu

B1 = 512
CHUNKS = 4
LEAD = 2


def _a2a_kernel(axis, n, x_ref, o_ref, send_sem, recv_sem, loc_sem):
    me = lax.axis_index(axis)
    barrier = pltpu.get_barrier_semaphore()
    for t in range(1, n):
        pl.semaphore_signal(barrier, inc=1, device_id={axis: (me + t) % n},
                            device_id_type=pl.DeviceIdType.MESH)
    pl.semaphore_wait(barrier, n - 1)
    local = pltpu.make_async_copy(x_ref.at[me], o_ref.at[me], loc_sem)
    local.start()
    copies = []
    for t in range(1, n):
        dst = (me + t) % n
        c = pltpu.make_async_remote_copy(
            src_ref=x_ref.at[dst],
            dst_ref=o_ref.at[me],
            send_sem=send_sem.at[t],
            recv_sem=recv_sem.at[t],
            device_id={axis: dst},
            device_id_type=pl.DeviceIdType.MESH,
        )
        c.start()
        copies.append(c)
    local.wait()
    for c in copies:
        c.wait_send()
    for c in copies:
        c.wait_recv()


def _a2a(x, axis, cid):
    n = x.shape[0]
    return pl.pallas_call(
        functools.partial(_a2a_kernel, axis, n),
        out_shape=jax.ShapeDtypeStruct(x.shape, x.dtype),
        in_specs=[pl.BlockSpec(memory_space=pl.ANY)],
        out_specs=pl.BlockSpec(memory_space=pl.ANY),
        scratch_shapes=[
            pltpu.SemaphoreType.DMA((n,)),
            pltpu.SemaphoreType.DMA((n,)),
            pltpu.SemaphoreType.DMA,
        ],
        compiler_params=pltpu.CompilerParams(collective_id=cid, has_side_effects=True),
    )(x)


def _back_gate_send_kernel(k_chunks, m_ref, got_ref, gate_ref, full_ref, sec, recv_s, gv, hid,
                           s_send, s_recv, c_send, c_recv, g_sem):
    n_s, n_j, n_i, _ = sec.shape
    n_c = full_ref.shape[0]
    jp = n_j // n_c
    w = n_i // k_chunks
    me_s = lax.axis_index("seq")
    me_c = lax.axis_index("chan")
    mesh_ids = pl.DeviceIdType.MESH
    barrier = pltpu.get_barrier_semaphore()
    for t in range(1, n_s):
        pl.semaphore_signal(barrier, inc=1, device_id={"seq": (me_s + t) % n_s}, device_id_type=mesh_ids)
    for t in range(1, n_c):
        pl.semaphore_signal(barrier, inc=1, device_id={"chan": (me_c + t) % n_c}, device_id_type=mesh_ids)
    pl.semaphore_wait(barrier, (n_s - 1) + (n_c - 1))

    gcopy = pltpu.make_async_copy(gate_ref, gv, g_sem)
    gcopy.start()
    def issue_seq(k):
        isl = pl.ds(k * w, w)
        m = m_ref[...]
        for i in range(k * w, (k + 1) * w):
            part = jnp.dot(m, got_ref[:, i, :], preferred_element_type=jnp.float32)
            sec[:, :, i, :] = part.astype(sec.dtype).reshape(n_s, n_j, part.shape[-1])
        row = []
        for t in range(n_s):
            if t == 0:
                c = pltpu.make_async_copy(sec.at[me_s, :, isl], recv_s.at[me_s, :, isl], s_recv.at[k, 0])
            else:
                dst = (me_s + t) % n_s
                c = pltpu.make_async_remote_copy(
                    src_ref=sec.at[dst, :, isl],
                    dst_ref=recv_s.at[me_s, :, isl],
                    send_sem=s_send.at[k, t],
                    recv_sem=s_recv.at[k, t],
                    device_id={"seq": dst},
                    device_id_type=mesh_ids,
                )
            c.start()
            row.append(c)
        return row

    seq_copies = [issue_seq(k) for k in range(min(LEAD, k_chunks))]
    gcopy.wait()
    chan_copies = []
    for k in range(k_chunks):
        isl = pl.ds(k * w, w)
        for t in range(n_s):
            if t == 0:
                seq_copies[k][t].wait()
            else:
                seq_copies[k][t].wait_recv()
        for s in range(n_s):
            prod = recv_s[s, :, isl, :].astype(jnp.float32) * gv[:, pl.ds(s * n_i + k * w, w), :].astype(jnp.float32)
            hid[:, s, isl, :] = prod.astype(hid.dtype)
        for t in range(n_c):
            dst = (me_c + t) % n_c
            src_view = hid.at[pl.ds(dst * jp, jp), :, isl, :]
            dst_view = full_ref.at[me_c, :, :, isl, :]
            if t == 0:
                c = pltpu.make_async_copy(src_view, dst_view, c_recv.at[k, 0])
            else:
                c = pltpu.make_async_remote_copy(
                    src_ref=src_view,
                    dst_ref=dst_view,
                    send_sem=c_send.at[k, t],
                    recv_sem=c_recv.at[k, t],
                    device_id={"chan": dst},
                    device_id_type=mesh_ids,
                )
            c.start()
            chan_copies.append((t, c))
        if k + LEAD < k_chunks:
            seq_copies.append(issue_seq(k + LEAD))
    for row in seq_copies:
        for c in row[1:]:
            c.wait_send()
    for t, c in chan_copies:
        if t == 0:
            c.wait()
        else:
            c.wait_send()
    for t, c in chan_copies:
        if t != 0:
            c.wait_recv()


def _back_gate_send(m2, got, gate, n_s, n_c, k_chunks, cid):
    _, n_i, cols = got.shape
    n_j = got.shape[0] // n_s
    jp = n_j // n_c
    return pl.pallas_call(
        functools.partial(_back_gate_send_kernel, k_chunks),
        out_shape=jax.ShapeDtypeStruct((n_c, jp, n_s, n_i, cols), got.dtype),
        in_specs=[pl.BlockSpec(memory_space=pltpu.VMEM)] * 2 + [pl.BlockSpec(memory_space=pl.ANY)],
        out_specs=pl.BlockSpec(memory_space=pl.ANY),
        scratch_shapes=[
            pltpu.VMEM((n_s, n_j, n_i, cols), got.dtype),
            pltpu.VMEM((n_s, n_j, n_i, cols), got.dtype),
            pltpu.VMEM((n_j, n_s * n_i, cols), got.dtype),
            pltpu.VMEM((n_j, n_s, n_i, cols), got.dtype),
            pltpu.SemaphoreType.DMA((k_chunks, n_s)),
            pltpu.SemaphoreType.DMA((k_chunks, n_s)),
            pltpu.SemaphoreType.DMA((k_chunks, n_c)),
            pltpu.SemaphoreType.DMA((k_chunks, n_c)),
            pltpu.SemaphoreType.DMA,
        ],
        compiler_params=pltpu.CompilerParams(collective_id=cid, has_side_effects=True),
    )(m2, got, gate)


def _first_send_kernel(mf_ref, tok_ref, tw_ref, got_ref, stage, send_sem, recv_sem):
    n, n_b, n_i, cols = stage.shape
    me = lax.axis_index("seq")
    mesh_ids = pl.DeviceIdType.MESH
    barrier = pltpu.get_barrier_semaphore()
    for t in range(1, n):
        pl.semaphore_signal(barrier, inc=1, device_id={"seq": (me + t) % n}, device_id_type=mesh_ids)
    for d in range(n):
        rows = pl.ds(d * n_i, n_i)
        m = mf_ref[rows, :]
        for b in range(n_b):
            part = jnp.dot(m, tok_ref[b], preferred_element_type=jnp.float32)
            stage[d, b] = (part * tw_ref[rows, pl.ds(b, 1)]).astype(stage.dtype)
    pl.semaphore_wait(barrier, n - 1)
    local = pltpu.make_async_copy(stage.at[me], got_ref.at[me], recv_sem.at[0])
    local.start()
    copies = []
    for t in range(1, n):
        dst = (me + t) % n
        c = pltpu.make_async_remote_copy(
            src_ref=stage.at[dst],
            dst_ref=got_ref.at[me],
            send_sem=send_sem.at[t],
            recv_sem=recv_sem.at[t],
            device_id={"seq": dst},
            device_id_type=mesh_ids,
        )
        c.start()
        copies.append(c)
    local.wait()
    for c in copies:
        c.wait_send()
    for c in copies:
        c.wait_recv()


def _first_send(mix_first, blocked, tw_t, n, cid):
    n_b, _, cols = blocked.shape
    n_i = mix_first.shape[0] // n
    return pl.pallas_call(
        _first_send_kernel,
        out_shape=jax.ShapeDtypeStruct((n, n_b, n_i, cols), blocked.dtype),
        in_specs=[pl.BlockSpec(memory_space=pltpu.VMEM)] * 3,
        out_specs=pl.BlockSpec(memory_space=pl.ANY),
        scratch_shapes=[
            pltpu.VMEM((n, n_b, n_i, cols), blocked.dtype),
            pltpu.SemaphoreType.DMA((n,)),
            pltpu.SemaphoreType.DMA((n,)),
        ],
        compiler_params=pltpu.CompilerParams(collective_id=cid, has_side_effects=True),
    )(mix_first, blocked, tw_t)


def body(tokens, gate_in, mix_first, mix_second, twiddle, out_proj):
    seq_rows, chan_cols = tokens.shape
    n_seq = lax.axis_size("seq")
    n_chan = lax.axis_size("chan")
    blocks_here = seq_rows // B1
    per_dev_i = B1 // n_seq
    d_out = out_proj.shape[1]

    blocked = tokens.reshape(blocks_here, B1, chan_cols)
    got = _first_send(mix_first, blocked, twiddle.T, n_seq, 0)
    got = got.reshape(n_seq * blocks_here, per_dev_i, chan_cols)
    gate = gate_in.reshape(blocks_here, B1, chan_cols)
    full = _back_gate_send(mix_second, got, gate, n_seq, n_chan, CHUNKS, 1)
    rows_per = seq_rows // n_chan
    full = full.reshape(n_chan, rows_per, chan_cols)
    wts = out_proj.reshape(n_chan, chan_cols, n_chan, d_out // n_chan)
    mixed = jnp.einsum("spc,scex->epx", full, wts, preferred_element_type=jnp.float32)
    mixed = mixed.astype(jnp.bfloat16)
    res = _a2a(mixed, "chan", 3)
    return res.reshape(seq_rows, chan_cols)


def solution(mesh):
    placed = (
        P(("batch", "seq"), "chan"),
        P(("batch", "seq"), "chan"),
        P(),
        P(),
        P("seq", None),
        P(),
    )
    return jax.shard_map(
        body, mesh=mesh, in_specs=placed, out_specs=P(("batch", "seq"), "chan"), check_vma=False
    )
```

```python
import functools

import jax
import jax.numpy as jnp
from jax import lax
from jax.sharding import PartitionSpec as P
from jax.experimental import pallas as pl
from jax.experimental.pallas import tpu as pltpu

B1 = 512
CHUNKS = 4
LEAD = 2


def _a2a_kernel(axis, n, x_ref, o_ref, send_sem, recv_sem, loc_sem):
    me = lax.axis_index(axis)
    barrier = pltpu.get_barrier_semaphore()
    for t in range(1, n):
        pl.semaphore_signal(barrier, inc=1, device_id={axis: (me + t) % n},
                            device_id_type=pl.DeviceIdType.MESH)
    pl.semaphore_wait(barrier, n - 1)
    local = pltpu.make_async_copy(x_ref.at[me], o_ref.at[me], loc_sem)
    local.start()
    copies = []
    for t in range(1, n):
        dst = (me + t) % n
        c = pltpu.make_async_remote_copy(
            src_ref=x_ref.at[dst],
            dst_ref=o_ref.at[me],
            send_sem=send_sem.at[t],
            recv_sem=recv_sem.at[t],
            device_id={axis: dst},
            device_id_type=pl.DeviceIdType.MESH,
        )
        c.start()
        copies.append(c)
    local.wait()
    for c in copies:
        c.wait_send()
    for c in copies:
        c.wait_recv()


def _a2a(x, axis, cid):
    n = x.shape[0]
    return pl.pallas_call(
        functools.partial(_a2a_kernel, axis, n),
        out_shape=jax.ShapeDtypeStruct(x.shape, x.dtype),
        in_specs=[pl.BlockSpec(memory_space=pl.ANY)],
        out_specs=pl.BlockSpec(memory_space=pl.ANY),
        scratch_shapes=[
            pltpu.SemaphoreType.DMA((n,)),
            pltpu.SemaphoreType.DMA((n,)),
            pltpu.SemaphoreType.DMA,
        ],
        compiler_params=pltpu.CompilerParams(collective_id=cid, has_side_effects=True),
    )(x)


def _back_gate_send_kernel(k_chunks, m_ref, got_ref, gate_ref, full_ref, sec, recv_s, hid,
                           s_send, s_recv, c_send, c_recv):
    n_s, n_j, n_i, _ = sec.shape
    n_c = full_ref.shape[0]
    jp = n_j // n_c
    w = n_i // k_chunks
    me_s = lax.axis_index("seq")
    me_c = lax.axis_index("chan")
    mesh_ids = pl.DeviceIdType.MESH
    barrier = pltpu.get_barrier_semaphore()
    for t in range(1, n_s):
        pl.semaphore_signal(barrier, inc=1, device_id={"seq": (me_s + t) % n_s}, device_id_type=mesh_ids)
    for t in range(1, n_c):
        pl.semaphore_signal(barrier, inc=1, device_id={"chan": (me_c + t) % n_c}, device_id_type=mesh_ids)
    pl.semaphore_wait(barrier, (n_s - 1) + (n_c - 1))

    def issue_seq(k):
        isl = pl.ds(k * w, w)
        m = m_ref[...]
        for i in range(k * w, (k + 1) * w):
            part = jnp.dot(m, got_ref[:, i, :], preferred_element_type=jnp.float32)
            sec[:, :, i, :] = part.astype(sec.dtype).reshape(n_s, n_j, part.shape[-1])
        row = []
        for t in range(n_s):
            if t == 0:
                c = pltpu.make_async_copy(sec.at[me_s, :, isl], recv_s.at[me_s, :, isl], s_recv.at[k, 0])
            else:
                dst = (me_s + t) % n_s
                c = pltpu.make_async_remote_copy(
                    src_ref=sec.at[dst, :, isl],
                    dst_ref=recv_s.at[me_s, :, isl],
                    send_sem=s_send.at[k, t],
                    recv_sem=s_recv.at[k, t],
                    device_id={"seq": dst},
                    device_id_type=mesh_ids,
                )
            c.start()
            row.append(c)
        return row

    seq_copies = [issue_seq(k) for k in range(min(LEAD, k_chunks))]
    chan_copies = []
    for k in range(k_chunks):
        isl = pl.ds(k * w, w)
        for t in range(n_s):
            if t == 0:
                seq_copies[k][t].wait()
            else:
                seq_copies[k][t].wait_recv()
        for s in range(n_s):
            prod = recv_s[s, :, isl, :].astype(jnp.float32) * gate_ref[:, pl.ds(s * n_i + k * w, w), :].astype(jnp.float32)
            hid[:, s, isl, :] = prod.astype(hid.dtype)
        for t in range(n_c):
            dst = (me_c + t) % n_c
            src_view = hid.at[pl.ds(dst * jp, jp), :, isl, :]
            dst_view = full_ref.at[me_c, :, :, isl, :]
            if t == 0:
                c = pltpu.make_async_copy(src_view, dst_view, c_recv.at[k, 0])
            else:
                c = pltpu.make_async_remote_copy(
                    src_ref=src_view,
                    dst_ref=dst_view,
                    send_sem=c_send.at[k, t],
                    recv_sem=c_recv.at[k, t],
                    device_id={"chan": dst},
                    device_id_type=mesh_ids,
                )
            c.start()
            chan_copies.append((t, c))
        if k + LEAD < k_chunks:
            seq_copies.append(issue_seq(k + LEAD))
    for row in seq_copies:
        for c in row[1:]:
            c.wait_send()
    for t, c in chan_copies:
        if t == 0:
            c.wait()
        else:
            c.wait_send()
    for t, c in chan_copies:
        if t != 0:
            c.wait_recv()


def _back_gate_send(m2, got, gate, n_s, n_c, k_chunks, cid):
    _, n_i, cols = got.shape
    n_j = got.shape[0] // n_s
    jp = n_j // n_c
    return pl.pallas_call(
        functools.partial(_back_gate_send_kernel, k_chunks),
        out_shape=jax.ShapeDtypeStruct((n_c, jp, n_s, n_i, cols), got.dtype),
        in_specs=[pl.BlockSpec(memory_space=pltpu.VMEM)] * 3,
        out_specs=pl.BlockSpec(memory_space=pl.ANY),
        scratch_shapes=[
            pltpu.VMEM((n_s, n_j, n_i, cols), got.dtype),
            pltpu.VMEM((n_s, n_j, n_i, cols), got.dtype),
            pltpu.VMEM((n_j, n_s, n_i, cols), got.dtype),
            pltpu.SemaphoreType.DMA((k_chunks, n_s)),
            pltpu.SemaphoreType.DMA((k_chunks, n_s)),
            pltpu.SemaphoreType.DMA((k_chunks, n_c)),
            pltpu.SemaphoreType.DMA((k_chunks, n_c)),
        ],
        compiler_params=pltpu.CompilerParams(collective_id=cid, has_side_effects=True),
    )(m2, got, gate)


def body(tokens, gate_in, mix_first, mix_second, twiddle, out_proj):
    seq_rows, chan_cols = tokens.shape
    n_seq = lax.axis_size("seq")
    n_chan = lax.axis_size("chan")
    blocks_here = seq_rows // B1
    per_dev_i = B1 // n_seq
    d_out = out_proj.shape[1]

    blocked = tokens.reshape(blocks_here, B1, chan_cols)
    mf = mix_first.reshape(n_seq, per_dev_i, B1)
    tw = twiddle.reshape(blocks_here, n_seq, per_dev_i).transpose(1, 0, 2)
    first = jnp.einsum("dik,bkc->dbic", mf, blocked, preferred_element_type=jnp.float32)
    first = (first * tw[:, :, :, None]).astype(jnp.bfloat16)
    got = _a2a(first, "seq", 0)
    got = got.reshape(n_seq * blocks_here, per_dev_i, chan_cols)
    gate = gate_in.reshape(blocks_here, B1, chan_cols)
    full = _back_gate_send(mix_second, got, gate, n_seq, n_chan, CHUNKS, 1)
    rows_per = seq_rows // n_chan
    full = full.reshape(n_chan, rows_per, chan_cols)
    wts = out_proj.reshape(n_chan, chan_cols, n_chan, d_out // n_chan)
    mixed = jnp.einsum("spc,scex->epx", full, wts, preferred_element_type=jnp.float32)
    mixed = mixed.astype(jnp.bfloat16)
    res = _a2a(mixed, "chan", 3)
    return res.reshape(seq_rows, chan_cols)


def solution(mesh):
    placed = (
        P(("batch", "seq"), "chan"),
        P(("batch", "seq"), "chan"),
        P(),
        P(),
        P("seq", None),
        P(),
    )
    return jax.shard_map(
        body, mesh=mesh, in_specs=placed, out_specs=P(("batch", "seq"), "chan"), check_vma=False
    )
```

```python
import functools

import jax
import jax.numpy as jnp
from jax import lax
from jax.sharding import PartitionSpec as P
from jax.experimental import pallas as pl
from jax.experimental.pallas import tpu as pltpu

B1 = 512
CHUNKS = 4
LEAD = 2


def _a2a_kernel(axis, n, x_ref, o_ref, send_sem, recv_sem, loc_sem):
    me = lax.axis_index(axis)
    barrier = pltpu.get_barrier_semaphore()
    for t in range(1, n):
        pl.semaphore_signal(barrier, inc=1, device_id={axis: (me + t) % n},
                            device_id_type=pl.DeviceIdType.MESH)
    pl.semaphore_wait(barrier, n - 1)
    local = pltpu.make_async_copy(x_ref.at[me], o_ref.at[me], loc_sem)
    local.start()
    copies = []
    for t in range(1, n):
        dst = (me + t) % n
        c = pltpu.make_async_remote_copy(
            src_ref=x_ref.at[dst],
            dst_ref=o_ref.at[me],
            send_sem=send_sem.at[t],
            recv_sem=recv_sem.at[t],
            device_id={axis: dst},
            device_id_type=pl.DeviceIdType.MESH,
        )
        c.start()
        copies.append(c)
    local.wait()
    for c in copies:
        c.wait_send()
    for c in copies:
        c.wait_recv()


def _a2a(x, axis, cid):
    n = x.shape[0]
    return pl.pallas_call(
        functools.partial(_a2a_kernel, axis, n),
        out_shape=jax.ShapeDtypeStruct(x.shape, x.dtype),
        in_specs=[pl.BlockSpec(memory_space=pl.ANY)],
        out_specs=pl.BlockSpec(memory_space=pl.ANY),
        scratch_shapes=[
            pltpu.SemaphoreType.DMA((n,)),
            pltpu.SemaphoreType.DMA((n,)),
            pltpu.SemaphoreType.DMA,
        ],
        compiler_params=pltpu.CompilerParams(collective_id=cid, has_side_effects=True),
    )(x)


def _back_gate_send_kernel(k_chunks, m_ref, got_ref, gate_ref, full_ref, sec, recv_s, gv, hid,
                           s_send, s_recv, c_send, c_recv, g_sem):
    n_s, n_j, n_i, _ = sec.shape
    n_c = full_ref.shape[0]
    jp = n_j // n_c
    w = n_i // k_chunks
    me_s = lax.axis_index("seq")
    me_c = lax.axis_index("chan")
    mesh_ids = pl.DeviceIdType.MESH
    barrier = pltpu.get_barrier_semaphore()
    for t in range(1, n_s):
        pl.semaphore_signal(barrier, inc=1, device_id={"seq": (me_s + t) % n_s}, device_id_type=mesh_ids)
    for t in range(1, n_c):
        pl.semaphore_signal(barrier, inc=1, device_id={"chan": (me_c + t) % n_c}, device_id_type=mesh_ids)
    pl.semaphore_wait(barrier, (n_s - 1) + (n_c - 1))

    gcopy = pltpu.make_async_copy(gate_ref, gv, g_sem)
    gcopy.start()
    def issue_seq(k):
        isl = pl.ds(k * w, w)
        m = m_ref[...]
        for i in range(k * w, (k + 1) * w):
            part = jnp.dot(m, got_ref[:, i, :], preferred_element_type=jnp.float32)
            sec[:, :, i, :] = part.astype(sec.dtype).reshape(n_s, n_j, part.shape[-1])
        row = []
        for t in range(n_s):
            if t == 0:
                c = pltpu.make_async_copy(sec.at[me_s, :, isl], recv_s.at[me_s, :, isl], s_recv.at[k, 0])
            else:
                dst = (me_s + t) % n_s
                c = pltpu.make_async_remote_copy(
                    src_ref=sec.at[dst, :, isl],
                    dst_ref=recv_s.at[me_s, :, isl],
                    send_sem=s_send.at[k, t],
                    recv_sem=s_recv.at[k, t],
                    device_id={"seq": dst},
                    device_id_type=mesh_ids,
                )
            c.start()
            row.append(c)
        return row

    seq_copies = [issue_seq(k) for k in range(min(LEAD, k_chunks))]
    gcopy.wait()
    chan_copies = []
    for k in range(k_chunks):
        isl = pl.ds(k * w, w)
        for t in range(n_s):
            if t == 0:
                seq_copies[k][t].wait()
            else:
                seq_copies[k][t].wait_recv()
        for s in range(n_s):
            prod = recv_s[s, :, isl, :].astype(jnp.float32) * gv[:, pl.ds(s * n_i + k * w, w), :].astype(jnp.float32)
            hid[:, s, isl, :] = prod.astype(hid.dtype)
        for t in range(n_c):
            dst = (me_c + t) % n_c
            src_view = hid.at[pl.ds(dst * jp, jp), :, isl, :]
            dst_view = full_ref.at[me_c, :, :, isl, :]
            if t == 0:
                c = pltpu.make_async_copy(src_view, dst_view, c_recv.at[k, 0])
            else:
                c = pltpu.make_async_remote_copy(
                    src_ref=src_view,
                    dst_ref=dst_view,
                    send_sem=c_send.at[k, t],
                    recv_sem=c_recv.at[k, t],
                    device_id={"chan": dst},
                    device_id_type=mesh_ids,
                )
            c.start()
            chan_copies.append((t, c))
        if k + LEAD < k_chunks:
            seq_copies.append(issue_seq(k + LEAD))
    for row in seq_copies:
        for c in row[1:]:
            c.wait_send()
    for t, c in chan_copies:
        if t == 0:
            c.wait()
        else:
            c.wait_send()
    for t, c in chan_copies:
        if t != 0:
            c.wait_recv()


def _back_gate_send(m2, got, gate, n_s, n_c, k_chunks, cid):
    _, n_i, cols = got.shape
    n_j = got.shape[0] // n_s
    jp = n_j // n_c
    return pl.pallas_call(
        functools.partial(_back_gate_send_kernel, k_chunks),
        out_shape=jax.ShapeDtypeStruct((n_c, jp, n_s, n_i, cols), got.dtype),
        in_specs=[pl.BlockSpec(memory_space=pltpu.VMEM)] * 2 + [pl.BlockSpec(memory_space=pl.ANY)],
        out_specs=pl.BlockSpec(memory_space=pl.ANY),
        scratch_shapes=[
            pltpu.VMEM((n_s, n_j, n_i, cols), got.dtype),
            pltpu.VMEM((n_s, n_j, n_i, cols), got.dtype),
            pltpu.VMEM((n_j, n_s * n_i, cols), got.dtype),
            pltpu.VMEM((n_j, n_s, n_i, cols), got.dtype),
            pltpu.SemaphoreType.DMA((k_chunks, n_s)),
            pltpu.SemaphoreType.DMA((k_chunks, n_s)),
            pltpu.SemaphoreType.DMA((k_chunks, n_c)),
            pltpu.SemaphoreType.DMA((k_chunks, n_c)),
            pltpu.SemaphoreType.DMA,
        ],
        compiler_params=pltpu.CompilerParams(collective_id=cid, has_side_effects=True),
    )(m2, got, gate)


def body(tokens, gate_in, mix_first, mix_second, twiddle, out_proj):
    seq_rows, chan_cols = tokens.shape
    n_seq = lax.axis_size("seq")
    n_chan = lax.axis_size("chan")
    blocks_here = seq_rows // B1
    per_dev_i = B1 // n_seq
    d_out = out_proj.shape[1]

    blocked = tokens.reshape(blocks_here, B1, chan_cols)
    mf = mix_first.reshape(n_seq, per_dev_i, B1)
    tw = twiddle.reshape(blocks_here, n_seq, per_dev_i).transpose(1, 0, 2)
    first = jnp.einsum("dik,bkc->dbic", mf, blocked, preferred_element_type=jnp.float32)
    first = (first * tw[:, :, :, None]).astype(jnp.bfloat16)
    got = _a2a(first, "seq", 0)
    got = got.reshape(n_seq * blocks_here, per_dev_i, chan_cols)
    gate = gate_in.reshape(blocks_here, B1, chan_cols)
    full = _back_gate_send(mix_second, got, gate, n_seq, n_chan, CHUNKS, 1)
    rows_per = seq_rows // n_chan
    full = full.reshape(n_chan, rows_per, chan_cols)
    wts = out_proj.reshape(n_chan, chan_cols, n_chan, d_out // n_chan)
    mixed = jnp.einsum("spc,scex->epx", full, wts, preferred_element_type=jnp.float32)
    mixed = mixed.astype(jnp.bfloat16)
    res = lax.all_to_all(mixed, "chan", split_axis=0, concat_axis=0, tiled=False)
    return res.reshape(seq_rows, chan_cols)


def solution(mesh):
    placed = (
        P(("batch", "seq"), "chan"),
        P(("batch", "seq"), "chan"),
        P(),
        P(),
        P("seq", None),
        P(),
    )
    return jax.shard_map(
        body, mesh=mesh, in_specs=placed, out_specs=P(("batch", "seq"), "chan"), check_vma=False
    )
```

```python
import functools

import jax
import jax.numpy as jnp
from jax import lax
from jax.sharding import PartitionSpec as P
from jax.experimental import pallas as pl
from jax.experimental.pallas import tpu as pltpu

B1 = 512
CHUNKS = 4
LEAD = 2


def _a2a_kernel(axis, n, x_ref, o_ref, send_sem, recv_sem, loc_sem):
    me = lax.axis_index(axis)
    barrier = pltpu.get_barrier_semaphore()
    for t in range(1, n):
        pl.semaphore_signal(barrier, inc=1, device_id={axis: (me + t) % n},
                            device_id_type=pl.DeviceIdType.MESH)
    pl.semaphore_wait(barrier, n - 1)
    local = pltpu.make_async_copy(x_ref.at[me], o_ref.at[me], loc_sem)
    local.start()
    copies = []
    for t in range(1, n):
        dst = (me + t) % n
        c = pltpu.make_async_remote_copy(
            src_ref=x_ref.at[dst],
            dst_ref=o_ref.at[me],
            send_sem=send_sem.at[t],
            recv_sem=recv_sem.at[t],
            device_id={axis: dst},
            device_id_type=pl.DeviceIdType.MESH,
        )
        c.start()
        copies.append(c)
    local.wait()
    for c in copies:
        c.wait_send()
    for c in copies:
        c.wait_recv()


def _a2a(x, axis, cid):
    n = x.shape[0]
    return pl.pallas_call(
        functools.partial(_a2a_kernel, axis, n),
        out_shape=jax.ShapeDtypeStruct(x.shape, x.dtype),
        in_specs=[pl.BlockSpec(memory_space=pl.ANY)],
        out_specs=pl.BlockSpec(memory_space=pl.ANY),
        scratch_shapes=[
            pltpu.SemaphoreType.DMA((n,)),
            pltpu.SemaphoreType.DMA((n,)),
            pltpu.SemaphoreType.DMA,
        ],
        compiler_params=pltpu.CompilerParams(collective_id=cid, has_side_effects=True),
    )(x)


def _back_gate_send_kernel(k_chunks, m_ref, got_ref, gate_ref, full_ref, sec, recv_s, gv, hid,
                           s_send, s_recv, c_send, c_recv, g_sem):
    n_s, n_j, n_i, _ = sec.shape
    n_c = full_ref.shape[0]
    jp = n_j // n_c
    w = n_i // k_chunks
    me_s = lax.axis_index("seq")
    me_c = lax.axis_index("chan")
    mesh_ids = pl.DeviceIdType.MESH
    barrier = pltpu.get_barrier_semaphore()
    for t in range(1, n_s):
        pl.semaphore_signal(barrier, inc=1, device_id={"seq": (me_s + t) % n_s}, device_id_type=mesh_ids)
    for t in range(1, n_c):
        pl.semaphore_signal(barrier, inc=1, device_id={"chan": (me_c + t) % n_c}, device_id_type=mesh_ids)

    gcopy = pltpu.make_async_copy(gate_ref, gv, g_sem)
    gcopy.start()

    def compute_sec(k):
        m = m_ref[...]
        for i in range(k * w, (k + 1) * w):
            part = jnp.dot(m, got_ref[:, i, :], preferred_element_type=jnp.float32)
            sec[:, :, i, :] = part.astype(sec.dtype).reshape(n_s, n_j, part.shape[-1])

    def issue_seq(k, computed=False):
        isl = pl.ds(k * w, w)
        if not computed:
            compute_sec(k)
        row = []
        for t in range(n_s):
            if t == 0:
                c = pltpu.make_async_copy(sec.at[me_s, :, isl], recv_s.at[me_s, :, isl], s_recv.at[k, 0])
            else:
                dst = (me_s + t) % n_s
                c = pltpu.make_async_remote_copy(
                    src_ref=sec.at[dst, :, isl],
                    dst_ref=recv_s.at[me_s, :, isl],
                    send_sem=s_send.at[k, t],
                    recv_sem=s_recv.at[k, t],
                    device_id={"seq": dst},
                    device_id_type=mesh_ids,
                )
            c.start()
            row.append(c)
        return row

    for k in range(min(LEAD, k_chunks)):
        compute_sec(k)
    pl.semaphore_wait(barrier, (n_s - 1) + (n_c - 1))
    seq_copies = [issue_seq(k, computed=True) for k in range(min(LEAD, k_chunks))]
    gcopy.wait()
    chan_copies = []
    for k in range(k_chunks):
        isl = pl.ds(k * w, w)
        for t in range(n_s):
            if t == 0:
                seq_copies[k][t].wait()
            else:
                seq_copies[k][t].wait_recv()
        for s in range(n_s):
            prod = recv_s[s, :, isl, :].astype(jnp.float32) * gv[:, pl.ds(s * n_i + k * w, w), :].astype(jnp.float32)
            hid[:, s, isl, :] = prod.astype(hid.dtype)
        for t in range(n_c):
            dst = (me_c + t) % n_c
            src_view = hid.at[pl.ds(dst * jp, jp), :, isl, :]
            dst_view = full_ref.at[me_c, :, :, isl, :]
            if t == 0:
                c = pltpu.make_async_copy(src_view, dst_view, c_recv.at[k, 0])
            else:
                c = pltpu.make_async_remote_copy(
                    src_ref=src_view,
                    dst_ref=dst_view,
                    send_sem=c_send.at[k, t],
                    recv_sem=c_recv.at[k, t],
                    device_id={"chan": dst},
                    device_id_type=mesh_ids,
                )
            c.start()
            chan_copies.append((t, c))
        if k + LEAD < k_chunks:
            seq_copies.append(issue_seq(k + LEAD))
    for row in seq_copies:
        for c in row[1:]:
            c.wait_send()
    for t, c in chan_copies:
        if t == 0:
            c.wait()
        else:
            c.wait_send()
    for t, c in chan_copies:
        if t != 0:
            c.wait_recv()


def _back_gate_send(m2, got, gate, n_s, n_c, k_chunks, cid):
    _, n_i, cols = got.shape
    n_j = got.shape[0] // n_s
    jp = n_j // n_c
    return pl.pallas_call(
        functools.partial(_back_gate_send_kernel, k_chunks),
        out_shape=jax.ShapeDtypeStruct((n_c, jp, n_s, n_i, cols), got.dtype),
        in_specs=[pl.BlockSpec(memory_space=pltpu.VMEM)] * 2 + [pl.BlockSpec(memory_space=pl.ANY)],
        out_specs=pl.BlockSpec(memory_space=pl.ANY),
        scratch_shapes=[
            pltpu.VMEM((n_s, n_j, n_i, cols), got.dtype),
            pltpu.VMEM((n_s, n_j, n_i, cols), got.dtype),
            pltpu.VMEM((n_j, n_s * n_i, cols), got.dtype),
            pltpu.VMEM((n_j, n_s, n_i, cols), got.dtype),
            pltpu.SemaphoreType.DMA((k_chunks, n_s)),
            pltpu.SemaphoreType.DMA((k_chunks, n_s)),
            pltpu.SemaphoreType.DMA((k_chunks, n_c)),
            pltpu.SemaphoreType.DMA((k_chunks, n_c)),
            pltpu.SemaphoreType.DMA,
        ],
        compiler_params=pltpu.CompilerParams(collective_id=cid, has_side_effects=True),
    )(m2, got, gate)


def body(tokens, gate_in, mix_first, mix_second, twiddle, out_proj):
    seq_rows, chan_cols = tokens.shape
    n_seq = lax.axis_size("seq")
    n_chan = lax.axis_size("chan")
    blocks_here = seq_rows // B1
    per_dev_i = B1 // n_seq
    d_out = out_proj.shape[1]

    blocked = tokens.reshape(blocks_here, B1, chan_cols)
    mf = mix_first.reshape(n_seq, per_dev_i, B1)
    tw = twiddle.reshape(blocks_here, n_seq, per_dev_i).transpose(1, 0, 2)
    first = jnp.einsum("dik,bkc->dbic", mf, blocked, preferred_element_type=jnp.float32)
    first = (first * tw[:, :, :, None]).astype(jnp.bfloat16)
    got = _a2a(first, "seq", 0)
    got = got.reshape(n_seq * blocks_here, per_dev_i, chan_cols)
    gate = gate_in.reshape(blocks_here, B1, chan_cols)
    full = _back_gate_send(mix_second, got, gate, n_seq, n_chan, CHUNKS, 1)
    rows_per = seq_rows // n_chan
    full = full.reshape(n_chan, rows_per, chan_cols)
    wts = out_proj.reshape(n_chan, chan_cols, n_chan, d_out // n_chan)
    mixed = jnp.einsum("spc,scex->epx", full, wts, preferred_element_type=jnp.float32)
    mixed = mixed.astype(jnp.bfloat16)
    res = _a2a(mixed, "chan", 3)
    return res.reshape(seq_rows, chan_cols)


def solution(mesh):
    placed = (
        P(("batch", "seq"), "chan"),
        P(("batch", "seq"), "chan"),
        P(),
        P(),
        P("seq", None),
        P(),
    )
    return jax.shard_map(
        body, mesh=mesh, in_specs=placed, out_specs=P(("batch", "seq"), "chan"), check_vma=False
    )
```

```python
import functools

import jax
import jax.numpy as jnp
from jax import lax
from jax.sharding import PartitionSpec as P
from jax.experimental import pallas as pl
from jax.experimental.pallas import tpu as pltpu

B1 = 512
CHUNKS = 4
LEAD = 2


def _a2a_kernel(axis, n, x_ref, o_ref, send_sem, recv_sem, loc_sem):
    me = lax.axis_index(axis)
    barrier = pltpu.get_barrier_semaphore()
    for t in range(1, n):
        pl.semaphore_signal(barrier, inc=1, device_id={axis: (me + t) % n},
                            device_id_type=pl.DeviceIdType.MESH)
    pl.semaphore_wait(barrier, n - 1)
    local = pltpu.make_async_copy(x_ref.at[me], o_ref.at[me], loc_sem)
    local.start()
    copies = []
    for t in range(1, n):
        dst = (me + t) % n
        c = pltpu.make_async_remote_copy(
            src_ref=x_ref.at[dst],
            dst_ref=o_ref.at[me],
            send_sem=send_sem.at[t],
            recv_sem=recv_sem.at[t],
            device_id={axis: dst},
            device_id_type=pl.DeviceIdType.MESH,
        )
        c.start()
        copies.append(c)
    local.wait()
    for c in copies:
        c.wait_send()
    for c in copies:
        c.wait_recv()


def _a2a(x, axis, cid):
    n = x.shape[0]
    return pl.pallas_call(
        functools.partial(_a2a_kernel, axis, n),
        out_shape=jax.ShapeDtypeStruct(x.shape, x.dtype),
        in_specs=[pl.BlockSpec(memory_space=pl.ANY)],
        out_specs=pl.BlockSpec(memory_space=pl.ANY),
        scratch_shapes=[
            pltpu.SemaphoreType.DMA((n,)),
            pltpu.SemaphoreType.DMA((n,)),
            pltpu.SemaphoreType.DMA,
        ],
        compiler_params=pltpu.CompilerParams(collective_id=cid, has_side_effects=True),
    )(x)


def _back_gate_send_kernel(k_chunks, m_ref, got_ref, gate_ref, full_ref, sec, recv_s, gv, hid,
                           s_send, s_recv, c_send, c_recv, g_sem):
    n_s, n_j, n_i, _ = sec.shape
    n_c = full_ref.shape[0]
    jp = n_j // n_c
    w = n_i // k_chunks
    me_s = lax.axis_index("seq")
    me_c = lax.axis_index("chan")
    mesh_ids = pl.DeviceIdType.MESH
    barrier = pltpu.get_barrier_semaphore()
    for t in range(1, n_s):
        pl.semaphore_signal(barrier, inc=1, device_id={"seq": (me_s + t) % n_s}, device_id_type=mesh_ids)
    for t in range(1, n_c):
        pl.semaphore_signal(barrier, inc=1, device_id={"chan": (me_c + t) % n_c}, device_id_type=mesh_ids)

    gcopy = pltpu.make_async_copy(gate_ref, gv, g_sem)
    gcopy.start()

    def compute_sec(k):
        m = m_ref[...]
        for i in range(k * w, (k + 1) * w):
            part = jnp.dot(m, got_ref[:, i, :], preferred_element_type=jnp.float32)
            sec[:, :, i, :] = part.astype(sec.dtype).reshape(n_s, n_j, part.shape[-1])

    def issue_seq(k, computed=False):
        isl = pl.ds(k * w, w)
        if not computed:
            compute_sec(k)
        row = []
        for t in range(n_s):
            if t == 0:
                c = pltpu.make_async_copy(sec.at[me_s, :, isl], recv_s.at[me_s, :, isl], s_recv.at[k, 0])
            else:
                dst = (me_s + t) % n_s
                c = pltpu.make_async_remote_copy(
                    src_ref=sec.at[dst, :, isl],
                    dst_ref=recv_s.at[me_s, :, isl],
                    send_sem=s_send.at[k, t],
                    recv_sem=s_recv.at[k, t],
                    device_id={"seq": dst},
                    device_id_type=mesh_ids,
                )
            c.start()
            row.append(c)
        return row

    for k in range(k_chunks):
        compute_sec(k)
    pl.semaphore_wait(barrier, (n_s - 1) + (n_c - 1))
    seq_copies = [issue_seq(k, computed=True) for k in range(min(LEAD, k_chunks))]
    gcopy.wait()
    chan_copies = []
    for k in range(k_chunks):
        isl = pl.ds(k * w, w)
        for t in range(n_s):
            if t == 0:
                seq_copies[k][t].wait()
            else:
                seq_copies[k][t].wait_recv()
        for s in range(n_s):
            prod = recv_s[s, :, isl, :].astype(jnp.float32) * gv[:, pl.ds(s * n_i + k * w, w), :].astype(jnp.float32)
            hid[:, s, isl, :] = prod.astype(hid.dtype)
        for t in range(n_c):
            dst = (me_c + t) % n_c
            src_view = hid.at[pl.ds(dst * jp, jp), :, isl, :]
            dst_view = full_ref.at[me_c, :, :, isl, :]
            if t == 0:
                c = pltpu.make_async_copy(src_view, dst_view, c_recv.at[k, 0])
            else:
                c = pltpu.make_async_remote_copy(
                    src_ref=src_view,
                    dst_ref=dst_view,
                    send_sem=c_send.at[k, t],
                    recv_sem=c_recv.at[k, t],
                    device_id={"chan": dst},
                    device_id_type=mesh_ids,
                )
            c.start()
            chan_copies.append((t, c))
        if k + LEAD < k_chunks:
            seq_copies.append(issue_seq(k + LEAD, computed=True))
    for row in seq_copies:
        for c in row[1:]:
            c.wait_send()
    for t, c in chan_copies:
        if t == 0:
            c.wait()
        else:
            c.wait_send()
    for t, c in chan_copies:
        if t != 0:
            c.wait_recv()


def _back_gate_send(m2, got, gate, n_s, n_c, k_chunks, cid):
    _, n_i, cols = got.shape
    n_j = got.shape[0] // n_s
    jp = n_j // n_c
    return pl.pallas_call(
        functools.partial(_back_gate_send_kernel, k_chunks),
        out_shape=jax.ShapeDtypeStruct((n_c, jp, n_s, n_i, cols), got.dtype),
        in_specs=[pl.BlockSpec(memory_space=pltpu.VMEM)] * 2 + [pl.BlockSpec(memory_space=pl.ANY)],
        out_specs=pl.BlockSpec(memory_space=pl.ANY),
        scratch_shapes=[
            pltpu.VMEM((n_s, n_j, n_i, cols), got.dtype),
            pltpu.VMEM((n_s, n_j, n_i, cols), got.dtype),
            pltpu.VMEM((n_j, n_s * n_i, cols), got.dtype),
            pltpu.VMEM((n_j, n_s, n_i, cols), got.dtype),
            pltpu.SemaphoreType.DMA((k_chunks, n_s)),
            pltpu.SemaphoreType.DMA((k_chunks, n_s)),
            pltpu.SemaphoreType.DMA((k_chunks, n_c)),
            pltpu.SemaphoreType.DMA((k_chunks, n_c)),
            pltpu.SemaphoreType.DMA,
        ],
        compiler_params=pltpu.CompilerParams(collective_id=cid, has_side_effects=True),
    )(m2, got, gate)


def body(tokens, gate_in, mix_first, mix_second, twiddle, out_proj):
    seq_rows, chan_cols = tokens.shape
    n_seq = lax.axis_size("seq")
    n_chan = lax.axis_size("chan")
    blocks_here = seq_rows // B1
    per_dev_i = B1 // n_seq
    d_out = out_proj.shape[1]

    blocked = tokens.reshape(blocks_here, B1, chan_cols)
    mf = mix_first.reshape(n_seq, per_dev_i, B1)
    tw = twiddle.reshape(blocks_here, n_seq, per_dev_i).transpose(1, 0, 2)
    first = jnp.einsum("dik,bkc->dbic", mf, blocked, preferred_element_type=jnp.float32)
    first = (first * tw[:, :, :, None]).astype(jnp.bfloat16)
    got = _a2a(first, "seq", 0)
    got = got.reshape(n_seq * blocks_here, per_dev_i, chan_cols)
    gate = gate_in.reshape(blocks_here, B1, chan_cols)
    full = _back_gate_send(mix_second, got, gate, n_seq, n_chan, CHUNKS, 1)
    rows_per = seq_rows // n_chan
    full = full.reshape(n_chan, rows_per, chan_cols)
    wts = out_proj.reshape(n_chan, chan_cols, n_chan, d_out // n_chan)
    mixed = jnp.einsum("spc,scex->epx", full, wts, preferred_element_type=jnp.float32)
    mixed = mixed.astype(jnp.bfloat16)
    res = _a2a(mixed, "chan", 3)
    return res.reshape(seq_rows, chan_cols)


def solution(mesh):
    placed = (
        P(("batch", "seq"), "chan"),
        P(("batch", "seq"), "chan"),
        P(),
        P(),
        P("seq", None),
        P(),
    )
    return jax.shard_map(
        body, mesh=mesh, in_specs=placed, out_specs=P(("batch", "seq"), "chan"), check_vma=False
    )
```

```python
import functools

import jax
import jax.numpy as jnp
from jax import lax
from jax.sharding import PartitionSpec as P
from jax.experimental import pallas as pl
from jax.experimental.pallas import tpu as pltpu

B1 = 512
CHUNKS = 4
LEAD = 2


def _a2a_kernel(axis, n, x_ref, o_ref, send_sem, recv_sem, loc_sem):
    me = lax.axis_index(axis)
    barrier = pltpu.get_barrier_semaphore()
    for t in range(1, n):
        pl.semaphore_signal(barrier, inc=1, device_id={axis: (me + t) % n},
                            device_id_type=pl.DeviceIdType.MESH)
    local = pltpu.make_async_copy(x_ref.at[me], o_ref.at[me], loc_sem)
    local.start()
    pl.semaphore_wait(barrier, n - 1)
    copies = []
    for t in range(1, n):
        dst = (me + t) % n
        c = pltpu.make_async_remote_copy(
            src_ref=x_ref.at[dst],
            dst_ref=o_ref.at[me],
            send_sem=send_sem.at[t],
            recv_sem=recv_sem.at[t],
            device_id={axis: dst},
            device_id_type=pl.DeviceIdType.MESH,
        )
        c.start()
        copies.append(c)
    local.wait()
    for c in copies:
        c.wait_send()
    for c in copies:
        c.wait_recv()


def _a2a(x, axis, cid):
    n = x.shape[0]
    return pl.pallas_call(
        functools.partial(_a2a_kernel, axis, n),
        out_shape=jax.ShapeDtypeStruct(x.shape, x.dtype),
        in_specs=[pl.BlockSpec(memory_space=pl.ANY)],
        out_specs=pl.BlockSpec(memory_space=pl.ANY),
        scratch_shapes=[
            pltpu.SemaphoreType.DMA((n,)),
            pltpu.SemaphoreType.DMA((n,)),
            pltpu.SemaphoreType.DMA,
        ],
        compiler_params=pltpu.CompilerParams(collective_id=cid, has_side_effects=True),
    )(x)


def _back_gate_send_kernel(k_chunks, m_ref, got_ref, gate_ref, full_ref, sec, recv_s, gv, hid,
                           s_send, s_recv, c_send, c_recv, g_sem):
    n_s, n_j, n_i, _ = sec.shape
    n_c = full_ref.shape[0]
    jp = n_j // n_c
    w = n_i // k_chunks
    me_s = lax.axis_index("seq")
    me_c = lax.axis_index("chan")
    mesh_ids = pl.DeviceIdType.MESH
    barrier = pltpu.get_barrier_semaphore()
    for t in range(1, n_s):
        pl.semaphore_signal(barrier, inc=1, device_id={"seq": (me_s + t) % n_s}, device_id_type=mesh_ids)
    for t in range(1, n_c):
        pl.semaphore_signal(barrier, inc=1, device_id={"chan": (me_c + t) % n_c}, device_id_type=mesh_ids)

    gcopy = pltpu.make_async_copy(gate_ref, gv, g_sem)
    gcopy.start()

    def compute_sec(k):
        m = m_ref[...]
        for i in range(k * w, (k + 1) * w):
            part = jnp.dot(m, got_ref[:, i, :], preferred_element_type=jnp.float32)
            sec[:, :, i, :] = part.astype(sec.dtype).reshape(n_s, n_j, part.shape[-1])

    def issue_seq(k, computed=False):
        isl = pl.ds(k * w, w)
        if not computed:
            compute_sec(k)
        row = []
        for t in range(n_s):
            if t == 0:
                c = pltpu.make_async_copy(sec.at[me_s, :, isl], recv_s.at[me_s, :, isl], s_recv.at[k, 0])
            else:
                dst = (me_s + t) % n_s
                c = pltpu.make_async_remote_copy(
                    src_ref=sec.at[dst, :, isl],
                    dst_ref=recv_s.at[me_s, :, isl],
                    send_sem=s_send.at[k, t],
                    recv_sem=s_recv.at[k, t],
                    device_id={"seq": dst},
                    device_id_type=mesh_ids,
                )
            c.start()
            row.append(c)
        return row

    for k in range(min(LEAD, k_chunks)):
        compute_sec(k)
    pl.semaphore_wait(barrier, (n_s - 1) + (n_c - 1))
    seq_copies = [issue_seq(k, computed=True) for k in range(min(LEAD, k_chunks))]
    gcopy.wait()
    chan_copies = []
    for k in range(k_chunks):
        isl = pl.ds(k * w, w)
        for t in range(n_s):
            if t == 0:
                seq_copies[k][t].wait()
            else:
                seq_copies[k][t].wait_recv()
        for s in range(n_s):
            prod = recv_s[s, :, isl, :].astype(jnp.float32) * gv[:, pl.ds(s * n_i + k * w, w), :].astype(jnp.float32)
            hid[:, s, isl, :] = prod.astype(hid.dtype)
        for t in range(n_c):
            dst = (me_c + t) % n_c
            src_view = hid.at[pl.ds(dst * jp, jp), :, isl, :]
            dst_view = full_ref.at[me_c, :, :, isl, :]
            if t == 0:
                c = pltpu.make_async_copy(src_view, dst_view, c_recv.at[k, 0])
            else:
                c = pltpu.make_async_remote_copy(
                    src_ref=src_view,
                    dst_ref=dst_view,
                    send_sem=c_send.at[k, t],
                    recv_sem=c_recv.at[k, t],
                    device_id={"chan": dst},
                    device_id_type=mesh_ids,
                )
            c.start()
            chan_copies.append((t, c))
        if k + LEAD < k_chunks:
            seq_copies.append(issue_seq(k + LEAD))
    for row in seq_copies:
        for c in row[1:]:
            c.wait_send()
    for t, c in chan_copies:
        if t == 0:
            c.wait()
        else:
            c.wait_send()
    for t, c in chan_copies:
        if t != 0:
            c.wait_recv()


def _back_gate_send(m2, got, gate, n_s, n_c, k_chunks, cid):
    _, n_i, cols = got.shape
    n_j = got.shape[0] // n_s
    jp = n_j // n_c
    return pl.pallas_call(
        functools.partial(_back_gate_send_kernel, k_chunks),
        out_shape=jax.ShapeDtypeStruct((n_c, jp, n_s, n_i, cols), got.dtype),
        in_specs=[pl.BlockSpec(memory_space=pltpu.VMEM)] * 2 + [pl.BlockSpec(memory_space=pl.ANY)],
        out_specs=pl.BlockSpec(memory_space=pl.ANY),
        scratch_shapes=[
            pltpu.VMEM((n_s, n_j, n_i, cols), got.dtype),
            pltpu.VMEM((n_s, n_j, n_i, cols), got.dtype),
            pltpu.VMEM((n_j, n_s * n_i, cols), got.dtype),
            pltpu.VMEM((n_j, n_s, n_i, cols), got.dtype),
            pltpu.SemaphoreType.DMA((k_chunks, n_s)),
            pltpu.SemaphoreType.DMA((k_chunks, n_s)),
            pltpu.SemaphoreType.DMA((k_chunks, n_c)),
            pltpu.SemaphoreType.DMA((k_chunks, n_c)),
            pltpu.SemaphoreType.DMA,
        ],
        compiler_params=pltpu.CompilerParams(collective_id=cid, has_side_effects=True),
    )(m2, got, gate)


def body(tokens, gate_in, mix_first, mix_second, twiddle, out_proj):
    seq_rows, chan_cols = tokens.shape
    n_seq = lax.axis_size("seq")
    n_chan = lax.axis_size("chan")
    blocks_here = seq_rows // B1
    per_dev_i = B1 // n_seq
    d_out = out_proj.shape[1]

    blocked = tokens.reshape(blocks_here, B1, chan_cols)
    mf = mix_first.reshape(n_seq, per_dev_i, B1)
    tw = twiddle.reshape(blocks_here, n_seq, per_dev_i).transpose(1, 0, 2)
    first = jnp.einsum("dik,bkc->dbic", mf, blocked, preferred_element_type=jnp.float32)
    first = (first * tw[:, :, :, None]).astype(jnp.bfloat16)
    got = _a2a(first, "seq", 0)
    got = got.reshape(n_seq * blocks_here, per_dev_i, chan_cols)
    gate = gate_in.reshape(blocks_here, B1, chan_cols)
    full = _back_gate_send(mix_second, got, gate, n_seq, n_chan, CHUNKS, 1)
    rows_per = seq_rows // n_chan
    full = full.reshape(n_chan, rows_per, chan_cols)
    wts = out_proj.reshape(n_chan, chan_cols, n_chan, d_out // n_chan)
    mixed = jnp.einsum("spc,scex->epx", full, wts, preferred_element_type=jnp.float32)
    mixed = mixed.astype(jnp.bfloat16)
    res = _a2a(mixed, "chan", 3)
    return res.reshape(seq_rows, chan_cols)


def solution(mesh):
    placed = (
        P(("batch", "seq"), "chan"),
        P(("batch", "seq"), "chan"),
        P(),
        P(),
        P("seq", None),
        P(),
    )
    return jax.shard_map(
        body, mesh=mesh, in_specs=placed, out_specs=P(("batch", "seq"), "chan"), check_vma=False
    )
```
